32 devices in a mesh: dp: 8 (over z, x), mp: 4 (over y, core).
Axes of the slice: x: 2, y: 2, z: 4, core: 2. Of those that a mesh axis runs over, the one named last changes fastest.
Arguments:
- tokens: bfloat16 [8, 3456, 768], P('dp', 'mp'), may hold values from -6 to 6
- latents: bfloat16 [8, 512, 768], P('dp', 'mp'), may hold values from -6 to 6
- segment_ids: int32 [8, 3456], P('dp'), may hold values from 0 to 3, as said below
- segment_block: int32 [8, 4], P('dp'), may hold values from 0 to 3, as said below
- block_mask: int32 [8, 4], P('dp'), may hold values from 0 to 1, as said below
- gain_tok: bfloat16 [768], replicated, may hold values from 0.5 to 1.5
- gain_cross: bfloat16 [768], replicated, may hold values from 0.5 to 1.5
- gain_self: bfloat16 [768], replicated, may hold values from 0.5 to 1.5
- gain_mlp: bfloat16 [768], replicated, may hold values from 0.5 to 1.5
- wq_cross: bfloat16 [768, 768], P(None, 'mp'), may hold values from -0.21875 to 0.21875
- wk_cross: bfloat16 [768, 768], P(None, 'mp'), may hold values from -0.21875 to 0.21875
- wv_cross: bfloat16 [768, 768], P(None, 'mp'), may hold values from -0.21875 to 0.21875
- wo_cross: bfloat16 [768, 768], P(None, 'mp'), may hold values from -6 to 6
- wq_self: bfloat16 [768, 768], P(None, 'mp'), may hold values from -0.21875 to 0.21875
- wk_self: bfloat16 [768, 768], P(None, 'mp'), may hold values from -0.21875 to 0.21875
- wv_self: bfloat16 [768, 768], P(None, 'mp'), may hold values from -0.21875 to 0.21875
- wo_self: bfloat16 [768, 768], P(None, 'mp'), may hold values from -1.5 to 1.5
- w_up: bfloat16 [768, 3072], P(None, 'mp'), may hold values from -0.21875 to 0.21875
- w_down: bfloat16 [768, 3072], P(None, 'mp'), may hold values from -0.109375 to 0.109375
- d_latents: bfloat16 [8, 512, 768], P('dp', 'mp'), may hold values from -6 to 6
Outputs:
- new_latents: bfloat16 [8, 512, 768], P('dp', 'mp')
- token_gradient_rows: float32 [8, 3456, 768], P('dp', 'mp')
- grad_latents: float32 [8, 512, 768], P('dp', 'mp')
- grad_gain_tok: float32 [768], replicated
- grad_gain_cross: float32 [768], replicated
- grad_gain_self: float32 [768], replicated
- grad_gain_mlp: float32 [768], replicated
- grad_wq_cross: float32 [768, 768], P('dp', 'mp')
- grad_wk_cross: float32 [768, 768], P('dp', 'mp')
- grad_wv_cross: float32 [768, 768], P('dp', 'mp')
- grad_wo_cross: float32 [768, 768], P('dp', 'mp')
- grad_wq_self: float32 [768, 768], P('dp', 'mp')
- grad_wk_self: float32 [768, 768], P('dp', 'mp')
- grad_wv_self: float32 [768, 768], P('dp', 'mp')
- grad_wo_self: float32 [768, 768], P('dp', 'mp')
- grad_w_up: float32 [768, 3072], P('dp', 'mp')
- grad_w_down: float32 [768, 3072], P('dp', 'mp')
The draws below stay inside these ranges and needn't reach their ends.
Inputs may be any that keep to these rules, and one draw needn't show every extreme that they name: `segment_ids`: within a row segment ids never fall; a row holds 2 to 4 segments numbered from 0 without gaps. `segment_block`: each row is a permutation of 0 to 3. block_mask is 1 exactly at the blocks that a segment present in the row owns.
All inputs are finite; a program needn't handle non-finite values.
Results may differ from the reference program's by a relative error of at most 0.02.
Values may be sent and summed in bfloat16 or wider, within the bound.
No kernel may reach another device: no remote copies, remote signals or barrier semaphores. Data moves between devices by JAX's collectives and lax.ppermute only.
A program may use at most 192 MiB of HBM per device.

```python
import math
import jax
import jax.numpy as jnp
from jax import lax

D = 768
HEADS = 12
HEAD = 64
FF = 3072
LAT = 128
NSEG = 4
ROW_LEN = 3456
ROWS = 8


def segment_counts(key):
    base = jax.random.fold_in(key, 101)
    counts = jax.random.randint(base, (ROWS,), 2, NSEG + 1)
    row_ids = jnp.arange(ROWS)
    return jnp.where(row_ids == 0, NSEG, jnp.where(row_ids == 1, 2, counts))


def draw_segment_ids(key, part):
    counts = segment_counts(key)
    jitter_key = jax.random.fold_in(key, 202)
    reach = ROW_LEN // (4 * NSEG)
    jitter = jax.random.randint(jitter_key, (ROWS, NSEG), -reach, reach + 1)
    cut_ids = jnp.arange(NSEG)
    cuts = cut_ids[None, :] * ROW_LEN // counts[:, None] + jitter
    active = (cut_ids[None, :] >= 1) & (cut_ids[None, :] < counts[:, None])
    position = jnp.arange(ROW_LEN)
    passed = active[:, None, :] & (position[None, :, None] >= cuts[:, None, :])
    return jnp.sum(jnp.where(passed, 1, 0), axis=-1).astype(jnp.int32)


def draw_segment_block(key, part):
    base = jax.random.fold_in(key, 303)
    scores = jax.random.randint(base, (ROWS, NSEG), 0, 1 << 20) * NSEG + jnp.arange(NSEG)[None, :]
    return jnp.argsort(scores, axis=-1, stable=True).astype(jnp.int32)


def draw_block_mask(key, part):
    counts = segment_counts(key)
    blocks = draw_segment_block(key, part)
    used = jnp.arange(NSEG)[None, :] < counts[:, None]
    hits = (blocks[:, :, None] == jnp.arange(NSEG)[None, None, :]) & used[:, :, None]
    return jnp.any(hits, axis=1).astype(jnp.int32)


def shard_levels(stream_key, extent, split, low, largest):
    gain, own = 1.0, jax.random.fold_in(stream_key, 6)
    for dim, blocks in split:
        draws = jnp.exp(jax.random.uniform(jax.random.fold_in(own, dim), (blocks,), jnp.float32, low / len(split), largest / len(split)))
        gain = gain * jnp.repeat(draws, extent[dim] // blocks).reshape([-1 if axis == dim else 1 for axis in range(len(extent))])
    return gain


def noise(own_key, shape, scale, most, pieces=(), held_as=jnp.bfloat16):
    loudness = shard_levels(own_key, shape, pieces, -0.22, 0.18) if pieces else 1.0
    array = jax.random.normal(own_key, shape, jnp.float32) * scale * loudness
    return jnp.minimum(jnp.maximum(array, -most), most).astype(held_as)


def setup_inputs(seed: int = 0) -> dict:
    key_list = jax.random.split(jax.random.key(seed), 21)
    return {
        "tokens": noise(key_list[0], (ROWS, ROW_LEN, D), 1.0, 6.0, ((0, 8), (1, 4))),
        "latents": noise(key_list[1], (ROWS, NSEG * LAT, D), 1.0, 6.0, ((0, 8), (1, 4))),
        "segment_ids": draw_segment_ids(jax.random.fold_in(key_list[20], 71), 0),
        "segment_block": draw_segment_block(jax.random.fold_in(key_list[20], 71), 0),
        "block_mask": draw_block_mask(jax.random.fold_in(key_list[20], 71), 0),
        "gain_tok": jnp.clip(1.0 + 0.1 * jax.random.normal(key_list[5], (D,), jnp.float32), 0.5, 1.5).astype(jnp.bfloat16),
        "gain_cross": jnp.clip(1.0 + 0.1 * jax.random.normal(key_list[6], (D,), jnp.float32), 0.5, 1.5).astype(jnp.bfloat16),
        "gain_self": jnp.clip(1.0 + 0.1 * jax.random.normal(key_list[7], (D,), jnp.float32), 0.5, 1.5).astype(jnp.bfloat16),
        "gain_mlp": jnp.clip(1.0 + 0.1 * jax.random.normal(key_list[8], (D,), jnp.float32), 0.5, 1.5).astype(jnp.bfloat16),
        "wq_cross": noise(key_list[9], (D, D), D ** -0.5, 0.21875, ((1, 4),)),
        "wk_cross": noise(key_list[10], (D, D), D ** -0.5, 0.21875, ((1, 4),)),
        "wv_cross": noise(key_list[11], (D, D), D ** -0.5, 0.21875, ((1, 4),)),
        "wo_cross": noise(key_list[12], (D, D), (max(1, D * 8 // ROW_LEN)) ** -0.5, 6.0, ((1, 4),)),
        "wq_self": noise(key_list[13], (D, D), D ** -0.5, 0.21875, ((1, 4),)),
        "wk_self": noise(key_list[14], (D, D), D ** -0.5, 0.21875, ((1, 4),)),
        "wv_self": noise(key_list[15], (D, D), D ** -0.5, 0.21875, ((1, 4),)),
        "wo_self": noise(key_list[16], (D, D), (max(1, D * 16 // (6 * LAT))) ** -0.5, 1.5, ((1, 4),)),
        "w_up": noise(key_list[17], (D, FF), D ** -0.5, 0.21875, ((1, 4),)),
        "w_down": noise(key_list[18], (D, FF), FF ** -0.5, 0.109375, ((1, 4),)),
        "d_latents": noise(key_list[19], (ROWS, NSEG * LAT, D), 1.0, 6.0, ((0, 8), (1, 4))),
    }


EPS = 1e-05
HIGH = lax.Precision.HIGHEST

@jax.custom_vjp
def low(v):
    return lax.optimization_barrier(v.astype(jnp.bfloat16)).astype(jnp.float32)

@jax.custom_vjp
def low_back(v):
    return v

def low_keep(v):
    return (low(v), None)

def low_pass(kept, grad):
    return (grad,)

def back_keep(v):
    return (v, None)

def back_low(kept, grad):
    return (low(grad),)
low.defvjp(low_keep, low_pass)
low_back.defvjp(back_keep, back_low)

def layer_norm(values, gain_vector):
    center = values - lax.optimization_barrier(jnp.mean(values, axis=-1, keepdims=True))
    spread = lax.optimization_barrier(jnp.mean(center * center, axis=-1, keepdims=True))
    return center * lax.rsqrt(spread + EPS) * gain_vector

def project(left, weight):
    return jnp.dot(left, weight, precision=HIGH)

def project_t(left, weight):
    return jnp.dot(left, weight.T, precision=HIGH)

def split_heads(values):
    return values.reshape(values.shape[0], HEADS, HEAD)

def attention(query_vals, key_vals, value_vals, allowed):
    scale = 1.0 / math.sqrt(HEAD)
    scores = jnp.einsum('qhd,khd->hqk', split_heads(query_vals), split_heads(key_vals), precision=HIGH)
    scores = low_back(scores * scale)
    scores = jnp.where(allowed[None], scores, -1e+30)
    probs = low(jax.nn.softmax(scores, axis=-1))
    result = jnp.einsum('hqk,khd->qhd', probs, split_heads(value_vals), precision=HIGH)
    return result.reshape(query_vals.shape[0], HEADS * HEAD)

def row_layer(tok_row, lat_row, seg_row, block_row, mask_row, params):
    token_gain_grad, g_cross, g_self, g_mlp, wq_c, wk_c, wv_c, wo_c, wq_s, wk_s, wv_s, wo_s, w_up, w_down = params
    block_ids = jnp.arange(NSEG)
    lat_block = jnp.arange(NSEG * LAT) // LAT
    tok_block = lax.optimization_barrier(jnp.sum(jnp.where(seg_row[:, None] == block_ids[None, :], block_row[None, :], 0), axis=1))
    keep_lat = lax.optimization_barrier(jnp.sum(jnp.where(lat_block[:, None] == block_ids[None, :], mask_row[None, :], 0), axis=1)).astype(jnp.float32)
    tok_norm = low(layer_norm(tok_row, token_gain_grad))
    lat_norm = low(layer_norm(lat_row, g_cross))
    query_c = low(low_back(project(lat_norm, wq_c)))
    key_c = low(low_back(project(tok_norm, wk_c)))
    value_c = low(low_back(project(tok_norm, wv_c)))
    attn_c = low(low_back(attention(query_c, key_c, value_c, lat_block[:, None] == tok_block[None, :])))
    state_one = lat_row + keep_lat[:, None] * low_back(project_t(attn_c, wo_c))
    self_norm = low(layer_norm(state_one, g_self))
    query_s = low(low_back(project(self_norm, wq_s)))
    key_s = low(low_back(project(self_norm, wk_s)))
    value_s = low(low_back(project(self_norm, wv_s)))
    attn_s = low(low_back(attention(query_s, key_s, value_s, lat_block[:, None] == lat_block[None, :])))
    state_two = state_one + low_back(project_t(attn_s, wo_s))
    mlp_in = low(layer_norm(state_two, g_mlp))
    hidden = low(jax.nn.gelu(low_back(project(mlp_in, w_up)), approximate=True))
    return state_two + low_back(project_t(hidden, w_down))

def reference(tokens, latents, segment_ids, segment_block, block_mask, gain_tok, gain_cross, gain_self, gain_mlp, wq_cross, wk_cross, wv_cross, wo_cross, wq_self, wk_self, wv_self, wo_self, w_up, w_down, d_latents):
    params = tuple((weight_arg.astype(jnp.float32) for weight_arg in (gain_tok, gain_cross, gain_self, gain_mlp, wq_cross, wk_cross, wv_cross, wo_cross, wq_self, wk_self, wv_self, wo_self, w_up, w_down)))
    step_fn = jax.checkpoint(row_layer)

    def forward(tok_all, lat_all, param_set):

        def one_row(carry_in, row_data):
            tok_row, lat_row, seg_row, block_row, mask_row = row_data
            return (carry_in, step_fn(tok_row, lat_row, seg_row, block_row, mask_row, param_set))
        _, new_state = lax.scan(one_row, jnp.zeros((), jnp.float32), (tok_all, lat_all, segment_ids, segment_block, block_mask))
        return new_state
    new_state, pullback = jax.vjp(forward, tokens.astype(jnp.float32), latents.astype(jnp.float32), params)
    grad_tok, grad_lat, grad_params = pullback(d_latents.astype(jnp.float32))
    return (new_state.astype(jnp.bfloat16), grad_tok, grad_lat, grad_params[0], grad_params[1], grad_params[2], grad_params[3], grad_params[4], grad_params[5], grad_params[6], grad_params[7], grad_params[8], grad_params[9], grad_params[10], grad_params[11], grad_params[12], grad_params[13])
```

```python
import functools
import math

import jax
import jax.numpy as jnp
from jax import lax
from jax.experimental import pallas as pl
from jax.experimental.pallas import tpu as pltpu
from jax.sharding import PartitionSpec as P

HEAD = 64
LAT = 128
NSEG = 4
GROUP = 3
EPS = 1e-05
FAR = -1e30
F32 = jnp.float32
BF = jnp.bfloat16
SCALE = 1.0 / math.sqrt(HEAD)
VMEM_BYTES = 58 * 1024 * 1024


def dot(a, b):
    return lax.dot_general(a, b, (((1,), (0,)), ((), ())), preferred_element_type=F32)


def dot_nt(a, b):
    return lax.dot_general(a, b, (((1,), (1,)), ((), ())), preferred_element_type=F32)


def standardize(v):
    center = v - jnp.mean(v, axis=-1, keepdims=True)
    inv = lax.rsqrt(jnp.mean(center * center, axis=-1, keepdims=True) + EPS)
    return center * inv, inv


def norm_back(dy, xhat, inv, gain):
    s = dy * gain
    return inv * (
        s - jnp.mean(s, axis=-1, keepdims=True) - xhat * jnp.mean(s * xhat, axis=-1, keepdims=True)
    )


def kernel_call(body, outs, flops, *args, scalars=()):
    n = len(scalars)
    specs = [pl.BlockSpec(memory_space=pltpu.SMEM)] * n
    specs += [pl.BlockSpec(memory_space=pltpu.VMEM)] * len(args)
    moved = sum(a.size * a.dtype.itemsize for a in args)
    moved += sum(math.prod(s) * jnp.dtype(d).itemsize for s, d in outs)
    return pl.pallas_call(
        body,
        out_shape=[jax.ShapeDtypeStruct(s, d) for s, d in outs],
        in_specs=specs,
        out_specs=[pl.BlockSpec(memory_space=pltpu.VMEM)] * len(outs),
        compiler_params=pltpu.CompilerParams(vmem_limit_bytes=VMEM_BYTES),
        cost_estimate=pl.CostEstimate(flops=flops, bytes_accessed=moved, transcendentals=0),
    )(*[jnp.reshape(s, (1,)).astype(jnp.int32) for s in scalars], *args)


def split3(v):
    a = v.astype(BF).astype(F32)
    b = (v - a).astype(BF).astype(F32)
    return a, b, v - a - b


def stack_rows(rows, pad):
    return jnp.concatenate(rows + [jnp.zeros((pad - len(rows), rows[0].shape[1]), F32)], 0)


def token_masks(tb_col, rows):
    tb = jnp.broadcast_to(tb_col, (rows, 128))
    side = (lax.broadcasted_iota(jnp.int32, (rows, 128), 1) >= HEAD).astype(jnp.int32)
    pair = [jnp.where(tb == side + 2 * i, 1.0, 0.0).astype(BF) for i in range(2)]
    return tb, pair


def spread(dup, pair):
    return jnp.concatenate([dup * pair[0], dup * pair[1]], 1)


def pick(tb, rows):
    out = rows[NSEG - 1]
    for b in range(NSEG - 2, -1, -1):
        out = jnp.where(tb == b, rows[b], out)
    return out


def pile(t, j):
    return jnp.concatenate(
        [t[j * HEAD : (j + 1) * HEAD, b * LAT : (b + 1) * LAT] for b in range(NSEG)], 0
    )


def cross_forward(tokn, wq0, wq1, wk0, wk1, wv0, wv1, l0, l1, l2, l3, tbc, tbr, *outs):
    wq, wk, wv = (wq0, wq1), (wk0, wk1), (wv0, wv1)
    kd_ref, vd_ref, kt_ref, qt_ref = outs[:4]
    pay = outs[4:]
    x = tokn[...]
    rows = x.shape[0]
    lat = jnp.concatenate([l0[...], l1[...], l2[...], l3[...]], 0)
    tb, pair = token_masks(tbc[...], rows)
    row_block = tbr[...]
    block_rows = (
        jnp.broadcast_to(row_block, (8, rows)) == lax.broadcasted_iota(jnp.int32, (8, rows), 0)
    )
    block_rows = jnp.where(block_rows, 1.0, 0.0).astype(BF)
    stats = [[] for _ in range(NSEG)]
    for g in range(2):
        qt = (dot_nt(wq[g][...], lat).astype(BF).astype(F32) * SCALE).astype(BF)
        qt_ref[g * 192 : (g + 1) * 192, :] = qt
        kt_ref[g * 192 : (g + 1) * 192, :] = dot_nt(wk[g][...], x).astype(BF)
        vt = dot_nt(wv[g][...], x).astype(BF)
        for j in range(GROUP):
            h = g * GROUP + j
            hs = slice(j * HEAD, (j + 1) * HEAD)
            ls = slice(h * 128, (h + 1) * 128)
            wkh, wvh = wk[g][hs, :], wv[g][hs, :]
            kd = dot_nt(x, jnp.concatenate([wkh, wkh], 0)).astype(BF)
            vd_ref[:, ls] = dot_nt(x, jnp.concatenate([wvh, wvh], 0)).astype(BF)
            kd_ref[:, ls] = kd
            s = dot(spread(kd, pair), pile(qt, j))
            top = [
                jnp.max(jnp.where(tb == b, s, FAR), axis=0, keepdims=True) for b in range(NSEG)
            ]
            p = jnp.exp(s - pick(tb, top)).astype(BF)
            total = dot(block_rows, p)
            vth = vt[hs, :]
            v4 = jnp.concatenate([vth * block_rows[b : b + 1, :] for b in range(NSEG)], 0)
            o = dot(v4, p)
            for b in range(NSEG):
                tot = total[b : b + 1, :]
                some = tot > 0.0
                safe = jnp.where(some, tot, 1.0)
                stats[b].append(jnp.where(some, top[b] + jnp.log(safe), FAR))
                pay[b][h * HEAD : (h + 1) * HEAD, :] = (
                    o[b * HEAD : (b + 1) * HEAD, :] / safe
                ).astype(BF)
    for b in range(NSEG):
        parts = split3(stack_rows(stats[b], 8))
        pay[b][384:416, :] = jnp.concatenate(list(parts) + [jnp.zeros((8, LAT), F32)], 0).astype(BF)


def latent_forward(keep_ref, *refs):
    pay = refs[:8]
    lat, wo_c, wq, wk, wv, wo, g_self, g_mlp = refs[8], *refs[9:14], *refs[14:16]
    (
        attn_ref,
        lse_ref,
        one_ref,
        two_ref,
        norm_ref,
        mlp_ref,
        at_ref,
        p_ref,
        kt_ref,
        qt_ref,
        v_ref,
    ) = refs[16:]
    keep = keep_ref[0].astype(F32)
    lse_rows = []
    table = {}
    for r in range(4):
        for half in range(2):
            st = pay[2 * r + half][384:416, :].astype(F32)
            table[r, half] = st[0:8] + st[8:16] + st[16:24]
    for g in range(4):
        for j in range(GROUP):
            found = []
            for r in range(4):
                src = g ^ r
                half, at = src >> 1, (src & 1) * GROUP + j
                found.append(
                    (
                        table[r, half][at : at + 1, :],
                        pay[2 * r + half][at * HEAD : (at + 1) * HEAD, :].astype(F32),
                    )
                )
            top = functools.reduce(jnp.maximum, [f[0] for f in found])
            w = [jnp.exp(f[0] - top) for f in found]
            total = w[0] + w[1] + w[2] + w[3]
            o = sum(w[r] * found[r][1] for r in range(4)) / total
            h = g * GROUP + j
            attn_ref[h * HEAD : (h + 1) * HEAD, :] = o.astype(BF)
            lse_rows.append(top + jnp.log(total))
    lse_ref[...] = stack_rows(lse_rows, 16)
    attn = attn_ref[...].astype(F32).T.astype(BF)
    one = lat[...].astype(F32) + keep * dot(attn, wo_c[...])
    one_ref[...] = one
    zhat, _ = standardize(one)
    x = (zhat * g_self[...]).astype(BF)
    norm_ref[...] = x
    qt_ref[...] = (dot_nt(wq[...], x).astype(BF).astype(F32) * SCALE).astype(BF)
    kt_ref[...] = dot_nt(wk[...], x).astype(BF)
    vt = dot_nt(wv[...], x).astype(BF)
    k = dot_nt(x, wk[...]).astype(BF)
    v_ref[...] = dot_nt(x, wv[...]).astype(BF)
    zero = jnp.zeros((HEAD, LAT), BF)
    for h in range(4 * GROUP):
        hs = slice(h * HEAD, (h + 1) * HEAD)
        ps = slice((h // 2) * 128, (h // 2) * 128 + 128)
        qh = qt_ref[hs, :]
        s = dot(k[:, ps], jnp.concatenate([qh, zero] if h % 2 == 0 else [zero, qh], 0))
        e = jnp.exp(s - jnp.max(s, axis=0, keepdims=True))
        p = e / jnp.sum(e, axis=0, keepdims=True)
        p_ref[h * LAT : (h + 1) * LAT, :] = p
        at_ref[hs, :] = dot(vt[hs, :], p.astype(BF)).astype(BF)
    two = one + dot(at_ref[...].astype(F32).T.astype(BF), wo[...])
    two_ref[...] = two
    zhat, _ = standardize(two)
    mlp_ref[...] = (zhat * g_mlp[...]).astype(BF)


def mlp_both(x0, x1, x2, x3, c0, c1, c2, c3, up, down, *outs):
    back, fwd, h_ref, d_ref = outs[:4], outs[4:8], outs[8], outs[9]
    c = math.sqrt(2.0 / math.pi)
    for r, (x, g) in enumerate(((x0, c0), (x1, c1), (x2, c2), (x3, c3))):
        pre = dot(x[...], up[...])
        sq = pre * pre
        t = jnp.tanh(c * pre * (1.0 + 0.044715 * sq))
        h = (0.5 * pre * (1.0 + t)).astype(BF)
        slope = 0.5 * (1.0 + t) + 0.5 * pre * (1.0 - t * t) * c * (1.0 + 3 * 0.044715 * sq)
        d = (dot(g[...], down[...]) * slope).astype(BF)
        rows = slice(r * LAT, (r + 1) * LAT)
        h_ref[rows, :] = h
        d_ref[rows, :] = d
        back[r][...] = dot_nt(d, up[...]).astype(BF)
        fwd[r][...] = dot_nt(h, down[...]).astype(BF)


def mlp_weights(dp_ref, x0, x1, x2, x3, c0, c1, c2, c3, h_ref, d_ref, out):
    me = dp_ref[0]
    n = out.shape[0]
    xt = jnp.concatenate([x0[...], x1[...], x2[...], x3[...]], 0).astype(F32).T.astype(BF)
    gt = jnp.concatenate([c0[...], c1[...], c2[...], c3[...]], 0).astype(F32).T.astype(BF)
    size = xt.shape[0] // n
    for k, (lhs, rhs) in enumerate(((xt, d_ref), (gt, h_ref))):
        full = dot(lhs, rhs[...]).astype(BF)
        for b in range(n):
            out[lax.bitwise_xor(me, b), k * size : (k + 1) * size, :] = full[
                b * size : (b + 1) * size, :
            ]


def latent_backward(keep_ref, *refs):
    b0, b1, b2, b3, two, one, cot, attn, lse, at, p_ref, kt, qt, v = refs[:14]
    wq, wk, wv, wo, wo_c, g_self, g_mlp = refs[14:21]
    pay, g1_ref, g2low, gclow, dqt_ref, dkt_ref, dvt_ref, dg_mlp, dg_self = refs[21:]
    keep = keep_ref[0].astype(F32)
    dmlp = b0[...].astype(F32) + b1[...].astype(F32) + b2[...].astype(F32) + b3[...].astype(F32)
    zhat, inv = standardize(two[...])
    g2 = cot[...].astype(F32) + norm_back(dmlp, zhat, inv, g_mlp[...])
    dg_mlp[...] = jnp.sum(dmlp * zhat, axis=0, keepdims=True)
    low = g2.astype(BF)
    g2low[...] = low
    dat = dot_nt(wo[...], low).astype(BF)
    zero = jnp.zeros((HEAD, LAT), BF)
    for h in range(4 * GROUP):
        hs = slice(h * HEAD, (h + 1) * HEAD)
        ps = slice((h // 2) * 128, (h // 2) * 128 + 128)
        dh = dat[hs, :]
        p = p_ref[h * LAT : (h + 1) * LAT, :]
        dp = dot(v[:, ps], jnp.concatenate([dh, zero] if h % 2 == 0 else [zero, dh], 0))
        ds = (p * (dp - jnp.sum(p * dp, axis=0, keepdims=True))).astype(BF)
        dvt_ref[hs, :] = dot_nt(dh, p.astype(BF)).astype(BF)
        dqt_ref[hs, :] = (dot(kt[hs, :], ds) * SCALE).astype(BF)
        dkt_ref[hs, :] = dot_nt(qt[hs, :], ds).astype(BF)
    back = dot(dqt_ref[...].astype(F32).T.astype(BF), wq[...])
    back += dot(dkt_ref[...].astype(F32).T.astype(BF), wk[...])
    back += dot(dvt_ref[...].astype(F32).T.astype(BF), wv[...])
    zhat, inv = standardize(one[...])
    g1 = g2 + norm_back(back, zhat, inv, g_self[...])
    dg_self[...] = jnp.sum(back * zhat, axis=0, keepdims=True)
    g1_ref[...] = g1
    gc = (keep * g1).astype(BF)
    gclow[...] = gc
    do = dot_nt(wo_c[...], gc).astype(BF)
    pay[0:768, :] = do
    deltas = []
    for h in range(4 * GROUP):
        hs = slice(h * HEAD, (h + 1) * HEAD)
        deltas.append(
            jnp.sum(do[hs, :].astype(F32) * attn[hs, :].astype(F32), axis=0, keepdims=True)
        )
    parts = list(split3(lse[...])) + list(split3(stack_rows(deltas, 16))[:2])
    pay[768:848, :] = jnp.concatenate(parts, 0).astype(BF)


def pack(full, put):
    low = lax.broadcasted_iota(jnp.int32, (48, 128), 1) < HEAD
    for b in range(8):
        r = 96 * b
        tail = jnp.where(low, full[r : r + 48, 128:], full[r + 48 : r + 96, 128:])
        put(b, jnp.concatenate([full[r : r + 96, :128], tail], 0).astype(BF))


def twice(xt, g):
    return jnp.concatenate(
        [xt[g * 192 : (g + 1) * 192, :], xt[g * 192 + 128 : (g + 1) * 192, :]], 0
    )


def latent_weights(dp_ref, *refs, pairs):
    me = dp_ref[0]
    out = refs[-1]
    for k in range(pairs):
        left = refs[2 * k][...].astype(F32).T.astype(BF)
        right = refs[2 * k + 1]
        for g in range(4):
            full = dot_nt(left, twice(right, g))

            def put(b, piece, g=g, k=k):
                out[g, lax.bitwise_xor(me, b), k * 144 : (k + 1) * 144, :] = piece

            pack(full, put)


def cross_backward(dp_ref, *refs, half, first):
    me = dp_ref[0]
    pays = refs[:4]
    kd_ref, vd_ref, kt_ref, qt_ref, tnt, wk0, wk1, wv0, wv1, tbc, tbr = refs[4:15]
    wk, wv = (wk0, wk1), (wv0, wv1)
    rest = refs[15:]
    if not first:
        acc_in, rest = rest[0], rest[1:]
    dqs, dw0, dw1, acc = rest[:4], rest[4], rest[5], rest[6]
    rows = kd_ref.shape[0]
    tb, pair = token_masks(tbc[...], rows)
    own = [jnp.where(tb == b, 1.0, 0.0).astype(BF) for b in range(NSEG)]
    row_mask = [jnp.where(tbr[...] == b, 1.0, 0.0).astype(BF) for b in range(NSEG)]
    lse, delta = [], []
    for r in range(4):
        st = pays[r][768:848, :].astype(F32)
        lse.append(st[0:16] + st[16:32] + st[32:48])
        delta.append(st[48:64] + st[64:80])
    zero = jnp.zeros((HEAD, NSEG * LAT), BF)
    for gi in range(2):
        g = 2 * half + gi
        kv = []
        for j in range(GROUP):
            h = gi * GROUP + j
            ls = slice(h * 128, (h + 1) * 128)
            at = [(g ^ r) * GROUP + j for r in range(4)]
            qcat = qt_ref[h * HEAD : (h + 1) * HEAD, :]
            q4 = jnp.concatenate([qcat[:, b * LAT : (b + 1) * LAT] for b in range(NSEG)], 0)
            dos = [pays[r][at[r] * HEAD : (at[r] + 1) * HEAD, :] for r in range(4)]
            s = dot(spread(kd_ref[:, ls], pair), q4)
            p = jnp.exp(s - pick(tb, [lse[r][at[r] : at[r] + 1, :] for r in range(4)]))
            dp = dot(spread(vd_ref[:, ls], pair), jnp.concatenate(dos, 0))
            ds = p * (dp - pick(tb, [delta[r][at[r] : at[r] + 1, :] for r in range(4)]))
            pb, dsb = p.astype(BF), ds.astype(BF)
            k4 = jnp.concatenate(
                [kt_ref[h * HEAD : (h + 1) * HEAD, :] * row_mask[b] for b in range(NSEG)], 0
            )
            dq = (dot(k4, dsb) * SCALE).astype(BF)
            for b in range(NSEG):
                dqs[b][h * HEAD : (h + 1) * HEAD, :] = dq[b * HEAD : (b + 1) * HEAD, :]
            pm = jnp.concatenate([pb * own[b] for b in range(NSEG)], 1)
            dsm = jnp.concatenate([dsb * own[b] for b in range(NSEG)], 1)
            docat = jnp.concatenate(dos, 1)
            for n, (m, cat) in enumerate(((dsm, qcat), (pm, docat))):
                wide = [[cat, zero], [zero, cat], [cat, cat]][j]
                part = dot_nt(m, jnp.concatenate(wide, 0))
                if j == 0:
                    kv.append([part])
                elif j == 1:
                    kv[n][0] = kv[n][0] + part
                else:
                    kv[n].append(part)
        dw = dw0 if gi == 0 else dw1
        for n in range(2):
            grad = jnp.concatenate([kv[n][0], kv[n][1]], 1).astype(BF)
            w = (wk, wv)[n][gi][...]
            wide = jnp.concatenate([w, jnp.zeros((HEAD, w.shape[1]), BF)], 0)
            part = dot(grad, wide)
            if gi == 0 and n == 0:
                acc[...] = part if first else acc_in[...] + part
            else:
                acc[...] += part

            def put(b, piece, n=n, dw=dw):
                dw[lax.bitwise_xor(me, b), n * 144 : (n + 1) * 144, :] = piece

            pack(dot(tnt[...], grad), put)


def token_norm(tok, gain, out, out_t):
    xhat, _ = standardize(tok[...].astype(F32))
    y = (xhat * gain[...]).astype(BF)
    out[...] = y
    out_t[...] = y.astype(F32).T.astype(BF)


def token_end(acc, tok, gain, out, dg):
    xhat, inv = standardize(tok[...].astype(F32))
    dy = acc[...]
    out[...] = norm_back(dy, xhat, inv, gain[...])
    dg[...] = jnp.sum(dy * xhat, axis=0, keepdims=True)


def latent_end(dp_ref, *refs):
    me = dp_ref[0]
    dqs = refs[:8]
    wq, lat, latn, g1, gain, out, dg, dw, dqt = refs[8:]
    for g in range(4):
        total = None
        for r in range(4):
            src = g ^ r
            at = (src & 1) * 192
            part = dqs[2 * r + (src >> 1)][at : at + 192, :].astype(F32)
            total = part if total is None else total + part
        dqt[g * 192 : (g + 1) * 192, :] = total.astype(BF)
    dlat = dot(dqt[...].astype(F32).T.astype(BF), wq[...])
    left = latn[...].astype(F32).T.astype(BF)
    for g in range(4):

        def put(b, piece, g=g):
            dw[g, lax.bitwise_xor(me, b), :, :] = piece

        pack(dot_nt(left, twice(dqt, g)), put)
    xhat, inv = standardize(lat[...].astype(F32))
    out[...] = g1[...] + norm_back(dlat, xhat, inv, gain[...])
    dg[...] = jnp.sum(dlat * xhat, axis=0, keepdims=True)


def per_device(
    tokens,
    latents,
    segment_ids,
    segment_block,
    block_mask,
    gain_tok,
    gain_cross,
    gain_self,
    gain_mlp,
    wq_cross,
    wk_cross,
    wv_cross,
    wo_cross,
    wq_self,
    wk_self,
    wv_self,
    wo_self,
    w_up,
    w_down,
    d_latents,
):
    mp, dp = lax.axis_size("mp"), lax.axis_size("dp")
    fine = dp // 8
    rank, row = lax.axis_index("mp"), lax.axis_index("dp") // fine
    _, n_tok, width = tokens.shape
    tok, lat, cot = tokens[0], latents[0], d_latents[0]

    def swap(v, r):
        return lax.ppermute(v, "mp", [(i, i ^ r) for i in range(mp)])

    def gather(v):
        far = swap(v, 2)
        return [v, swap(v, 1), far, swap(far, 1)]

    def halve(v, axis, bits):
        count = mp if axis == "mp" else dp
        for i, bit in enumerate(bits):
            got = lax.ppermute(v[1], axis, [(k, k ^ (1 << bit)) for k in range(count)])
            v = v[0].astype(F32) + got.astype(F32)
            if i < len(bits) - 1:
                v = v.astype(BF)
        return v

    g_tok, g_cross, g_self, g_mlp = (
        g.astype(F32)[None, :] for g in (gain_tok, gain_cross, gain_self, gain_mlp)
    )
    latn = (standardize(lat.astype(F32))[0] * g_cross).astype(BF)
    lats = gather(latn)
    wqc, wkc, wvc = gather(wq_cross.T), gather(wk_cross.T), gather(wv_cross.T)
    woc, wqs, wks, wvs, wos = (
        jnp.concatenate(gather(w.T), 0) for w in (wo_cross, wq_self, wk_self, wv_self, wo_self)
    )
    cots = gather(cot)

    ids = lax.dynamic_slice_in_dim(segment_ids[0], rank * n_tok, n_tok, 0)
    block = functools.reduce(
        lambda a, s: jnp.where(ids == s, segment_block[0, s], a), range(NSEG), jnp.zeros_like(ids)
    )
    block = lax.bitwise_xor(block, rank)
    tbc, tbr = block[:, None], block[None, :]
    keep = lax.dynamic_index_in_dim(block_mask[0], rank, keepdims=False)

    tokn, toknt = kernel_call(
        token_norm, [((n_tok, width), BF), ((width, n_tok), BF)], 0, tok, g_tok
    )
    halves, pays = [], []
    for half in range(2):
        a, b = 2 * half, 2 * half + 1
        outs = kernel_call(
            cross_forward,
            [((n_tok, 768), BF)] * 2
            + [((384, n_tok), BF), ((384, NSEG * LAT), BF)]
            + [((416, LAT), BF)] * 4,
            8 * 10**9,
            tokn,
            wqc[a],
            wqc[b],
            wkc[a],
            wkc[b],
            wvc[a],
            wvc[b],
            *lats,
            tbc,
            tbr,
        )
        halves.append(outs[:4])
        pays.append([outs[4]] + [swap(outs[4 + r], r) for r in (1, 2, 3)])
    flat = [pays[half][r] for r in range(4) for half in range(2)]

    sq = (width, LAT)
    attn, lse, one, two, selfn, mlp_in, at, probs, kts, qts, vs = kernel_call(
        latent_forward,
        [
            (sq, BF),
            ((16, LAT), F32),
            ((LAT, width), F32),
            ((LAT, width), F32),
            ((LAT, width), BF),
            ((LAT, width), BF),
            (sq, BF),
            ((12 * LAT, LAT), F32),
            (sq, BF),
            (sq, BF),
            ((LAT, width), BF),
        ],
        10**9,
        *flat,
        lat,
        woc,
        wqs,
        wks,
        wvs,
        wos,
        g_self,
        g_mlp,
        scalars=(keep,),
    )
    xs = gather(mlp_in)
    hid = w_up.shape[1]
    outs = kernel_call(
        mlp_both,
        [((LAT, width), BF)] * 8 + [((4 * LAT, hid), BF)] * 2,
        3 * 10**9,
        *xs,
        *cots,
        w_up,
        w_down,
    )
    backs = [outs[0]] + [swap(outs[r], r) for r in (1, 2, 3)]
    fwds = [outs[4]] + [swap(outs[4 + r], r) for r in (1, 2, 3)]
    hidden, dpre = outs[8:]
    mlp_rows = functools.reduce(jnp.add, [f.astype(F32) for f in fwds])
    new_latents = (two + mlp_rows).astype(BF)

    pay, g1, g2low, gclow, dqt, dkt, dvt, dg_mlp, dg_self = kernel_call(
        latent_backward,
        [
            ((848, LAT), BF),
            ((LAT, width), F32),
            ((LAT, width), BF),
            ((LAT, width), BF),
            (sq, BF),
            (sq, BF),
            (sq, BF),
            ((1, width), F32),
            ((1, width), F32),
        ],
        2 * 10**9,
        *backs,
        two,
        one,
        cot,
        attn,
        lse,
        at,
        probs,
        kts,
        qts,
        vs,
        wqs,
        wks,
        wvs,
        wos,
        woc,
        g_self,
        g_mlp,
        scalars=(keep,),
    )
    pays = gather(pay)

    part = width // 8
    (mlp_dw,) = kernel_call(
        mlp_weights,
        [((8, 2 * part, hid), BF)],
        3 * 10**9,
        *xs,
        *cots,
        hidden,
        dpre,
        scalars=(row,),
    )
    (self_dw,) = kernel_call(
        functools.partial(latent_weights, pairs=5),
        [((4, 8, 5 * 144, 128), BF)],
        2 * 10**9,
        selfn,
        dqt,
        selfn,
        dkt,
        selfn,
        dvt,
        g2low,
        at,
        gclow,
        attn,
        scalars=(row,),
    )

    acc = None
    dqs, dws = {}, {}
    for half in (1, 0):
        a, b = 2 * half, 2 * half + 1
        first = acc is None
        outs = kernel_call(
            functools.partial(cross_backward, half=half, first=first),
            [((384, LAT), BF)] * 4 + [((8, 288, 128), BF)] * 2 + [((n_tok, width), F32)],
            16 * 10**9,
            *pays,
            *halves[half],
            toknt,
            wkc[a],
            wkc[b],
            wvc[a],
            wvc[b],
            tbc,
            tbr,
            *(() if first else (acc,)),
            scalars=(row,),
        )
        dqs[half] = [outs[0]] + [swap(outs[r], r) for r in (1, 2, 3)]
        dws[half] = outs[4].astype(F32) + swap(outs[5], 1).astype(F32)
        acc = outs[6]
    kv_dw = dws[0] + swap(dws[1].astype(BF), 2).astype(F32)

    out_tok, dg_tok = kernel_call(
        token_end, [((n_tok, width), F32), ((1, width), F32)], 0, acc, tok, g_tok
    )
    grad_lat, dg_cross, q_dw, _ = kernel_call(
        latent_end,
        [((LAT, width), F32), ((1, width), F32), ((4, 8, 144, 128), BF), (sq, BF)],
        10**9,
        *[dqs[half][r] for r in range(4) for half in range(2)],
        jnp.concatenate(wqc, 0),
        lat,
        latn,
        g1,
        g_cross,
        scalars=(row,),
    )

    def by_row(v):
        v = v.reshape((2, 2, 2) + v.shape[1:])
        return v.transpose((2, 1, 0) + tuple(range(3, v.ndim)))

    def across(v):
        v = v.reshape((2, 2) + v.shape[1:]).swapaxes(0, 1)
        return halve(v, "mp", (0, 1)).astype(BF)

    low = fine.bit_length() - 1
    rows_bits = (low, low + 1, low + 2)
    groups = [list(range(k * fine, (k + 1) * fine)) for k in range(8)]

    def shard(v):
        if fine == 1:
            return v
        return lax.psum_scatter(v, "dp", scatter_dimension=0, axis_index_groups=groups, tiled=True)
    mlp_sum = halve(by_row(mlp_dw), "dp", rows_bits)
    self_sum = halve(by_row(across(self_dw)), "dp", rows_bits)
    q_sum = halve(by_row(across(q_dw)), "dp", rows_bits)
    kv_sum = halve(by_row(kv_dw.astype(BF)), "dp", rows_bits)

    def unpack(v):
        tail = jnp.concatenate([v[96:, :HEAD], v[96:, HEAD:]], 0)
        return jnp.concatenate([v[:96], tail], 1)

    def piece(v, k):
        return shard(unpack(v[k * 144 : (k + 1) * 144]))

    gains = lax.psum(jnp.concatenate([dg_tok, dg_cross, dg_self, dg_mlp], 0), ("dp", "mp"))
    return (
        new_latents[None],
        out_tok[None],
        grad_lat[None],
        gains[0],
        gains[1],
        gains[2],
        gains[3],
        piece(q_sum, 0),
        piece(kv_sum, 0),
        piece(kv_sum, 1),
        piece(self_sum, 4),
        piece(self_sum, 0),
        piece(self_sum, 1),
        piece(self_sum, 2),
        piece(self_sum, 3),
        shard(mlp_sum[:part]),
        shard(mlp_sum[part:]),
    )


def solution(mesh):
    rows, cols, lone = P("dp", "mp", None), P(None, "mp"), P("dp", None)
    in_specs = (rows, rows, lone, lone, lone) + (P(),) * 4 + (cols,) * 10 + (rows,)
    out_specs = (rows,) * 3 + (P(),) * 4 + (P("dp", "mp"),) * 10
    return jax.shard_map(
        per_device, mesh=mesh, in_specs=in_specs, out_specs=out_specs, check_vma=False
    )
```

```python
import functools
import math

import jax
import jax.numpy as jnp
from jax import lax
from jax.experimental import pallas as pl
from jax.experimental.pallas import tpu as pltpu
from jax.sharding import PartitionSpec as P

HEAD = 64
LAT = 128
NSEG = 4
GROUP = 3
EPS = 1e-05
FAR = -1e30
F32 = jnp.float32
BF = jnp.bfloat16
SCALE = 1.0 / math.sqrt(HEAD)
VMEM_BYTES = 58 * 1024 * 1024


def dot(a, b):
    return lax.dot_general(a, b, (((1,), (0,)), ((), ())), preferred_element_type=F32)


def dot_nt(a, b):
    return lax.dot_general(a, b, (((1,), (1,)), ((), ())), preferred_element_type=F32)


def standardize(v):
    center = v - jnp.mean(v, axis=-1, keepdims=True)
    inv = lax.rsqrt(jnp.mean(center * center, axis=-1, keepdims=True) + EPS)
    return center * inv, inv


def norm_back(dy, xhat, inv, gain):
    s = dy * gain
    return inv * (
        s - jnp.mean(s, axis=-1, keepdims=True) - xhat * jnp.mean(s * xhat, axis=-1, keepdims=True)
    )


def as_row(gain):
    return gain[...].astype(F32).reshape(1, -1)


def kernel_call(body, outs, flops, *args, scalars=(), scratch=(), tables=()):
    n = len(scalars)
    specs = [pl.BlockSpec(memory_space=pltpu.SMEM)] * n
    specs += [
        pl.BlockSpec(memory_space=pltpu.SMEM if i in tables else pltpu.VMEM)
        for i in range(len(args))
    ]
    moved = sum(a.size * a.dtype.itemsize for a in args)
    moved += sum(math.prod(s) * jnp.dtype(d).itemsize for s, d in outs)
    return pl.pallas_call(
        body,
        out_shape=[jax.ShapeDtypeStruct(s, d) for s, d in outs],
        in_specs=specs,
        out_specs=[pl.BlockSpec(memory_space=pltpu.VMEM)] * len(outs),
        scratch_shapes=[pltpu.VMEM(s, d) for s, d in scratch],
        compiler_params=pltpu.CompilerParams(vmem_limit_bytes=VMEM_BYTES),
        cost_estimate=pl.CostEstimate(flops=flops, bytes_accessed=moved, transcendentals=0),
    )(*[jnp.reshape(s, (1,)).astype(jnp.int32) for s in scalars], *args)


def split3(v):
    a = v.astype(BF).astype(F32)
    b = (v - a).astype(BF).astype(F32)
    return a, b, v - a - b


def stack_rows(rows, pad):
    return jnp.concatenate(rows + [jnp.zeros((pad - len(rows), rows[0].shape[1]), F32)], 0)


def lane_masks(tb):
    side = jnp.where(lax.broadcasted_iota(jnp.int32, tb.shape, 1) >= HEAD, 1.0, 0.0)
    return [jnp.where(tb == side + 2.0 * i, 1.0, 0.0).astype(BF) for i in range(2)]


def spread(dup, pair):
    return jnp.concatenate([dup * pair[0], dup * pair[1]], 1)


def pick(tb, rows):
    out = rows[NSEG - 1]
    for b in range(NSEG - 2, -1, -1):
        out = jnp.where(tb == b, rows[b], out)
    return out


def pile(t, j):
    return jnp.concatenate(
        [t[j * HEAD : (j + 1) * HEAD, b * LAT : (b + 1) * LAT] for b in range(NSEG)], 0
    )


SHARE = 208


def cross_forward(*refs, groups, passed):
    tokn, l0, l1, l2, l3, tbs, hot = refs[:7]
    ws, rest = refs[7 : 7 + groups], refs[7 + groups :]
    if passed:
        early, rest = rest[:4], rest[4:]
    kd_ref, vd_ref, kt_ref, qt_ref = rest[:4]
    pay = rest[4:]
    x = tokn[...]
    lat = jnp.concatenate([l0[...], l1[...], l2[...], l3[...]], 0)
    tb = tbs[...]
    pair = lane_masks(tb)
    block_rows = hot[...]
    for g in range(groups):
        wq, wk, wv = ws[g][0:192, :], ws[g][192:384, :], ws[g][384:576, :]
        qt = (dot_nt(wq, lat).astype(BF).astype(F32) * SCALE).astype(BF)
        qt_ref[g * 192 : (g + 1) * 192, :] = qt
        kt_ref[g * 192 : (g + 1) * 192, :] = dot_nt(wk, x).astype(BF)
        vt = dot_nt(wv, x).astype(BF)
        stats = [[] for _ in range(NSEG)]
        base = passed + g * SHARE
        for j in range(GROUP):
            h = g * GROUP + j
            hs = slice(j * HEAD, (j + 1) * HEAD)
            ls = slice(h * 128, (h + 1) * 128)
            kd = dot_nt(x, jnp.concatenate([wk[hs], wk[hs]], 0)).astype(BF)
            vd_ref[:, ls] = dot_nt(x, jnp.concatenate([wv[hs], wv[hs]], 0)).astype(BF)
            kd_ref[:, ls] = kd
            s = dot(spread(kd, pair), pile(qt, j))
            top = [
                jnp.max(jnp.where(tb == b, s, FAR), axis=0, keepdims=True) for b in range(NSEG)
            ]
            p = jnp.exp(s - pick(tb, top)).astype(BF)
            total = dot(block_rows, p)
            vth = vt[hs, :]
            v4 = jnp.concatenate([vth * block_rows[b : b + 1, :] for b in range(NSEG)], 0)
            o = dot(v4, p)
            for b in range(NSEG):
                tot = total[b : b + 1, :]
                some = tot > 0.0
                safe = jnp.where(some, tot, 1.0)
                stats[b].append(jnp.where(some, top[b] + jnp.log(safe), FAR))
                pay[b][base + j * HEAD : base + (j + 1) * HEAD, :] = (
                    o[b * HEAD : (b + 1) * HEAD, :] / safe
                ).astype(BF)
        for b in range(NSEG):
            parts = [v[i : i + 1] for v in split3(stack_rows(stats[b], 8)) for i in range(GROUP)]
            pay[b][base + 192 : base + SHARE, :] = stack_rows(parts, 16).astype(BF)
    if passed:
        for b in range(NSEG):
            pay[b][0:passed, :] = early[b][...]


def join_weights(side, pieces, full):
    own, near = pieces[:2]
    for r, stack in ((0, own), (1, near)):
        for k in range(5):
            full[k][r * 192 : (r + 1) * 192, :] = stack[k * 192 : (k + 1) * 192, :]
    for r, (y0, y1, x0, x1) in ((2, pieces[2:6]), (3, pieces[6:10])):
        parts = []
        for flip in (0, 1):
            for mine, other in ((y0, x0), (y1, x1)):
                parts.append(jnp.where(side == flip, mine[...], other[...]))
        stack = jnp.concatenate(parts, 0)
        for k in range(5):
            full[k][r * 192 : (r + 1) * 192, :] = stack[k * 192 : (k + 1) * 192, :]


def latent_forward(keep_ref, side_ref, *refs):
    pay = refs[:4]
    lat, g_self, g_mlp = refs[4], refs[5], refs[6]
    pieces, full = refs[7:17], refs[-5:]
    (
        attn_ref,
        lse_ref,
        one_ref,
        two_ref,
        norm_ref,
        mlp_ref,
        at_ref,
        p_ref,
        kt_ref,
        qt_ref,
        v_ref,
    ) = refs[17:-5]
    wo_c, wq, wk, wv, wo = full
    keep = keep_ref[0].astype(F32)
    join_weights(side_ref[0], pieces, full)
    lse_rows = []
    for g in range(4):
        tables = []
        for r in range(4):
            base = (g ^ r) * SHARE
            st = pay[r][base + 192 : base + SHARE, :].astype(F32)
            tables.append(st[0:3] + st[3:6] + st[6:9])
        for j in range(GROUP):
            found = []
            for r in range(4):
                base = (g ^ r) * SHARE + j * HEAD
                found.append((tables[r][j : j + 1, :], pay[r][base : base + HEAD, :].astype(F32)))
            top = functools.reduce(jnp.maximum, [f[0] for f in found])
            w = [jnp.exp(f[0] - top) for f in found]
            total = w[0] + w[1] + w[2] + w[3]
            o = sum(w[r] * found[r][1] for r in range(4)) / total
            h = g * GROUP + j
            attn_ref[h * HEAD : (h + 1) * HEAD, :] = o.astype(BF)
            lse_rows.append(top + jnp.log(total))
    lse_ref[...] = stack_rows(lse_rows, 16)
    attn = attn_ref[...].astype(F32).T.astype(BF)
    one = lat[...].astype(F32) + keep * dot(attn, wo_c[...])
    one_ref[...] = one
    zhat, _ = standardize(one)
    x = (zhat * as_row(g_self)).astype(BF)
    norm_ref[...] = x
    qt_ref[...] = (dot_nt(wq[...], x).astype(BF).astype(F32) * SCALE).astype(BF)
    kt_ref[...] = dot_nt(wk[...], x).astype(BF)
    vt = dot_nt(wv[...], x).astype(BF)
    k = dot_nt(x, wk[...]).astype(BF)
    v_ref[...] = dot_nt(x, wv[...]).astype(BF)
    zero = jnp.zeros((HEAD, LAT), BF)
    for h in range(4 * GROUP):
        hs = slice(h * HEAD, (h + 1) * HEAD)
        ps = slice((h // 2) * 128, (h // 2) * 128 + 128)
        qh = qt_ref[hs, :]
        s = dot(k[:, ps], jnp.concatenate([qh, zero] if h % 2 == 0 else [zero, qh], 0))
        e = jnp.exp(s - jnp.max(s, axis=0, keepdims=True))
        p = e / jnp.sum(e, axis=0, keepdims=True)
        p_ref[h * LAT : (h + 1) * LAT, :] = p
        at_ref[hs, :] = dot(vt[hs, :], p.astype(BF)).astype(BF)
    two = one + dot(at_ref[...].astype(F32).T.astype(BF), wo[...])
    two_ref[...] = two
    zhat, _ = standardize(two)
    mlp_ref[...] = (zhat * as_row(g_mlp)).astype(BF)


def mlp_before(c0, c1, c2, c3, l0, l1, l2, l3, down, dh_ref, cot_t, lat_t):
    g = jnp.concatenate([c0[...], c1[...], c2[...], c3[...]], 0)
    dh_ref[...] = dot(g, down[...])
    cot_t[...] = g.astype(F32).T.astype(BF)
    lat = jnp.concatenate([l0[...], l1[...], l2[...], l3[...]], 0)
    lat_t[...] = lat.astype(F32).T.astype(BF)


def mlp_main(x0, x1, x2, x3, dh_ref, up, *outs):
    back, h_ref, d_ref = outs[:4], outs[4], outs[5]
    c = math.sqrt(2.0 / math.pi)
    x = jnp.concatenate([x0[...], x1[...], x2[...], x3[...]], 0)
    pre = dot(x, up[...])
    sq = pre * pre
    t = jnp.tanh(c * pre * (1.0 + 0.044715 * sq))
    h_ref[...] = (0.5 * pre * (1.0 + t)).astype(BF)
    slope = 0.5 * (1.0 + t) + 0.5 * pre * (1.0 - t * t) * c * (1.0 + 3 * 0.044715 * sq)
    d = (dh_ref[...] * slope).astype(BF)
    d_ref[...] = d
    dx = dot_nt(d, up[...]).astype(BF)
    for r in range(4):
        back[r][...] = dx[r * LAT : (r + 1) * LAT, :]


def mlp_weights(dp_ref, x0, x1, x2, x3, gt, h_ref, d_ref, *outs):
    me = dp_ref[0]
    xt = jnp.concatenate([x0[...], x1[...], x2[...], x3[...]], 0).astype(F32).T.astype(BF)
    for k, (lhs, rhs) in enumerate(((xt, d_ref[...]), (gt[...], h_ref[...]))):
        full = dot(lhs, rhs).astype(BF)
        for b in range(8):
            v = lax.bitwise_xor(me, b)
            first, at = (
                (bit(v, 1), 2 * bit(v, 2) + bit(v, 0)),
                (bit(v, 0), 2 * bit(v, 1) + bit(v, 2)),
            )[k]
            piece = full[b * 96 : (b + 1) * 96, :]
            for side in range(2):

                @pl.when(first == side)
                def _(at=at, piece=piece, k=k, side=side):
                    outs[2 * k + side][at, :, :] = piece


def mlp_out(h_ref, down, *outs):
    y = dot_nt(h_ref[...], down[...]).astype(BF)
    for r in range(4):
        outs[r][...] = y[r * LAT : (r + 1) * LAT, :]


def latent_backward(keep_ref, side_ref, *refs):
    b0, b1, b2, b3, two, one, cot, attn, lse, p_ref, kt, qt, v, g_self, g_mlp = refs[:15]
    pieces, full = refs[15:25], refs[-5:]
    pay, g1_ref, g2low, gclow, dqt_ref, dkt_ref, dvt_ref, dg_mlp, dg_self = refs[25:-5]
    wo_c, wq, wk, wv, wo = full
    keep = keep_ref[0].astype(F32)
    join_weights(side_ref[0], pieces, full)
    dmlp = b0[...].astype(F32) + b1[...].astype(F32) + b2[...].astype(F32) + b3[...].astype(F32)
    zhat, inv = standardize(two[...])
    g2 = cot[...].astype(F32) + norm_back(dmlp, zhat, inv, as_row(g_mlp))
    dg_mlp[...] = jnp.sum(dmlp * zhat, axis=0, keepdims=True)
    low = g2.astype(BF)
    g2low[...] = low
    dat = dot_nt(wo[...], low).astype(BF)
    zero = jnp.zeros((HEAD, LAT), BF)
    for h in range(4 * GROUP):
        hs = slice(h * HEAD, (h + 1) * HEAD)
        ps = slice((h // 2) * 128, (h // 2) * 128 + 128)
        dh = dat[hs, :]
        p = p_ref[h * LAT : (h + 1) * LAT, :]
        dp = dot(v[:, ps], jnp.concatenate([dh, zero] if h % 2 == 0 else [zero, dh], 0))
        ds = (p * (dp - jnp.sum(p * dp, axis=0, keepdims=True))).astype(BF)
        dvt_ref[hs, :] = dot_nt(dh, p.astype(BF)).astype(BF)
        dqt_ref[hs, :] = (dot(kt[hs, :], ds) * SCALE).astype(BF)
        dkt_ref[hs, :] = dot_nt(qt[hs, :], ds).astype(BF)
    back = dot(dqt_ref[...].astype(F32).T.astype(BF), wq[...])
    back += dot(dkt_ref[...].astype(F32).T.astype(BF), wk[...])
    back += dot(dvt_ref[...].astype(F32).T.astype(BF), wv[...])
    zhat, inv = standardize(one[...])
    g1 = g2 + norm_back(back, zhat, inv, as_row(g_self))
    dg_self[...] = jnp.sum(back * zhat, axis=0, keepdims=True)
    g1_ref[...] = g1
    gc = (keep * g1).astype(BF)
    gclow[...] = gc
    do = dot_nt(wo_c[...], gc).astype(BF)
    pay[0:768, :] = do
    deltas = []
    for h in range(4 * GROUP):
        hs = slice(h * HEAD, (h + 1) * HEAD)
        deltas.append(
            jnp.sum(do[hs, :].astype(F32) * attn[hs, :].astype(F32), axis=0, keepdims=True)
        )
    parts = list(split3(lse[...])) + list(split3(stack_rows(deltas, 16))[:2])
    pay[768:848, :] = jnp.concatenate(parts, 0).astype(BF)


def bit(v, k):
    return lax.bitwise_and(lax.shift_right_logical(v, k), 1)


def reverse3(v):
    return 4 * bit(v, 0) + 2 * bit(v, 1) + bit(v, 2)


def pack(full, put):
    low = lax.broadcasted_iota(jnp.int32, (48, 128), 1) < HEAD
    for b in range(8):
        r = 96 * b
        tail = jnp.where(low, full[r : r + 48, 128:], full[r + 48 : r + 96, 128:])
        put(b, jnp.concatenate([full[r : r + 96, :128], tail], 0).astype(BF))


def twice(xt, g):
    return jnp.concatenate(
        [xt[g * 192 : (g + 1) * 192, :], xt[g * 192 + 128 : (g + 1) * 192, :]], 0
    )


def latent_weights(dp_ref, *refs, pairs):
    me = dp_ref[0]
    for k in range(pairs):
        left = refs[2 * k][...].astype(F32).T.astype(BF)
        right = refs[2 * k + 1]
        for g in range(4):
            full = dot_nt(left, twice(right, g))

            def put(b, piece, g=g, k=k):
                v = lax.bitwise_xor(me, b)
                lead = 8 * bit(v, 0) + 4 * (g >> 1) if k < 2 else 8 * (g >> 1) + 4 * bit(v, 0)
                at = lead + 2 * bit(v, 1) + bit(v, 2)
                refs[2 * pairs + (g & 1)][at, k * 144 : (k + 1) * 144, :] = piece

            pack(full, put)


def cross_backward(dp_ref, *refs, half, calls):
    me = dp_ref[0]
    first = half == 1
    pays = refs[:4]
    tnt, ltt, tbs, hot, w0, w1 = refs[4:10]
    ws = (w0, w1)
    saved = [refs[10 + 4 * i : 14 + 4 * i] for i in range(calls)]
    rest = refs[10 + 4 * calls :]
    if not first:
        acc_in, dg_in, early, rest = rest[0], rest[1], rest[2:6], rest[6:]
    dqs, dw0, dw1, acc, dg = rest[:4], rest[4], rest[5], rest[6], rest[7]
    if not first:
        for b in range(NSEG):
            dqs[b][384:768, :] = early[b][...]
    tb = tbs[...]
    pair = lane_masks(tb)
    own = [jnp.where(tb == b, 1.0, 0.0).astype(BF) for b in range(NSEG)]
    row_mask = [hot[b : b + 1, :] for b in range(NSEG)]
    lse, delta = [], []
    for r in range(4):
        st = pays[r][768:848, :].astype(F32)
        lse.append(st[0:16] + st[16:32] + st[32:48])
        delta.append(st[48:64] + st[64:80])
    zero = jnp.zeros((HEAD, NSEG * LAT), BF)
    for gi in range(2):
        g = 2 * half + gi
        kv, dqt = [], []
        kd_ref, vd_ref, kt_ref, qt_ref = saved[gi * calls // 2]
        for j in range(GROUP):
            h = (gi * GROUP if calls == 1 else 0) + j
            to = (gi * GROUP + j) * HEAD
            ls = slice(h * 128, (h + 1) * 128)
            at = [(g ^ r) * GROUP + j for r in range(4)]
            qcat = qt_ref[h * HEAD : (h + 1) * HEAD, :]
            q4 = jnp.concatenate([qcat[:, b * LAT : (b + 1) * LAT] for b in range(NSEG)], 0)
            dos = [pays[r][at[r] * HEAD : (at[r] + 1) * HEAD, :] for r in range(4)]
            s = dot(spread(kd_ref[:, ls], pair), q4)
            p = jnp.exp(s - pick(tb, [lse[r][at[r] : at[r] + 1, :] for r in range(4)]))
            dp = dot(spread(vd_ref[:, ls], pair), jnp.concatenate(dos, 0))
            ds = p * (dp - pick(tb, [delta[r][at[r] : at[r] + 1, :] for r in range(4)]))
            pb, dsb = p.astype(BF), ds.astype(BF)
            k4 = jnp.concatenate(
                [kt_ref[h * HEAD : (h + 1) * HEAD, :] * row_mask[b] for b in range(NSEG)], 0
            )
            dq = (dot(k4, dsb) * SCALE).astype(BF)
            for b in range(NSEG):
                dqs[b][to : to + HEAD, :] = dq[b * HEAD : (b + 1) * HEAD, :]
            dqt.append(jnp.concatenate([dq[b * HEAD : (b + 1) * HEAD, :] for b in range(NSEG)], 1))
            pm = jnp.concatenate([pb * own[b] for b in range(NSEG)], 1)
            dsm = jnp.concatenate([dsb * own[b] for b in range(NSEG)], 1)
            docat = jnp.concatenate(dos, 1)
            for n, (m, cat) in enumerate(((dsm, qcat), (pm, docat))):
                wide = [[cat, zero], [zero, cat], [cat, cat]][j]
                part = dot_nt(m, jnp.concatenate(wide, 0))
                if j == 0:
                    kv.append([part])
                elif j == 1:
                    kv[n][0] = kv[n][0] + part
                else:
                    kv[n].append(part)
        dw = dw0 if gi == 0 else dw1
        for n in range(2):
            grad = jnp.concatenate([kv[n][0], kv[n][1]], 1).astype(BF)
            w = ws[gi][(n + 1) * 192 : (n + 2) * 192, :]
            wide = jnp.concatenate([w, jnp.zeros((HEAD, w.shape[1]), BF)], 0)
            part = dot(grad, wide)
            if gi == 0 and n == 0:
                acc[...] = part if first else acc_in[...] + part
            else:
                acc[...] += part

            def put(b, piece, n=n, dw=dw):
                dw[reverse3(lax.bitwise_xor(me, b)), n * 144 : (n + 1) * 144, :] = piece

            pack(dot(tnt[...], grad), put)

        def put(b, piece, dw=dw):
            dw[reverse3(lax.bitwise_xor(me, b)), 288:432, :] = piece

        full = dot_nt(ltt[...], jnp.concatenate(dqt + dqt[2:], 0))
        pack(full, put)
        wide = jnp.concatenate([ws[gi][0:192, :], jnp.zeros((HEAD, full.shape[0]), BF)], 0)
        prod = full * wide.astype(F32).T
        part = jnp.sum((prod[:, :128] + prod[:, 128:]).T, axis=0, keepdims=True)
        if gi == 0:
            dg[...] = part if first else dg_in[...] + part
        else:
            dg[...] += part


def opening(lat, gain, wq, wk, wv, out, ws):
    out[...] = (standardize(lat[...].astype(F32))[0] * as_row(gain)).astype(BF)
    for k, w in enumerate((wq, wk, wv)):
        ws[k * 192 : (k + 1) * 192, :] = w[...]


def stack_weights(side_ref, *refs):
    stack, quarters = refs[5], refs[6:]
    for k in range(5):
        stack[k * 192 : (k + 1) * 192, :] = refs[k][...]
    size = quarters[0].shape[0]
    for c in range(2):
        start = pl.multiple_of((2 * side_ref[0] + c) * size, 16)
        quarters[c][...] = stack[pl.ds(start, size), :]


def prepare(rank_ref, ids, owner, tok, gain, out, out_t, tbs, hot):
    rank = rank_ref[0]
    rows = tok.shape[0]
    mine = ids[:, 0:rows]
    for r in range(1, ids.shape[1] // rows):
        mine = jnp.where(rank == r, ids[:, r * rows : (r + 1) * rows], mine)
    block = jnp.zeros((1, rows), jnp.int32)
    for seg in range(NSEG):
        block = jnp.where(mine == seg, lax.bitwise_xor(owner[0, seg], rank), block)
    block = block.astype(F32)
    eight = lax.broadcasted_iota(jnp.int32, (8, rows), 0).astype(F32)
    hot[...] = jnp.where(jnp.broadcast_to(block, (8, rows)) == eight, 1.0, 0.0).astype(BF)
    tbs[...] = jnp.broadcast_to(block, (128, rows)).T
    xhat, _ = standardize(tok[...].astype(F32))
    y = (xhat * as_row(gain)).astype(BF)
    out[...] = y
    out_t[...] = y.astype(F32).T.astype(BF)


def token_end(acc, tok, gain, out, dg):
    xhat, inv = standardize(tok[...].astype(F32))
    dy = acc[...]
    out[...] = norm_back(dy, xhat, inv, as_row(gain))
    dg[...] = jnp.sum(dy * xhat, axis=0, keepdims=True)


def latent_end(*refs):
    dqs = refs[:4]
    w0, w1, w2, w3, lat, g1, gain, out, dqt = refs[4:]
    for g in range(4):
        total = None
        for r in range(4):
            at = (g ^ r) * 192
            part = dqs[r][at : at + 192, :].astype(F32)
            total = part if total is None else total + part
        dqt[g * 192 : (g + 1) * 192, :] = total.astype(BF)
    wq = jnp.concatenate([w[0:192, :] for w in (w0, w1, w2, w3)], 0)
    dlat = dot(dqt[...].astype(F32).T.astype(BF), wq)
    xhat, inv = standardize(lat[...].astype(F32))
    out[...] = g1[...] + norm_back(dlat, xhat, inv, as_row(gain))


def per_device(
    tokens,
    latents,
    segment_ids,
    segment_block,
    block_mask,
    gain_tok,
    gain_cross,
    gain_self,
    gain_mlp,
    wq_cross,
    wk_cross,
    wv_cross,
    wo_cross,
    wq_self,
    wk_self,
    wv_self,
    wo_self,
    w_up,
    w_down,
    d_latents,
):
    mp, dp = lax.axis_size("mp"), lax.axis_size("dp")
    fine = dp // 8
    low = fine.bit_length() - 1
    rank, place = lax.axis_index("mp"), lax.axis_index("dp")
    row = place // fine
    side = (place >> low) & 1
    _, n_tok, width = tokens.shape
    hid = w_up.shape[1]
    part = width // 8
    tok, lat, cot = tokens[0], latents[0], d_latents[0]
    full, sq = (LAT, width), (width, LAT)

    def after(v, *first):
        return lax.optimization_barrier((v,) + first)[0]

    def together(*v):
        return lax.optimization_barrier(v)

    def swap(v, r):
        return lax.ppermute(v, "mp", [(i, i ^ r) for i in range(mp)])

    def cross(v, k):
        flip = 1 << (low + k)
        return lax.ppermute(v, "dp", [(i, i ^ flip) for i in range(dp)])

    def add(a, b):
        return a.astype(F32) + b.astype(F32)

    latn, own = kernel_call(
        opening,
        [(full, BF), ((576, width), BF)],
        0,
        lat,
        gain_cross,
        wq_cross.T,
        wk_cross.T,
        wv_cross.T,
    )
    l_far, l_near = swap(latn, 2), swap(latn, 1)
    far, near = swap(own, 2), swap(own, 1)
    stack, quarter0, quarter1 = kernel_call(
        stack_weights,
        [((960, width), BF)] + [((240, width), BF)] * 2,
        0,
        wo_cross.T,
        after(wq_self.T, latn),
        wk_self.T,
        wv_self.T,
        wo_self.T,
        scalars=(side,),
    )
    far_self = [swap(q, 2) for q in (quarter0, quarter1)]
    tokn, toknt, tbs, hot = kernel_call(
        prepare,
        [((n_tok, width), BF), ((width, n_tok), BF), ((n_tok, 128), F32), ((8, n_tok), BF)],
        4 * 10**9,
        segment_ids,
        segment_block,
        after(tok, stack),
        gain_tok,
        scalars=(rank,),
        tables=(1,),
    )
    lats = [latn, l_near, l_far, swap(l_far, 1)]
    keep = lax.dynamic_index_in_dim(block_mask[0], rank, keepdims=False)

    def cross_call(weights, early, gate):
        n, passed = len(weights), early[0].shape[0] if early else 0
        outs = kernel_call(
            functools.partial(cross_forward, groups=n, passed=passed),
            [((n_tok, n * 384), BF)] * 2
            + [((n * 192, n_tok), BF), ((n * 192, NSEG * LAT), BF)]
            + [((passed + n * SHARE, LAT), BF)] * 4,
            n * 65 * 10**8,
            after(tokn, *gate),
            *lats,
            tbs,
            hot,
            *weights,
            *early,
        )
        return outs[:4], outs[4:]

    def share(outs):
        return [outs[0]] + [swap(outs[r], r) for r in (1, 2, 3)]

    saved0, pays = cross_call([own, near], [], [])
    far_near = swap(after(far, *pays), 1)
    saved1, pays = cross_call([far], pays, [])
    side_self = [cross(after(far_self[0], pays[0]), 0)]
    saved2, pays = cross_call([far_near], pays, [after(far_self[0], pays[0])])
    side_self.append(cross(after(far_self[1], pays[0]), 0))
    stack_near = swap(after(stack, saved0[0]), 1)
    pays = share(pays)
    pieces = [stack, stack_near] + far_self + side_self
    pieces += [swap(after(w, pays[0]), 1) for w in far_self + side_self]
    weights = [((768, width), BF)] * 5

    c_far = swap(after(cot, pays[0]), 2)
    cots = [cot, swap(after(cot, pays[0]), 1), c_far, swap(c_far, 1)]

    attn, lse, one, two, selfn, mlp_in, at, probs, kts, qts, vs = kernel_call(
        latent_forward,
        [
            (sq, BF),
            ((16, LAT), F32),
            (full, F32),
            (full, F32),
            (full, BF),
            (full, BF),
            (sq, BF),
            ((12 * LAT, LAT), F32),
            (sq, BF),
            (sq, BF),
            (full, BF),
        ],
        8 * 10**9,
        *pays,
        lat,
        gain_self,
        gain_mlp,
        *pieces,
        scalars=(keep, side),
        scratch=weights,
    )
    x_far, x_near = swap(mlp_in, 2), swap(mlp_in, 1)
    xs = [mlp_in, x_near, x_far, swap(x_far, 1)]
    dh, cot_t, lat_t = kernel_call(
        mlp_before,
        [((4 * LAT, hid), F32), ((width, 4 * LAT), BF), ((width, 4 * LAT), BF)],
        4 * 10**9,
        *cots[:3],
        after(cots[3], mlp_in),
        *lats,
        w_down,
    )
    outs = kernel_call(
        mlp_main,
        [(full, BF)] * 4 + [((4 * LAT, hid), BF)] * 2,
        5 * 10**9,
        *xs,
        dh,
        w_up,
    )
    backs = share(outs[:4])
    hidden, dpre = outs[4:]
    outs = kernel_call(
        mlp_weights,
        [((4, part, hid), BF)] * 4,
        4 * 10**9,
        *xs,
        cot_t,
        hidden,
        dpre,
        scalars=(row,),
    )
    up_keep, up_send, down_keep, down_send = outs[:4]
    up_got, down_got = cross(up_send, 1), cross(down_send, 0)
    forwards = kernel_call(mlp_out, [(full, BF)] * 4, 2 * 10**9, after(hidden, up_send), w_down)
    fwds = share([after(v, *backs) for v in forwards])

    pay, g1, g2low, gclow, dqt, dkt, dvt, dg_mlp, dg_self = kernel_call(
        latent_backward,
        [
            ((848, LAT), BF),
            (full, F32),
            (full, BF),
            (full, BF),
            (sq, BF),
            (sq, BF),
            (sq, BF),
            ((1, width), F32),
            ((1, width), F32),
        ],
        9 * 10**9,
        *backs,
        after(two, forwards[0]),
        one,
        cot,
        attn,
        lse,
        probs,
        kts,
        qts,
        vs,
        gain_self,
        gain_mlp,
        *pieces,
        scalars=(keep, side),
        scratch=weights,
    )
    pay, up_got, down_got, *fwds = together(pay, up_got, down_got, *fwds)
    new_latents = (two + functools.reduce(jnp.add, [f.astype(F32) for f in fwds])).astype(BF)
    p_far, p_near = swap(pay, 2), swap(pay, 1)
    pays = [pay, p_near, p_far, swap(p_far, 1)]

    self_keep, self_send = kernel_call(
        functools.partial(latent_weights, pairs=5),
        [((16, 5 * 144, 128), BF)] * 2,
        6 * 10**9,
        selfn,
        dqt,
        selfn,
        dkt,
        selfn,
        dvt,
        g2low,
        at,
        gclow,
        attn,
        scalars=(row,),
    )

    def lead(v):
        return v.reshape((2, v.shape[0] // 2) + v.shape[1:])

    def part_sum(kept, got):
        kept, got = lead(kept), lead(got)
        return add(kept[0], got[0]).astype(BF), add(kept[1], got[1]).astype(BF)

    self_near = swap(after(self_send, p_far), 1)
    rows_a, rows_b, rows_c = slice(0, 288), slice(288, 576), slice(576, 720)
    a_kept, a_sent = part_sum(self_keep[:, rows_a], self_near[:, rows_a])
    b_kept, b_sent = part_sum(self_keep[:, rows_b], self_near[:, rows_b])
    c_kept, c_sent = part_sum(self_keep[:, rows_c], self_near[:, rows_c])
    up_kept, up_sent = part_sum(up_keep, up_got)
    down_kept, down_sent = part_sum(down_keep, down_got)

    def cross_back(half, ws, saved, more, gate):
        return kernel_call(
            functools.partial(cross_backward, half=half, calls=len(saved)),
            [((768 - 384 * half, LAT), BF)] * 4
            + [((8, 432, 128), BF)] * 2
            + [((n_tok, width), F32), ((1, width), F32)],
            15 * 10**9,
            after(pays[0], *gate),
            *pays[1:],
            toknt,
            lat_t,
            tbs,
            hot,
            *ws,
            *[v for group in saved for v in group],
            *more,
            scalars=(row,),
        )

    outs = cross_back(
        1, (far, far_near), (saved1, saved2), (), (a_sent, b_sent, up_sent, down_sent)
    )
    a_got, b_got = cross(a_sent, 0), swap(b_sent, 2)
    up_got, down_got = cross(up_sent, 2), cross(down_sent, 1)
    early, acc, dg_cross = outs[:4], outs[6], outs[7]
    other, a_got, b_got, up_got, down_got = together(outs[5], a_got, b_got, up_got, down_got)
    far_kept, far_sent = part_sum(outs[4], swap(other, 1))
    a_kept, a_sent = part_sum(a_kept, a_got)
    b_kept, b_sent = part_sum(b_kept, b_got)
    down_kept, down_sent = part_sum(down_kept, down_got)
    c_sent = after(c_sent, other)
    outs = cross_back(
        0, (own, near), (saved0,), (acc, dg_cross, *early), (far_sent, a_sent, b_sent, c_sent, down_sent)
    )
    a_got, b_got = swap(a_sent, 2), cross(b_sent, 0)
    c_got, far_got = swap(c_sent, 2), cross(far_sent, 0)
    down_got = cross(down_sent, 2)
    dqs, acc, dg_cross = outs[:4], outs[6], outs[7]
    other, a_got, b_got, c_got, far_got, down_got = together(
        outs[5], a_got, b_got, c_got, far_got, down_got
    )
    cross_kept, cross_sent = part_sum(outs[4], swap(other, 1))
    far_sum = add(far_kept, far_got).astype(BF)
    cross_got, far_got = cross(cross_sent, 0), swap(far_sum, 2)
    dqs = share([after(v, cross_sent, far_sum) for v in dqs])
    out_tok, dg_tok = kernel_call(
        token_end,
        [((n_tok, width), F32), ((1, width), F32)],
        5 * 10**9,
        after(acc, cross_sent, far_sum),
        tok,
        gain_tok,
    )
    grad_lat, _ = kernel_call(
        latent_end,
        [(full, F32), (sq, BF)],
        3 * 10**9,
        *dqs,
        own,
        near,
        far,
        far_near,
        lat,
        g1,
        gain_cross,
    )
    dg_cross = dg_cross / gain_cross.astype(F32)[None, :]
    gains = jnp.concatenate([dg_tok, dg_cross, dg_self, dg_mlp], 0)

    def ahead(pair, move):
        kept, sent = part_sum(*pair)
        return kept, move(sent)

    c_kept, c_sent = part_sum(c_kept, c_got)
    up_kept, up_sent = part_sum(up_kept, up_got)
    c_got, up_got = cross(after(c_sent, cross_sent), 0), cross(after(up_sent, cross_sent), 0)
    gains = gains + swap(gains, 1)
    gains = gains + swap(gains, 2)
    cross_got, far_got, c_got, up_got, gains = together(cross_got, far_got, c_got, up_got, gains)
    cross_sum = ahead((cross_kept, add(cross_got, far_got)), lambda v: cross(v, 1))
    kept = jnp.concatenate((a_kept, b_kept, c_kept), 1)
    got = jnp.concatenate((a_got, b_got, c_got), 1)
    self_sum = ahead((kept, got), lambda v: cross(v, 1))
    for k in range(3):
        gains = gains + cross(gains, k)
    cross_sum = ahead(cross_sum, lambda v: cross(v, 2))
    self_sum = ahead(self_sum, lambda v: cross(v, 2))
    up_sum, down_sum, self_sum, cross_sum = (
        add(*pair)[0]
        for pair in ((up_kept, up_got), (down_kept, down_got), self_sum, cross_sum)
    )
    for k in range(low):
        gains = gains + lax.ppermute(gains, "dp", [(i, i ^ (1 << k)) for i in range(dp)])

    groups = [list(range(k * fine, (k + 1) * fine)) for k in range(8)]

    def shard(v):
        if fine == 1:
            return v
        return lax.psum_scatter(v, "dp", scatter_dimension=0, axis_index_groups=groups, tiled=True)

    def piece(v, k):
        v = v[k * 144 : (k + 1) * 144]
        tail = jnp.concatenate([v[96:, :HEAD], v[96:, HEAD:]], 0)
        return shard(jnp.concatenate([v[:96], tail], 1))

    return (
        new_latents[None],
        out_tok[None],
        grad_lat[None],
        gains[0],
        gains[1],
        gains[2],
        gains[3],
        piece(cross_sum, 2),
        piece(cross_sum, 0),
        piece(cross_sum, 1),
        piece(self_sum, 4),
        piece(self_sum, 0),
        piece(self_sum, 1),
        piece(self_sum, 2),
        piece(self_sum, 3),
        shard(up_sum),
        shard(down_sum),
    )


def solution(mesh):
    rows, cols, lone = P("dp", "mp", None), P(None, "mp"), P("dp", None)
    in_specs = (rows, rows, lone, lone, lone) + (P(),) * 4 + (cols,) * 10 + (rows,)
    out_specs = (rows,) * 3 + (P(),) * 4 + (P("dp", "mp"),) * 10
    return jax.shard_map(
        per_device, mesh=mesh, in_specs=in_specs, out_specs=out_specs, check_vma=False
    )
```

```python
import functools
import math

import jax
import jax.numpy as jnp
from jax import lax
from jax.experimental import pallas as pl
from jax.experimental.pallas import tpu as pltpu
from jax.sharding import PartitionSpec as P

HEAD = 64
LAT = 128
NSEG = 4
GROUP = 3
EPS = 1e-05
FAR = -1e30
F32 = jnp.float32
BF = jnp.bfloat16
SCALE = 1.0 / math.sqrt(HEAD)
MIB = 1024 * 1024
VMEM_CROSS = 24
VMEM_LATENT = 20


def dot(a, b):
    return lax.dot_general(a, b, (((1,), (0,)), ((), ())), preferred_element_type=F32)


def dot_nt(a, b):
    return lax.dot_general(a, b, (((1,), (1,)), ((), ())), preferred_element_type=F32)


def standardize(v):
    center = v - jnp.mean(v, axis=-1, keepdims=True)
    inv = lax.rsqrt(jnp.mean(center * center, axis=-1, keepdims=True) + EPS)
    return center * inv, inv


def norm_back(dy, xhat, inv, gain):
    s = dy * gain
    return inv * (
        s - jnp.mean(s, axis=-1, keepdims=True) - xhat * jnp.mean(s * xhat, axis=-1, keepdims=True)
    )


def as_row(gain):
    return gain[...].astype(F32).reshape(1, -1)


def kernel_call(body, outs, flops, *args, scalars=(), scratch=(), tables=(), vmem=12, far=()):
    n = len(scalars)
    specs = [pl.BlockSpec(memory_space=pltpu.SMEM)] * n
    specs += [
        pl.BlockSpec(memory_space=pltpu.SMEM if i in tables else pltpu.VMEM)
        for i in range(len(args))
    ]
    moved = sum(a.size * a.dtype.itemsize for a in args)
    moved += sum(math.prod(s) * jnp.dtype(d).itemsize for s, d in outs)
    return pl.pallas_call(
        body,
        out_shape=[jax.ShapeDtypeStruct(s, d) for s, d in outs],
        in_specs=specs,
        out_specs=[
            pl.BlockSpec(memory_space=pltpu.HBM if i in far else pltpu.VMEM)
            for i in range(len(outs))
        ],
        scratch_shapes=[
            pltpu.VMEM(*x) if isinstance(x, tuple) else x for x in scratch
        ],
        compiler_params=pltpu.CompilerParams(vmem_limit_bytes=vmem * MIB),
        cost_estimate=pl.CostEstimate(flops=flops, bytes_accessed=moved, transcendentals=0),
    )(*[jnp.reshape(s, (1,)).astype(jnp.int32) for s in scalars], *args)


def split3(v):
    a = v.astype(BF).astype(F32)
    b = (v - a).astype(BF).astype(F32)
    return a, b, v - a - b


def stack_rows(rows, pad):
    return jnp.concatenate(rows + [jnp.zeros((pad - len(rows), rows[0].shape[1]), F32)], 0)


def pick(tb, rows):
    out = rows[NSEG - 1]
    for b in range(NSEG - 2, -1, -1):
        out = jnp.where(tb == b, rows[b], out)
    return out


def widen(v, own):
    return jnp.concatenate([v] * NSEG, 1) * own


def pile(t):
    top = lax.broadcasted_iota(jnp.int32, (2 * HEAD, LAT), 0) < HEAD
    zero = jnp.zeros((2 * HEAD, LAT), t.dtype)
    rows = []
    for b in range(NSEG):
        part = t[:, b * LAT : (b + 1) * LAT]
        rows.append(
            jnp.concatenate([jnp.where(top, part, zero), jnp.where(top, zero, part)], 1)
        )
    return jnp.concatenate(rows, 0)


def fill_masks(tb, own):
    for b in range(NSEG):
        own[:, b * 128 : (b + 1) * 128] = jnp.where(tb == b, 1.0, 0.0).astype(BF)


SHARE = 416


def cross_forward(side_ref, *refs, second):
    x_ref, l0, l1, first2, first3, tbs, hot = refs[:7]
    rest = refs[7:]
    if second:
        halves, early, rest = rest[:2], rest[2:4], rest[4:]
    else:
        pieces, rest = rest[:2], rest[2:]
    kn_out, vn_out, kt_out, qt_out, mine, other = rest[:6]
    if second:
        pieces, rest = rest[6:8], rest[8:]
        for piece, by_mp, by_dp in zip(pieces, (first2, first3), halves):
            low = side_ref[0] == 0
            piece[0:288, :] = jnp.where(low, by_mp[128:416, :], by_dp[...])
            piece[288:576, :] = jnp.where(low, by_dp[...], by_mp[128:416, :])
    else:
        rest = rest[6:]
    kn, vn, kt, vt, qt, own, stat, sems = rest
    w = [
        jnp.concatenate([p[k * 192 : (k + 1) * 192, :] for p in pieces], 0) for k in range(3)
    ]
    lat = jnp.concatenate([l0[...], l1[...], first2[0:128, :], first3[0:128, :]], 0)
    qt[...] = (dot_nt(w[0], lat).astype(BF).astype(F32) * SCALE).astype(BF)
    kn[...] = dot_nt(x_ref[...], w[1]).astype(BF)
    vn[...] = dot_nt(x_ref[...], w[2]).astype(BF)
    kt[...] = dot_nt(w[1], x_ref[...]).astype(BF)
    vt[...] = dot_nt(w[2], x_ref[...]).astype(BF)
    copies = [
        pltpu.make_async_copy(v, out, sems.at[i])
        for i, (v, out) in enumerate(((kn, kn_out), (vn, vn_out), (kt, kt_out), (qt, qt_out)))
    ]
    for copy in copies:
        copy.start()
    fill_masks(tbs[...], own)
    base = SHARE if second else 0
    stat[...] = jnp.zeros_like(stat)
    block_rows = hot[...]

    def two_heads(i, _):
        lanes = pl.ds(pl.multiple_of(i * 128, 128), 128)
        tb = tbs[...]
        s = dot(widen(kn[:, lanes], own[...]), pile(qt[lanes, :]))
        for j in range(2):
            sj = s[:, j * LAT : (j + 1) * LAT]
            top = [
                jnp.max(jnp.where(tb == b, sj, FAR), axis=0, keepdims=True) for b in range(NSEG)
            ]
            p = jnp.exp(sj - pick(tb, top)).astype(BF)
            total_of = dot(block_rows, p)
            rows = pl.ds(pl.multiple_of(i * 128 + j * HEAD, HEAD), HEAD)
            vth = vt[rows, :]
            v4 = jnp.concatenate([vth * block_rows[b : b + 1, :] for b in range(NSEG)], 0)
            o = dot(v4, p)
            to = pl.ds(pl.multiple_of(base + i * 128 + j * HEAD, 32), HEAD)
            for b in range(NSEG):
                tot = total_of[b : b + 1, :]
                some = tot > 0.0
                safe = jnp.where(some, tot, 1.0)
                stat[b, pl.ds(2 * i + j, 1), :] = jnp.where(some, top[b] + jnp.log(safe), FAR)
                out = (mine, other)[b & 1]
                out[b >> 1, to, :] = (o[b * HEAD : (b + 1) * HEAD, :] / safe).astype(BF)
        return 0

    lax.fori_loop(0, 3, two_heads, 0)
    for b in range(NSEG):
        out = (mine, other)[b & 1]
        out[b >> 1, base + 384 : base + SHARE, :] = jnp.concatenate(
            list(split3(stat[b])) + [jnp.zeros((8, LAT), F32)], 0
        ).astype(BF)
    if second:
        for out, first in ((mine, early[0]), (other, early[1])):
            out[:, 0:SHARE, :] = first[...]
    for copy in copies:
        copy.wait()


def merge(parts, head, lse_of):
    tables = []
    for read, _ in parts:
        one = []
        for half in range(2):
            st = read(half * SHARE + 384, 32).astype(F32)
            one.append(st[0:8] + st[8:16] + st[16:24])
        tables.append(one)
    for g in range(4):
        for j in range(GROUP):
            found = []
            for (read, flip), table in zip(parts, tables):
                src = g ^ flip
                half, at = src >> 1, (src & 1) * GROUP + j
                found.append(
                    (table[half][at : at + 1, :], read(half * SHARE + at * HEAD, HEAD).astype(F32))
                )
            top = functools.reduce(jnp.maximum, [f[0] for f in found])
            w = [jnp.exp(f[0] - top) for f in found]
            all_w = functools.reduce(jnp.add, w)
            o = functools.reduce(jnp.add, [a * f[1] for a, f in zip(w, found)]) / all_w
            head(g, j, o.astype(BF))
            lse_of(g, j, top + jnp.log(all_w))


def merge_pair(mine, got, keep, send):
    for k, out in enumerate((keep, send)):
        rows = [[], []]

        def head(g, j, o, out=out):
            at = (g >> 1) * SHARE + ((g & 1) * GROUP + j) * HEAD
            out[at : at + HEAD, :] = o

        def lse_of(g, j, v, rows=rows):
            rows[g >> 1].append(v)

        merge(
            [
                (lambda a, n, k=k: mine[k, a : a + n, :], 0),
                (lambda a, n, k=k: got[k, a : a + n, :], 1),
            ],
            head,
            lse_of,
        )
        for half in range(2):
            parts = list(split3(stack_rows(rows[half], 8))) + [jnp.zeros((8, LAT), F32)]
            out[half * SHARE + 384 : (half + 1) * SHARE, :] = jnp.concatenate(parts, 0).astype(BF)


def join_weights(side, pieces, full):
    own, near = pieces[:2]
    for r, stack in ((0, own), (1, near)):
        for k in range(5):
            full[k][r * 192 : (r + 1) * 192, :] = stack[k * 192 : (k + 1) * 192, :]
    for r, (by_mp, by_dp, last) in ((2, pieces[2:5]), (3, pieces[5:8])):
        low = side == 0
        stack = jnp.concatenate(
            [
                jnp.where(low, by_mp[...], by_dp[...]),
                jnp.where(low, by_dp[...], by_mp[...]),
                last[...],
            ],
            0,
        )
        for k in range(5):
            full[k][r * 192 : (r + 1) * 192, :] = stack[k * 192 : (k + 1) * 192, :]


def latent_forward(keep_ref, side_ref, *refs):
    pay = refs[:2]
    lat, g_self, g_mlp = refs[2], refs[3], refs[4]
    pieces, full = refs[5:13], refs[-5:]
    (
        attn_ref,
        lse_ref,
        one_ref,
        two_ref,
        norm_ref,
        mlp_ref,
        at_ref,
        p_ref,
        kt_ref,
        qt_ref,
        v_ref,
    ) = refs[13:-5]
    wo_c, wq, wk, wv, wo = full
    keep = keep_ref[0].astype(F32)
    join_weights(side_ref[0], pieces, full)
    lse_rows = []

    def head(g, j, o):
        at = (g * GROUP + j) * HEAD
        attn_ref[at : at + HEAD, :] = o

    merge(
        [(lambda a, n: pay[0][a : a + n, :], 0), (lambda a, n: pay[1][a : a + n, :], 2)],
        head,
        lambda g, j, v: lse_rows.append(v),
    )
    lse_ref[...] = stack_rows(lse_rows, 16)
    attn = attn_ref[...].astype(F32).T.astype(BF)
    one = lat[...].astype(F32) + keep * dot(attn, wo_c[...])
    one_ref[...] = one
    zhat, _ = standardize(one)
    x = (zhat * as_row(g_self)).astype(BF)
    norm_ref[...] = x.astype(F32).T.astype(BF)
    qt_ref[...] = (dot_nt(wq[...], x).astype(BF).astype(F32) * SCALE).astype(BF)
    kt_ref[...] = dot_nt(wk[...], x).astype(BF)
    vt = dot_nt(wv[...], x).astype(BF)
    k = dot_nt(x, wk[...]).astype(BF)
    v_ref[...] = dot_nt(x, wv[...]).astype(BF)
    zero = jnp.zeros((HEAD, LAT), BF)
    for h in range(4 * GROUP):
        hs = slice(h * HEAD, (h + 1) * HEAD)
        ps = slice((h // 2) * 128, (h // 2) * 128 + 128)
        qh = qt_ref[hs, :]
        s = dot(k[:, ps], jnp.concatenate([qh, zero] if h % 2 == 0 else [zero, qh], 0))
        e = jnp.exp(s - jnp.max(s, axis=0, keepdims=True))
        p = e / jnp.sum(e, axis=0, keepdims=True)
        p_ref[h * LAT : (h + 1) * LAT, :] = p
        at_ref[hs, :] = dot(vt[hs, :], p.astype(BF)).astype(BF)
    two = one + dot(at_ref[...].astype(F32).T.astype(BF), wo[...])
    two_ref[...] = two
    zhat, _ = standardize(two)
    mlp_ref[...] = (zhat * as_row(g_mlp)).astype(BF)


def mlp_before(c0, c1, c2, c3, l0, l1, first2, first3, down, dh_ref, cot_t, lat_t):
    g = jnp.concatenate([c0[...], c1[...], c2[...], c3[...]], 0)
    dh_ref[...] = dot(g, down[...])
    cot_t[...] = g.astype(F32).T.astype(BF)
    lat = jnp.concatenate([l0[...], l1[...], first2[0:128, :], first3[0:128, :]], 0)
    lat_t[...] = lat.astype(F32).T.astype(BF)


def deal(v, mine, other):
    for r in range(4):
        out = (mine, other)[r & 1]
        out[r >> 1, :, :] = v[r * LAT : (r + 1) * LAT, :]


def mlp_main(x0, x1, x2, x3, dh_ref, up, *outs):
    mine, other, h_ref, d_ref = outs
    c = math.sqrt(2.0 / math.pi)
    x = jnp.concatenate([x0[...], x1[...], x2[...], x3[...]], 0)
    pre = dot(x, up[...])
    sq = pre * pre
    t = jnp.tanh(c * pre * (1.0 + 0.044715 * sq))
    h_ref[...] = (0.5 * pre * (1.0 + t)).astype(BF)
    slope = 0.5 * (1.0 + t) + 0.5 * pre * (1.0 - t * t) * c * (1.0 + 3 * 0.044715 * sq)
    d = (dh_ref[...] * slope).astype(BF)
    d_ref[...] = d
    deal(dot_nt(d, up[...]).astype(BF), mine, other)


def mlp_weights(dp_ref, x0, x1, x2, x3, gt, h_ref, d_ref, *outs):
    me = dp_ref[0]
    rows = outs[4]
    xt = jnp.concatenate([x0[...], x1[...], x2[...], x3[...]], 0).astype(F32).T.astype(BF)
    for k, (lhs, rhs) in enumerate(((xt, d_ref[...]), (gt[...], h_ref[...]))):
        full = dot(lhs, rhs).astype(BF)
        for b in range(8):
            at = place_of(me, b, ((1, 0, 2), (0, 1, 2))[k])
            for c in range(6):
                rows[at, c * 96 : (c + 1) * 96, :] = full[
                    b * 96 : (b + 1) * 96, c * 128 : (c + 1) * 128
                ]
        outs[2 * k][...] = rows[0:4]
        outs[2 * k + 1][...] = rows[4:8]


def mlp_out(h_ref, down, mine, other):
    deal(dot_nt(h_ref[...], down[...]).astype(BF), mine, other)


def latent_backward(keep_ref, side_ref, *refs):
    b0, b1, two, one, cot, attn, at_ref, lse, p_ref, kt, qt, v, g_self, g_mlp = refs[:14]
    pieces, full = refs[14:22], refs[-5:]
    pay, g1_ref, grads, *mine, dg_mlp, dg_self = refs[22:-8]
    dqt_ref, dkt_ref, dvt_ref = refs[-8:-5]
    wo_c, wq, wk, wv, wo = full
    keep = keep_ref[0].astype(F32)
    join_weights(side_ref[0], pieces, full)
    dmlp = b0[...] + b1[...].astype(F32)
    zhat, inv = standardize(two[...])
    g2 = cot[...].astype(F32) + norm_back(dmlp, zhat, inv, as_row(g_mlp))
    dg_mlp[...] = jnp.sum(dmlp * zhat, axis=0, keepdims=True)
    low = g2.astype(BF)
    grads[0:768, :] = g2.T.astype(BF)
    dat = dot_nt(wo[...], low).astype(BF)
    zero = jnp.zeros((HEAD, LAT), BF)
    for h in range(4 * GROUP):
        hs = slice(h * HEAD, (h + 1) * HEAD)
        ps = slice((h // 2) * 128, (h // 2) * 128 + 128)
        dh = dat[hs, :]
        p = p_ref[h * LAT : (h + 1) * LAT, :]
        dp = dot(v[:, ps], jnp.concatenate([dh, zero] if h % 2 == 0 else [zero, dh], 0))
        ds = (p * (dp - jnp.sum(p * dp, axis=0, keepdims=True))).astype(BF)
        dvt_ref[hs, :] = dot_nt(dh, p.astype(BF)).astype(BF)
        dqt_ref[hs, :] = (dot(kt[hs, :], ds) * SCALE).astype(BF)
        dkt_ref[hs, :] = dot_nt(qt[hs, :], ds).astype(BF)
    back = dot(dqt_ref[...].astype(F32).T.astype(BF), wq[...])
    back += dot(dkt_ref[...].astype(F32).T.astype(BF), wk[...])
    back += dot(dvt_ref[...].astype(F32).T.astype(BF), wv[...])
    zhat, inv = standardize(one[...])
    g1 = g2 + norm_back(back, zhat, inv, as_row(g_self))
    dg_self[...] = jnp.sum(back * zhat, axis=0, keepdims=True)
    g1_ref[...] = g1
    gc = (keep * g1).astype(BF)
    grads[768:1536, :] = (keep * g1).T.astype(BF)
    for r in range(4):
        for k, part in enumerate((dqt_ref, dkt_ref, dvt_ref, at_ref, attn)):
            mine[r][k * 192 : (k + 1) * 192, :] = part[r * 192 : (r + 1) * 192, :]
    do = dot_nt(wo_c[...], gc).astype(BF)
    pay[0:768, :] = do
    deltas = []
    for h in range(4 * GROUP):
        hs = slice(h * HEAD, (h + 1) * HEAD)
        deltas.append(
            jnp.sum(do[hs, :].astype(F32) * attn[hs, :].astype(F32), axis=0, keepdims=True)
        )
    parts = list(split3(lse[...])) + list(split3(stack_rows(deltas, 16))[:2])
    pay[768:848, :] = jnp.concatenate(parts, 0).astype(BF)


def bit(v, k):
    return lax.bitwise_and(lax.shift_right_logical(v, k), 1)


def place_of(me, b, bits):
    v = lax.bitwise_xor(me, b)
    return 4 * bit(v, bits[0]) + 2 * bit(v, bits[1]) + bit(v, bits[2])


def pack(whole, third, third_rolled, put):
    low = lax.broadcasted_iota(jnp.int32, (48, 128), 1) < HEAD
    for b in range(8):
        r = 96 * b
        tail = jnp.where(low, third[r : r + 48], third_rolled[r + 48 : r + 96])
        put(b, jnp.concatenate([whole[r : r + 96], tail], 0).astype(BF))


def pack_halves(full, put0, put1):
    low = lax.broadcasted_iota(jnp.int32, (full.shape[0], 128), 1) < HEAD
    a, b, c = full[:, 0:128], full[:, 128:256], full[:, 256:384]
    b_turned, c_turned = pltpu.roll(b, HEAD, 1), pltpu.roll(c, HEAD, 1)
    pack(a, b, b_turned, put0)
    pack(jnp.where(low, b_turned, c_turned), c_turned, c, put1)


def latent_weights(dp_ref, *refs):
    me = dp_ref[0]
    norms, grads, heads = refs[:4], refs[4:8], refs[8:12]
    keep, send, one_keep, one_send, rows, one_rows = refs[12:]
    for k in range(5):
        if k < 3:
            left = jnp.concatenate([n[...] for n in norms], 1)
        else:
            at = (k - 3) * 768
            left = jnp.concatenate([g[at : at + 768, :] for g in grads], 1)
        right = jnp.concatenate([h[k * 192 : (k + 1) * 192, :] for h in heads], 1)
        full = dot_nt(left, jnp.concatenate([right, right[128:192]], 0))

        def put(b, piece, k=k):
            if k < 4:
                rows[place_of(me, b, (1, 0, 2)), k * 144 : (k + 1) * 144, :] = piece
            else:
                one_rows[place_of(me, b, (0, 1, 2)), :, :] = piece

        pack(full[:, :128], full[:, 128:], full[:, 128:], put)
    keep[...] = rows[0:4]
    send[...] = rows[4:8]
    one_keep[...] = one_rows[0:4]
    one_send[...] = one_rows[4:8]


def total(a, b):
    return a.astype(F32) + b.astype(F32)


def mix_first(dw, dw_got, up, up_got, down, down_got, *outs):
    sent, far_keep, mlp_keep, mlp_send = outs
    far_keep[...] = total(dw[0:4], dw_got[0:4]).astype(BF)
    sent[...] = total(dw[4:8], dw_got[4:8]).astype(BF)
    for k, out in enumerate((mlp_keep, mlp_send)):
        out[0:576, :] = total(up[k], up_got[k]).astype(BF)
        out[576:1152, :] = total(down[k], down_got[k]).astype(BF)


def mix_second(dw, dw_got, far, got, one_send, keep, send, far_send):
    keep[...] = total(dw[0:4], dw_got[0:4]).astype(BF)
    send[0:1728, :] = total(dw[4:8], dw_got[4:8]).astype(BF).reshape(1728, 128)
    send[1728:2304, :] = one_send[...].reshape(576, 128)
    far_send[...] = total(far[...], got[...]).astype(BF)


def mix_third(dw, got, far_got, one, own, own_got, *outs):
    keep, send, one_keep, own_keep, own_send = outs
    dw_got = got[0:1728, :].reshape(4, 432, 128)
    one_got = got[1728:2304, :].reshape(4, 144, 128)
    keep[...] = (total(dw[0:2], dw_got[0:2]) + far_got[0:2].astype(F32)).astype(BF)
    part = total(dw[2:4], dw_got[2:4]) + far_got[2:4].astype(F32)
    send[0:864, :] = part.astype(BF).reshape(864, 128)
    one_keep[...] = total(one[0:2], one_got[0:2]).astype(BF)
    send[864:1152, :] = total(one[2:4], one_got[2:4]).astype(BF).reshape(288, 128)
    own_keep[...] = total(own[0:2], own_got[0:2]).astype(BF)
    own_send[...] = total(own[2:4], own_got[2:4]).astype(BF)


def mix_fourth(dw, got, one, own, own_got, keep, send):
    for k, out in enumerate((keep, send)):
        out[0:432, :] = total(dw[k], got[k * 432 : (k + 1) * 432, :]).astype(BF)
        at = 864 + k * 144
        out[432:576, :] = total(one[k], got[at : at + 144, :]).astype(BF)
        out[576:1152, :] = total(own[k], own_got[k]).astype(BF)


def unpack(v, out):
    out[:, 0:128] = v[0:96]
    out[0:48, 128:192] = v[96:144, 0:64]
    out[48:96, 128:192] = v[96:144, 64:128]


def last_mlp(kept, got, *outs):
    sums = total(kept[...], got[...])
    for k in range(2):
        for c in range(6):
            at = (6 * k + c) * 96
            outs[k][:, c * 128 : (c + 1) * 128] = sums[at : at + 96]


def last_heads(kept, got, *outs):
    sums = total(kept[...], got[...])
    for k, out in enumerate(outs):
        unpack(sums[k * 144 : (k + 1) * 144], out)


def cross_backward(dp_ref, *refs, half):
    me = dp_ref[0]
    pays = refs[:4]
    tnt, ltt, tbs, hot, w0, w1, kn, vn, kt, qt = refs[4:14]
    rest = refs[14:]
    if half == 0:
        early, dg_in, rest = rest[0], rest[1], rest[2:]
        dk, dv, mine, other, dw0, dw1, dg = rest[:7]
    else:
        dk, dv, dq_out, dw0, dw1, dg = rest[:6]
    dq, do, own, lse, delta = rest[-5:]
    for r in range(4):
        st = pays[r][768:848, :].astype(F32)
        sums = (st[0:16] + st[16:32] + st[32:48], st[48:64] + st[64:80])
        for gi in range(2):
            src = (2 * half + gi) ^ r
            do[gi * 192 : (gi + 1) * 192, r * LAT : (r + 1) * LAT] = pays[r][
                src * 192 : (src + 1) * 192, :
            ]
            for j in range(GROUP):
                for table, v in zip((lse, delta), sums):
                    at = src * GROUP + j
                    table[gi * GROUP + j, r : r + 1, :] = v[at : at + 1, :]
    fill_masks(tbs[...], own)
    block_rows = hot[...]

    def two_heads(i, _):
        lanes = pl.ds(pl.multiple_of(i * 128, 128), 128)
        tb = tbs[...]
        qp, dop = qt[lanes, :], do[lanes, :]
        s = dot(widen(kn[:, lanes], own[...]), pile(qp))
        dp = dot(widen(vn[:, lanes], own[...]), pile(dop))
        probs, grads = [], []
        for j in range(2):
            h = 2 * i + j
            rows = [lse[h, b : b + 1, :] for b in range(NSEG)]
            p = jnp.exp(s[:, j * LAT : (j + 1) * LAT] - pick(tb, rows))
            rows = [delta[h, b : b + 1, :] for b in range(NSEG)]
            ds = (p * (dp[:, j * LAT : (j + 1) * LAT] - pick(tb, rows))).astype(BF)
            probs.append(widen(p.astype(BF), own[...]))
            grads.append(widen(ds, own[...]))
            at = pl.ds(pl.multiple_of(i * 128 + j * HEAD, HEAD), HEAD)
            kth = kt[at, :]
            k4 = jnp.concatenate([kth * block_rows[b : b + 1, :] for b in range(NSEG)], 0)
            dqh = (dot(k4, ds) * SCALE).astype(BF)
            dq[at, :] = jnp.concatenate(
                [dqh[b * HEAD : (b + 1) * HEAD, :] for b in range(NSEG)], 1
            )
        top = lax.broadcasted_iota(jnp.int32, qp.shape, 0) < HEAD
        zero = jnp.zeros_like(qp)
        for out, parts, t in ((dk, grads, qp), (dv, probs, dop)):
            right = jnp.concatenate([jnp.where(top, t, zero), jnp.where(top, zero, t)], 1)
            out[:, lanes] = dot_nt(jnp.concatenate(parts, 1), right).astype(BF)
        return 0

    lax.fori_loop(0, 3, two_heads, 0)

    for k in range(3):
        full = dot_nt(ltt[...], dq[...]) if k == 2 else dot(tnt[...], (dk, dv)[k][...])

        def put0(b, piece, k=k):
            dw0[place_of(me, b, (0, 1, 2)), k * 144 : (k + 1) * 144, :] = piece

        def put1(b, piece, k=k):
            dw1[place_of(me, b, (0, 1, 2)), k * 144 : (k + 1) * 144, :] = piece

        pack_halves(full, put0, put1)
        at = ((k + 1) % 3) * 192
        w = jnp.concatenate([w0[at : at + 192, :], w1[at : at + 192, :]], 0).astype(F32)
        prod = full * w.T
        part = prod[:, 0:128] + prod[:, 128:256] + prod[:, 256:384]
        if k == 0:
            gain_tok = part
            continue
        if k == 1:
            part += gain_tok
        part = jnp.sum(part.T, axis=0, keepdims=True)
        dg[k - 1 : k, :] = part if half == 1 else dg_in[k - 1 : k, :] + part
    if half == 0:
        for b in range(NSEG):
            out = (mine, other)[b & 1]
            out[b >> 1, 0:384, :] = dq[:, b * LAT : (b + 1) * LAT]
            out[b >> 1, 384:768, :] = early[:, b * LAT : (b + 1) * LAT]
    else:
        dq_out[...] = dq[...]


def pair_queries(mine, got, keep, send):
    for k, out in enumerate((keep, send)):
        for g in range(4):
            at, there = g * 192, (g ^ 1) * 192
            v = total(mine[k, at : at + 192, :], got[k, there : there + 192, :])
            out[at : at + 192, :] = v.astype(out.dtype)


def opening(side_ref, lat, gain, wq, wk, wv, out, ws, first):
    y = (standardize(lat[...].astype(F32))[0] * as_row(gain)).astype(BF)
    out[...] = y
    for k, w in enumerate((wq, wk, wv)):
        ws[k * 192 : (k + 1) * 192, :] = w[...]
    first[0:128, :] = y
    first[128:416, :] = ws[pl.ds(pl.multiple_of(side_ref[0] * 288, 16), 288), :]


def stack_weights(side_ref, *refs):
    stack, half, last = refs[5:]
    for k in range(5):
        stack[k * 192 : (k + 1) * 192, :] = refs[k][...]
    half[...] = stack[pl.ds(pl.multiple_of(side_ref[0] * 320, 16), 320), :]
    last[...] = stack[640:960, :]


def prepare(rank_ref, ids, owner, tok, gain, out, out_t, tbs, hot):
    rank = rank_ref[0]
    rows = tok.shape[0]
    mine = ids[:, 0:rows]
    for r in range(1, ids.shape[1] // rows):
        mine = jnp.where(rank == r, ids[:, r * rows : (r + 1) * rows], mine)
    block = jnp.zeros((1, rows), jnp.int32)
    for seg in range(NSEG):
        block = jnp.where(mine == seg, lax.bitwise_xor(owner[0, seg], rank), block)
    block = block.astype(F32)
    eight = lax.broadcasted_iota(jnp.int32, (8, rows), 0).astype(F32)
    hot[...] = jnp.where(jnp.broadcast_to(block, (8, rows)) == eight, 1.0, 0.0).astype(BF)
    tbs[...] = jnp.broadcast_to(block, (128, rows)).T
    xhat, _ = standardize(tok[...].astype(F32))
    y = (xhat * as_row(gain)).astype(BF)
    out[...] = y
    out_t[...] = y.astype(F32).T.astype(BF)


def token_end(dk0, dv0, dk1, dv1, w0, w1, w2, w3, tok, gain, out):
    xhat, inv = standardize(tok[...].astype(F32))
    dy = None
    for k, (a, b) in enumerate(((dk0, dk1), (dv0, dv1))):
        at = (k + 1) * 192
        for grad, pieces in ((a, (w0, w1)), (b, (w2, w3))):
            w = jnp.concatenate([p[at : at + 192, :] for p in pieces], 0)
            part = dot(grad[...], w)
            dy = part if dy is None else dy + part
    out[...] = norm_back(dy, xhat, inv, as_row(gain))


def latent_end(*refs):
    near, far, w0, w1, w2, w3, lat, g1, gain, out, dqt = refs
    for g in range(4):
        at, there = g * 192, (g ^ 2) * 192
        v = near[at : at + 192, :] + far[there : there + 192, :].astype(F32)
        dqt[at : at + 192, :] = v.astype(BF)
    wq = jnp.concatenate([w[0:192, :] for w in (w0, w1, w2, w3)], 0)
    dlat = dot(dqt[...].astype(F32).T.astype(BF), wq)
    xhat, inv = standardize(lat[...].astype(F32))
    out[...] = g1[...] + norm_back(dlat, xhat, inv, as_row(gain))


def per_device(
    tokens,
    latents,
    segment_ids,
    segment_block,
    block_mask,
    gain_tok,
    gain_cross,
    gain_self,
    gain_mlp,
    wq_cross,
    wk_cross,
    wv_cross,
    wo_cross,
    wq_self,
    wk_self,
    wv_self,
    wo_self,
    w_up,
    w_down,
    d_latents,
):
    mp, dp = lax.axis_size("mp"), lax.axis_size("dp")
    fine = dp // 8
    low = fine.bit_length() - 1
    rank, place = lax.axis_index("mp"), lax.axis_index("dp")
    row = place // fine
    side = (place >> low) & 1
    _, n_tok, width = tokens.shape
    hid = w_up.shape[1]
    part = width // 8
    tok, lat, cot = tokens[0], latents[0], d_latents[0]
    full, sq = (LAT, width), (width, LAT)

    def after(v, *first):
        return lax.optimization_barrier((v,) + first)[0]

    def together(*v):
        return lax.optimization_barrier(v)

    def swap(v, r):
        return lax.ppermute(v, "mp", [(i, i ^ r) for i in range(mp)])

    def cross(v, k):
        flip = (1 << low) * (1, 2, 4, 6)[k]
        return lax.ppermute(v, "dp", [(i, i ^ flip) for i in range(dp)])

    def share(outs):
        return [outs[0]] + [swap(outs[r], r) for r in (1, 2, 3)]

    def add(a, b):
        return a.astype(F32) + b.astype(F32)

    latn, own, first = kernel_call(
        opening,
        [(full, BF), ((576, width), BF), ((416, width), BF)],
        0,
        lat,
        gain_cross,
        wq_cross.T,
        wk_cross.T,
        wv_cross.T,
        scalars=(side,),
        vmem=56,
    )
    l_near, near = swap(latn, 1), swap(own, 1)
    first2 = swap(first, 2)
    stack, half, last = kernel_call(
        stack_weights,
        [((960, width), BF)] + [((320, width), BF)] * 2,
        0,
        wo_cross.T,
        after(wq_self.T, latn),
        wk_self.T,
        wv_self.T,
        wo_self.T,
        scalars=(side,),
        vmem=56,
    )
    tokn, toknt, tbs, hot = kernel_call(
        prepare,
        [((n_tok, width), BF), ((width, n_tok), BF), ((n_tok, 128), F32), ((8, n_tok), BF)],
        2 * 10**9,
        segment_ids,
        segment_block,
        after(tok, stack),
        gain_tok,
        scalars=(rank,),
        tables=(1,),
        vmem=56,
    )
    first2 = after(first2, tokn)
    lats = [latn, l_near, first2, swap(first2, 1)]
    keep = lax.dynamic_index_in_dim(block_mask[0], rank, keepdims=False)

    def cross_call(weights, early, gate):
        second = bool(early)
        outs = kernel_call(
            functools.partial(cross_forward, second=second),
            [((n_tok, 384), BF)] * 2
            + [((384, n_tok), BF), ((384, NSEG * LAT), BF)]
            + [((2, SHARE * (1 + second), LAT), BF)] * 2
            + [((576, width), BF)] * (2 * second),
            9 * 10**9,
            after(tokn, *gate),
            *lats,
            tbs,
            hot,
            *weights,
            *early,
            scalars=(side,),
            far=range(4),
            scratch=[((n_tok, 384), BF)] * 2
            + [((384, n_tok), BF)] * 2
            + [((384, NSEG * LAT), BF), ((n_tok, 512), BF), ((NSEG, 8, LAT), F32)]
            + [pltpu.SemaphoreType.DMA((4,))],
            vmem=56,
        )
        return outs[:4], outs[4:6], outs[6:]

    half2, last2 = swap(after(half, first), 2), swap(after(last, first), 2)
    stack_near = swap(stack, 1)
    far_x = cross(first2[128:416], 0)
    saved0, pays, _ = cross_call([own, near], [], [])
    far_x, half2, stack_near, *pays = together(far_x, half2, stack_near, *pays)
    half_x, half3 = cross(after(half2, far_x), 0), swap(half2, 1)
    saved1, (mine, other), (far, far_near) = cross_call(
        [far_x, swap(far_x, 1)], pays, [half3]
    )
    other, half_x, last2 = together(other, half_x, last2)
    got = swap(other, 1)
    mine, pay_send = kernel_call(merge_pair, [((2 * SHARE, LAT), BF)] * 2, 10**9, mine, got)
    pay_far = swap(pay_send, 2)
    pieces = [stack, stack_near, half2, half_x, last2]
    pieces += [half3, swap(after(half_x, mine), 1), swap(after(last2, mine), 1)]
    weights = [((768, width), BF)] * 5
    pays = [mine, pay_far]

    attn, lse, one, two, selfn, mlp_in, at, probs, kts, qts, vs = kernel_call(
        latent_forward,
        [
            (sq, BF),
            ((16, LAT), F32),
            (full, F32),
            (full, F32),
            (sq, BF),
            (full, BF),
            (sq, BF),
            ((12 * LAT, LAT), F32),
            (sq, BF),
            (sq, BF),
            (full, BF),
        ],
        8 * 10**9,
        *pays,
        lat,
        gain_self,
        gain_mlp,
        *pieces,
        scalars=(keep, side),
        scratch=weights,
        vmem=56,
    )
    x_far, x_near = swap(mlp_in, 2), swap(mlp_in, 1)
    c_far = after(swap(after(cot, pay_send), 2), mlp_in)
    cots = [cot, swap(after(cot, pay_send), 1), c_far, swap(c_far, 1)]
    dh, cot_t, lat_t = kernel_call(
        mlp_before,
        [((4 * LAT, hid), F32), ((width, 4 * LAT), BF), ((width, 4 * LAT), BF)],
        4 * 10**9,
        *cots[:3],
        after(cots[3], mlp_in),
        *lats,
        w_down,
    )
    xs = [mlp_in, x_near, x_far, swap(after(x_far, dh), 1)]
    n_far = swap(after(selfn, dh), 2)
    mine, other, hidden, dpre = kernel_call(
        mlp_main,
        [((2, LAT, width), BF)] * 2 + [((4 * LAT, hid), BF)] * 2,
        3 * 10**9,
        *xs,
        dh,
        w_up,
    )
    got = swap(other, 1)
    back_near, back_send = add(mine[0], got[0]), add(mine[1], got[1]).astype(BF)
    back_far = swap(back_send, 2)
    rows_of = part * hid // 128
    up, up_send, down, down_send = kernel_call(
        mlp_weights,
        [((4, rows_of, 128), BF)] * 4,
        3 * 10**9,
        *xs,
        cot_t,
        hidden,
        after(dpre, back_send),
        scalars=(row,),
        scratch=[((8, rows_of, 128), BF)],
    )
    up_got, down_got = cross(up_send, 1), cross(down_send, 0)
    n_far = swap(after(selfn, up_send), 2)
    n_near = swap(after(selfn, up_send), 1)

    pay, g1, grads, m0, m1, m2, m3, dg_mlp, dg_self = kernel_call(
        latent_backward,
        [((848, LAT), BF), (full, F32), ((1536, LAT), BF)]
        + [((960, LAT), BF)] * 4
        + [((1, width), F32)] * 2,
        9 * 10**9,
        back_near,
        after(back_far, up_send),
        two,
        one,
        cot,
        attn,
        at,
        lse,
        probs,
        kts,
        qts,
        vs,
        gain_self,
        gain_mlp,
        *pieces,
        scalars=(keep, side),
        scratch=[(sq, BF)] * 3 + weights,
        vmem=VMEM_LATENT,
    )
    pay, up_got, down_got, n_far = together(pay, up_got, down_got, n_far)
    p_far, p_near = swap(pay, 2), swap(pay, 1)
    pays = [pay, p_near, p_far, swap(p_far, 1)]

    def part_sum(kept, got):
        n = kept.shape[0] // 2
        return add(kept[:n], got[:n]).astype(BF), add(kept[n:], got[n:]).astype(BF)

    up, up_send = part_sum(up, up_got)
    down, down_send = part_sum(down, down_got)
    forwards = kernel_call(
        mlp_out, [((2, LAT, width), BF)] * 2, 10**9, after(hidden, pay), w_down
    )
    f_got = swap(forwards[1], 1)
    grads = after(grads, pay)
    g_far, g_near = swap(grads, 2), swap(grads, 1)
    m_near, n_last = swap(after(m1, p_far), 1), swap(after(n_far, p_far), 1)

    def cross_back(half, ws, saved, more, gate):
        return kernel_call(
            functools.partial(cross_backward, half=half),
            [((n_tok, 384), BF)] * 2
            + ([((2, 768, LAT), BF)] * 2 if half == 0 else [((384, NSEG * LAT), BF)])
            + [((8, 432, 128), BF)] * 2
            + [((2, width), F32)],
            11 * 10**9,
            after(pays[0], *gate),
            *pays[1:],
            toknt,
            lat_t,
            tbs,
            hot,
            *ws,
            *saved,
            *more,
            scalars=(row,),
            scratch=[((384, NSEG * LAT), BF)] * 2
            + [((n_tok, 512), BF)]
            + [((8, NSEG, LAT), F32)] * 2,
            vmem=VMEM_CROSS,
        )

    dk1, dv1, dq1, dw, other, dg_cross = cross_back(
        1, (far, far_near), saved1, (), (up_send, down_send)
    )
    up_got, down_got = cross(up_send, 0), cross(down_send, 1)
    other, up_got, down_got, g_far, g_near, m_near, n_last, f_got = together(
        other, up_got, down_got, g_far, g_near, m_near, n_last, f_got
    )
    f_near, f_send = add(forwards[0][0], f_got[0]), add(forwards[0][1], f_got[1]).astype(BF)
    norms = [selfn, n_near, n_far, n_last]
    m2, m3 = after(m2, other), after(m3, other)
    sent, far_dw, mlp_keep, mlp_send = kernel_call(
        mix_first,
        [((4, 432, 128), BF)] * 2 + [((2 * rows_of, 128), BF)] * 2,
        10**9,
        dw,
        swap(other, 1),
        up,
        up_got,
        down,
        down_got,
    )
    dk0, dv0, dq_mine, dq_other, dw, other, dg_cross = cross_back(
        0, (own, near), saved0, (dq1, dg_cross), (sent,)
    )
    got, mlp_got = cross(sent, 0), cross(mlp_send, 2)
    m_far, m_last = swap(m2, 2), swap(m3, 3)
    other, got, mlp_got, m_far, m_last = together(other, got, mlp_got, m_far, m_last)
    dg_tok, dg_cross = (
        dg_cross[k : k + 1] / g.astype(F32)[None, :] for k, g in enumerate((gain_tok, gain_cross))
    )
    gains = jnp.concatenate([dg_tok, dg_cross, dg_self, dg_mlp], 0)
    dw_got, g_last = swap(other, 1), swap(after(g_far, other), 1)
    dq_got, gains_got = swap(after(dq_other, other), 1), swap(after(gains, other), 1)
    heads = [m0, m_near, m_far, m_last]
    mine, mine_send, one_keep, one_send = kernel_call(
        latent_weights,
        [((4, 576, 128), BF)] * 2 + [((4, 144, 128), BF)] * 2,
        2 * 10**9,
        *norms,
        grads,
        g_near,
        g_far,
        g_last,
        *heads,
        scalars=(row,),
        scratch=[((8, 576, 128), BF), ((8, 144, 128), BF)],
    )
    dw, sent, far_send = kernel_call(
        mix_second,
        [((4, 432, 128), BF), ((2304, 128), BF), ((4, 432, 128), BF)],
        10**9,
        dw,
        dw_got,
        far_dw,
        got,
        one_send,
    )
    got, far_got, mine_got = cross(sent, 0), swap(far_send, 2), cross(mine_send, 1)
    gains = after(gains + gains_got, sent)
    gains_got, f_far = swap(gains, 2), swap(after(f_send, sent), 2)
    (out_tok,) = kernel_call(
        token_end,
        [((n_tok, width), F32)],
        5 * 10**9,
        dk0,
        dv0,
        dk1,
        after(dv1, sent, mine_send, far_send),
        own,
        near,
        far,
        far_near,
        tok,
        gain_tok,
        vmem=24,
    )
    got, far_got, mine_got, gains_got, f_far, out_tok = together(
        got, far_got, mine_got, gains_got, f_far, out_tok
    )
    dw, sent, one_keep, mine, mine_send = kernel_call(
        mix_third,
        [
            ((2, 432, 128), BF),
            ((1152, 128), BF),
            ((2, 144, 128), BF),
            ((2, 576, 128), BF),
            ((2, 576, 128), BF),
        ],
        10**9,
        dw,
        got,
        far_got,
        one_keep,
        mine,
        mine_got,
    )
    got, mine_got = cross(sent, 1), cross(mine_send, 0)
    gains = after(gains + gains_got, sent)
    gains_got = cross(gains, 0)
    dq_near, dq_send = kernel_call(
        pair_queries, [(sq, F32), (sq, BF)], 10**9, after(dq_mine, sent), dq_got
    )
    dq_far = swap(dq_send, 2)
    mlps = kernel_call(
        last_mlp, [((96, hid), F32)] * 2, 10**9, mlp_keep, after(mlp_got, dq_send)
    )
    got, mine_got, gains_got, dq_far, *mlps = together(got, mine_got, gains_got, dq_far, *mlps)
    kept, sent = kernel_call(
        mix_fourth, [((1152, 128), BF)] * 2, 10**9, dw, got, one_keep, mine, mine_got
    )
    got = cross(sent, 2)
    gains = after(gains + gains_got, sent)
    gains = gains + cross(gains, 1) + (cross(gains, 2) + cross(gains, 3))
    for k in range(low):
        gains = gains + lax.ppermute(gains, "dp", [(i, i ^ (1 << k)) for i in range(dp)])
    new_latents = (two + add(f_near, f_far)).astype(BF)
    grad_lat, _ = kernel_call(
        latent_end,
        [(full, F32), (sq, BF)],
        3 * 10**9,
        dq_near,
        after(dq_far, sent),
        own,
        near,
        far,
        far_near,
        lat,
        g1,
        gain_cross,
    )
    lasts = kernel_call(last_heads, [((96, 192), F32)] * 8, 10**9, kept, got)

    groups = [list(range(k * fine, (k + 1) * fine)) for k in range(8)]

    def shard(v):
        if fine == 1:
            return v
        return lax.psum_scatter(v, "dp", scatter_dimension=0, axis_index_groups=groups, tiled=True)

    order = (lasts[2], lasts[0], lasts[1], *lasts[3:], *mlps)
    return (
        new_latents[None],
        out_tok[None],
        grad_lat[None],
        *(gains[k] for k in range(4)),
        *(shard(v) for v in order),
    )


def solution(mesh):
    rows, cols, lone = P("dp", "mp", None), P(None, "mp"), P("dp", None)
    in_specs = (rows, rows, lone, lone, lone) + (P(),) * 4 + (cols,) * 10 + (rows,)
    out_specs = (rows,) * 3 + (P(),) * 4 + (P("dp", "mp"),) * 10
    return jax.shard_map(
        per_device, mesh=mesh, in_specs=in_specs, out_specs=out_specs, check_vma=False
    )
```

```python
import functools
import math

import jax
import jax.numpy as jnp
from jax import lax
from jax.experimental import pallas as pl
from jax.experimental.pallas import tpu as pltpu
from jax.sharding import PartitionSpec as P

HEAD = 64
LAT = 128
NSEG = 4
GROUP = 3
EPS = 1e-05
FAR = -1e30
F32 = jnp.float32
BF = jnp.bfloat16
SCALE = 1.0 / math.sqrt(HEAD)
MIB = 1024 * 1024
VMEM_CROSS = 20
VMEM_LATENT = 20


def dot(a, b):
    return lax.dot_general(a, b, (((1,), (0,)), ((), ())), preferred_element_type=F32)


def dot_nt(a, b):
    return lax.dot_general(a, b, (((1,), (1,)), ((), ())), preferred_element_type=F32)


def standardize(v):
    center = v - jnp.mean(v, axis=-1, keepdims=True)
    inv = lax.rsqrt(jnp.mean(center * center, axis=-1, keepdims=True) + EPS)
    return center * inv, inv


def norm_back(dy, xhat, inv, gain):
    s = dy * gain
    return inv * (
        s - jnp.mean(s, axis=-1, keepdims=True) - xhat * jnp.mean(s * xhat, axis=-1, keepdims=True)
    )


def as_row(gain):
    return gain[...].astype(F32).reshape(1, -1)


def kernel_call(body, outs, flops, *args, scalars=(), scratch=(), tables=(), vmem=12, far=(), loose=()):
    n = len(scalars)
    specs = [pl.BlockSpec(memory_space=pltpu.SMEM)] * n
    specs += [
        pl.BlockSpec(
            memory_space=pltpu.SMEM if i in tables else pl.ANY if i in loose else pltpu.VMEM
        )
        for i in range(len(args))
    ]
    moved = sum(a.size * a.dtype.itemsize for a in args)
    moved += sum(math.prod(s) * jnp.dtype(d).itemsize for s, d in outs)
    return pl.pallas_call(
        body,
        out_shape=[jax.ShapeDtypeStruct(s, d) for s, d in outs],
        in_specs=specs,
        out_specs=[
            pl.BlockSpec(memory_space=pltpu.HBM if i in far else pltpu.VMEM)
            for i in range(len(outs))
        ],
        scratch_shapes=[
            pltpu.VMEM(*x) if isinstance(x, tuple) else x for x in scratch
        ],
        compiler_params=pltpu.CompilerParams(vmem_limit_bytes=vmem * MIB),
        cost_estimate=pl.CostEstimate(flops=flops, bytes_accessed=moved, transcendentals=0),
    )(*[jnp.reshape(s, (1,)).astype(jnp.int32) for s in scalars], *args)


def split3(v):
    a = v.astype(BF).astype(F32)
    b = (v - a).astype(BF).astype(F32)
    return a, b, v - a - b


def stack_rows(rows, pad):
    return jnp.concatenate(rows + [jnp.zeros((pad - len(rows), rows[0].shape[1]), F32)], 0)


def pick(tb, rows):
    out = rows[NSEG - 1]
    for b in range(NSEG - 2, -1, -1):
        out = jnp.where(tb == b, rows[b], out)
    return out


def widen(v, own):
    return jnp.concatenate([v] * NSEG, 1) * own


def pile(t):
    top = lax.broadcasted_iota(jnp.int32, (2 * HEAD, LAT), 0) < HEAD
    zero = jnp.zeros((2 * HEAD, LAT), t.dtype)
    rows = []
    for b in range(NSEG):
        part = t[:, b * LAT : (b + 1) * LAT]
        rows.append(
            jnp.concatenate([jnp.where(top, part, zero), jnp.where(top, zero, part)], 1)
        )
    return jnp.concatenate(rows, 0)


def fill_masks(tb, own):
    for b in range(NSEG):
        own[:, b * 128 : (b + 1) * 128] = jnp.where(tb == b, 1.0, 0.0).astype(BF)


SHARE = 416


def cross_forward(side_ref, *refs, second):
    x_ref, l0, l1, first2, first3, tbs, hot = refs[:7]
    rest = refs[7:]
    if second:
        halves, early, rest = rest[:2], rest[2:4], rest[4:]
    else:
        pieces, rest = rest[:2], rest[2:]
    mine, other = rest[:2]
    if second:
        pieces, rest = rest[2:4], rest[4:]
        for piece, by_mp, by_dp in zip(pieces, (first2, first3), halves):
            low = side_ref[0] == 0
            piece[0:288, :] = jnp.where(low, by_mp[128:416, :], by_dp[...])
            piece[288:576, :] = jnp.where(low, by_dp[...], by_mp[128:416, :])
    else:
        rest = rest[2:]
    kn, vt, qt, own, stat = rest
    w = [
        jnp.concatenate([p[k * 192 : (k + 1) * 192, :] for p in pieces], 0) for k in range(3)
    ]
    lat = jnp.concatenate([l0[...], l1[...], first2[0:128, :], first3[0:128, :]], 0)
    qt[...] = (dot_nt(w[0], lat).astype(BF).astype(F32) * SCALE).astype(BF)
    kn[...] = dot_nt(x_ref[...], w[1]).astype(BF)
    vt[...] = dot_nt(x_ref[...], w[2]).T.astype(BF)
    fill_masks(tbs[...], own)
    base = SHARE if second else 0
    stat[...] = jnp.zeros_like(stat)
    block_rows = hot[...]

    def two_heads(i, _):
        lanes = pl.ds(pl.multiple_of(i * 128, 128), 128)
        tb = tbs[...]
        s = dot(widen(kn[:, lanes], own[...]), pile(qt[lanes, :]))
        for j in range(2):
            sj = s[:, j * LAT : (j + 1) * LAT]
            top = [
                jnp.max(jnp.where(tb == b, sj, FAR), axis=0, keepdims=True) for b in range(NSEG)
            ]
            p = jnp.exp(sj - pick(tb, top)).astype(BF)
            total_of = dot(block_rows, p)
            rows = pl.ds(pl.multiple_of(i * 128 + j * HEAD, HEAD), HEAD)
            vth = vt[rows, :]
            v4 = jnp.concatenate([vth * block_rows[b : b + 1, :] for b in range(NSEG)], 0)
            o = dot(v4, p)
            to = pl.ds(pl.multiple_of(base + i * 128 + j * HEAD, 32), HEAD)
            for b in range(NSEG):
                tot = total_of[b : b + 1, :]
                some = tot > 0.0
                safe = jnp.where(some, tot, 1.0)
                stat[b, pl.ds(2 * i + j, 1), :] = jnp.where(some, top[b] + jnp.log(safe), FAR)
                out = (mine, other)[b & 1]
                out[b >> 1, to, :] = (o[b * HEAD : (b + 1) * HEAD, :] / safe).astype(BF)
        return 0

    lax.fori_loop(0, 3, two_heads, 0, unroll=True)
    for b in range(NSEG):
        out = (mine, other)[b & 1]
        out[b >> 1, base + 384 : base + SHARE, :] = jnp.concatenate(
            list(split3(stat[b])) + [jnp.zeros((8, LAT), F32)], 0
        ).astype(BF)
    if second:
        for out, first in ((mine, early[0]), (other, early[1])):
            out[:, 0:SHARE, :] = first[...]


def merge(parts, head, lse_of):
    tables = []
    for read, _ in parts:
        one = []
        for half in range(2):
            st = read(half * SHARE + 384, 32).astype(F32)
            one.append(st[0:8] + st[8:16] + st[16:24])
        tables.append(one)
    for g in range(4):
        for j in range(GROUP):
            found = []
            for (read, flip), table in zip(parts, tables):
                src = g ^ flip
                half, at = src >> 1, (src & 1) * GROUP + j
                found.append(
                    (table[half][at : at + 1, :], read(half * SHARE + at * HEAD, HEAD).astype(F32))
                )
            top = functools.reduce(jnp.maximum, [f[0] for f in found])
            w = [jnp.exp(f[0] - top) for f in found]
            all_w = functools.reduce(jnp.add, w)
            o = functools.reduce(jnp.add, [a * f[1] for a, f in zip(w, found)]) / all_w
            head(g, j, o.astype(BF))
            lse_of(g, j, top + jnp.log(all_w))


def merge_pair(mine, got, keep, send):
    for k, out in enumerate((keep, send)):
        rows = [[], []]

        def head(g, j, o, out=out):
            at = (g >> 1) * SHARE + ((g & 1) * GROUP + j) * HEAD
            out[at : at + HEAD, :] = o

        def lse_of(g, j, v, rows=rows):
            rows[g >> 1].append(v)

        merge(
            [
                (lambda a, n, k=k: mine[k, a : a + n, :], 0),
                (lambda a, n, k=k: got[k, a : a + n, :], 1),
            ],
            head,
            lse_of,
        )
        for half in range(2):
            parts = list(split3(stack_rows(rows[half], 8))) + [jnp.zeros((8, LAT), F32)]
            out[half * SHARE + 384 : (half + 1) * SHARE, :] = jnp.concatenate(parts, 0).astype(BF)


def weight_copies(side, pieces, full, sems):
    plan = [[] for _ in full]
    for r in range(4):
        for k in range(5):
            at = 192 * k
            while at < 192 * (k + 1):
                part = at // 320 if r > 1 else 0
                end = min(192 * (k + 1), (part + 1) * 320 if r > 1 else 960)
                plan[k].append((r, part, at, end))
                at = end

    def run(k, act):
        base = sum(len(p) for p in plan[:k])
        for n, (r, part, at, end) in enumerate(plan[k]):
            to = full[k].at[r * 192 + at - 192 * k : r * 192 + end - 192 * k, :]

            def copy(src, start, to=to, n=n, size=end - at):
                act(pltpu.make_async_copy(src.at[start : start + size, :], to, sems.at[base + n]))

            if r < 2:
                copy(pieces[r], at)
            elif part == 2:
                copy(pieces[4 + 3 * (r - 2)], at - 640)
            else:
                for turn in range(2):

                    @pl.when(side == part if turn == 0 else side != part)
                    def _(turn=turn):
                        copy(pieces[2 + 3 * (r - 2) + turn], at - 320 * part)

    return run


def join_weights(side, pieces, full):
    own, near = pieces[:2]
    for r, stack in ((0, own), (1, near)):
        for k in range(5):
            full[k][r * 192 : (r + 1) * 192, :] = stack[k * 192 : (k + 1) * 192, :]
    for r, (by_mp, by_dp, last) in ((2, pieces[2:5]), (3, pieces[5:8])):
        low = side == 0
        stack = jnp.concatenate(
            [
                jnp.where(low, by_mp[...], by_dp[...]),
                jnp.where(low, by_dp[...], by_mp[...]),
                last[...],
            ],
            0,
        )
        for k in range(5):
            full[k][r * 192 : (r + 1) * 192, :] = stack[k * 192 : (k + 1) * 192, :]


def latent_forward(rank_ref, side_ref, mask_ref, *refs):
    pay = refs[:2]
    lat, g_self, g_mlp = refs[2], refs[3], refs[4]
    pieces, full, sems = refs[5:13], refs[-6:-1], refs[-1]
    (
        attn_ref,
        lse_ref,
        one_ref,
        two_ref,
        norm_ref,
        mlp_ref,
        at_ref,
        p_ref,
        kt_ref,
        qt_ref,
        v_ref,
        early_other,
        early_own,
    ) = refs[13:-6]
    wo_c, wq, wk, wv, wo = full
    keep = mask_ref[0, rank_ref[0]].astype(F32)
    weight = weight_copies(side_ref[0], pieces, full, sems)
    for k in range(5):
        weight(k, lambda copy: copy.start())

    def ready(k):
        weight(k, lambda copy: copy.wait())

    lse_rows = []

    def head(g, j, o):
        at = (g * GROUP + j) * HEAD
        attn_ref[at : at + HEAD, :] = o

    merge(
        [(lambda a, n: pay[0][a : a + n, :], 0), (lambda a, n: pay[1][a : a + n, :], 2)],
        head,
        lambda g, j, v: lse_rows.append(v),
    )
    lse_ref[...] = stack_rows(lse_rows, 16)
    attn = attn_ref[...].astype(F32).T.astype(BF)
    ready(0)
    one = lat[...].astype(F32) + keep * dot(attn, wo_c[...])
    one_ref[...] = one
    zhat, _ = standardize(one)
    x = (zhat * as_row(g_self)).astype(BF)
    norm_ref[0:768, :] = x.astype(F32).T.astype(BF)
    ready(1)
    qt_ref[...] = (dot_nt(wq[...], x).astype(BF).astype(F32) * SCALE).astype(BF)
    ready(2)
    ready(3)
    kt_ref[...] = dot_nt(wk[...], x).astype(BF)
    vt = dot_nt(wv[...], x).astype(BF)
    k = dot_nt(x, wk[...]).astype(BF)
    v_ref[...] = dot_nt(x, wv[...]).astype(BF)
    zero = jnp.zeros((HEAD, LAT), BF)
    for h in range(4 * GROUP):
        hs = slice(h * HEAD, (h + 1) * HEAD)
        ps = slice((h // 2) * 128, (h // 2) * 128 + 128)
        qh = qt_ref[hs, :]
        s = dot(k[:, ps], jnp.concatenate([qh, zero] if h % 2 == 0 else [zero, qh], 0))
        e = jnp.exp(s - jnp.max(s, axis=0, keepdims=True))
        p = e / jnp.sum(e, axis=0, keepdims=True)
        p_ref[h * LAT : (h + 1) * LAT, :] = p
        at_ref[hs, :] = dot(vt[hs, :], p.astype(BF)).astype(BF)
    ready(4)
    two = one + dot(at_ref[...].astype(F32).T.astype(BF), wo[...])
    for r, to in enumerate((early_own, early_other.at[0], norm_ref.at[768:1152, :], early_other.at[1])):
        to[0:192, :] = at_ref[r * 192 : (r + 1) * 192, :]
        to[192:384, :] = attn_ref[r * 192 : (r + 1) * 192, :]
    two_ref[...] = two
    zhat, _ = standardize(two)
    mlp_ref[...] = (zhat * as_row(g_mlp)).astype(BF)


def mlp_before(c0, c1, c2, c3, l0, l1, first2, first3, down, dh_ref, cot_t, lat_t):
    g = jnp.concatenate([c0[...], c1[...], c2[...], c3[...]], 0)
    dh_ref[...] = dot(g, down[...])
    cot_t[...] = g.astype(F32).T.astype(BF)
    lat = jnp.concatenate([l0[...], l1[...], first2[0:128, :], first3[0:128, :]], 0)
    lat_t[...] = lat.astype(F32).T.astype(BF)


def deal(v, mine, other):
    for r in range(4):
        out = (mine, other)[r & 1]
        out[r >> 1, :, :] = v[r * LAT : (r + 1) * LAT, :]


def mlp_main(x0, x1, x2, x3, dh_ref, up, *outs):
    mine, other, h_ref, d_ref = outs
    c = math.sqrt(2.0 / math.pi)
    x = jnp.concatenate([x0[...], x1[...], x2[...], x3[...]], 0)
    pre = dot(x, up[...])
    sq = pre * pre
    t = jnp.tanh(c * pre * (1.0 + 0.044715 * sq))
    h_ref[...] = (0.5 * pre * (1.0 + t)).astype(BF)
    slope = 0.5 * (1.0 + t) + 0.5 * pre * (1.0 - t * t) * c * (1.0 + 3 * 0.044715 * sq)
    d = (dh_ref[...] * slope).astype(BF)
    d_ref[...] = d
    deal(dot_nt(d, up[...]).astype(BF), mine, other)


def mlp_weights(dp_ref, x0, x1, x2, x3, gt, h_ref, d_ref, *outs):
    me = dp_ref[0]
    rows = outs[4]
    xt = jnp.concatenate([x0[...], x1[...], x2[...], x3[...]], 0).astype(F32).T.astype(BF)
    for k, (lhs, rhs) in enumerate(((xt, d_ref[...]), (gt[...], h_ref[...]))):
        full = dot(lhs, rhs).astype(BF)
        for b in range(8):
            at = place_of(me, b, ((1, 0, 2), (0, 2, 1))[k])
            for c in range(6):
                rows[at, c * 96 : (c + 1) * 96, :] = full[
                    b * 96 : (b + 1) * 96, c * 128 : (c + 1) * 128
                ]
        outs[2 * k][...] = rows[0:4]
        outs[2 * k + 1][...] = rows[4:8]


def mlp_out(h_ref, down, mine, other):
    deal(dot_nt(h_ref[...], down[...]).astype(BF), mine, other)


def latent_backward(rank_ref, side_ref, mask_ref, *refs):
    b0, b1, two, one, cot, attn, lse, p_ref, kt, qt, v, g_self, g_mlp = refs[:13]
    pieces, full = refs[13:21], refs[-5:]
    pay, g1_ref, grads, *mine, dg_mlp, dg_self = refs[21:-8]
    dqt_ref, dkt_ref, dvt_ref = refs[-8:-5]
    wo_c, wq, wk, wv, wo = full
    keep = mask_ref[0, rank_ref[0]].astype(F32)
    join_weights(side_ref[0], pieces, full)
    dmlp = b0[...] + b1[...].astype(F32)
    zhat, inv = standardize(two[...])
    g2 = cot[...].astype(F32) + norm_back(dmlp, zhat, inv, as_row(g_mlp))
    dg_mlp[...] = jnp.sum(dmlp * zhat, axis=0, keepdims=True)
    low = g2.astype(BF)
    grads[0:768, :] = g2.T.astype(BF)
    dat = dot_nt(wo[...], low).astype(BF)
    zero = jnp.zeros((HEAD, LAT), BF)
    for h in range(4 * GROUP):
        hs = slice(h * HEAD, (h + 1) * HEAD)
        ps = slice((h // 2) * 128, (h // 2) * 128 + 128)
        dh = dat[hs, :]
        p = p_ref[h * LAT : (h + 1) * LAT, :]
        dp = dot(v[:, ps], jnp.concatenate([dh, zero] if h % 2 == 0 else [zero, dh], 0))
        ds = (p * (dp - jnp.sum(p * dp, axis=0, keepdims=True))).astype(BF)
        dvt_ref[hs, :] = dot_nt(dh, p.astype(BF)).astype(BF)
        dqt_ref[hs, :] = (dot(kt[hs, :], ds) * SCALE).astype(BF)
        dkt_ref[hs, :] = dot_nt(qt[hs, :], ds).astype(BF)
    back = dot(dqt_ref[...].astype(F32).T.astype(BF), wq[...])
    back += dot(dkt_ref[...].astype(F32).T.astype(BF), wk[...])
    back += dot(dvt_ref[...].astype(F32).T.astype(BF), wv[...])
    zhat, inv = standardize(one[...])
    g1 = g2 + norm_back(back, zhat, inv, as_row(g_self))
    dg_self[...] = jnp.sum(back * zhat, axis=0, keepdims=True)
    g1_ref[...] = g1
    gc = (keep * g1).astype(BF)
    grads[768:1536, :] = (keep * g1).T.astype(BF)
    for r in range(4):
        for k, part in enumerate((dqt_ref, dkt_ref, dvt_ref)):
            to = (mine[0], mine[1].at[0], mine[2], mine[1].at[1])[r]
            to[k * 192 : (k + 1) * 192, :] = part[r * 192 : (r + 1) * 192, :]
    do = dot_nt(wo_c[...], gc).astype(BF)
    pay[0:768, :] = do
    deltas = []
    for h in range(4 * GROUP):
        hs = slice(h * HEAD, (h + 1) * HEAD)
        deltas.append(
            jnp.sum(do[hs, :].astype(F32) * attn[hs, :].astype(F32), axis=0, keepdims=True)
        )
    parts = list(split3(lse[...])) + list(split3(stack_rows(deltas, 16))[:2])
    pay[768:848, :] = jnp.concatenate(parts, 0).astype(BF)


def bit(v, k):
    return lax.bitwise_and(lax.shift_right_logical(v, k), 1)


def place_of(me, b, bits):
    v = lax.bitwise_xor(me, b)
    return 4 * bit(v, bits[0]) + 2 * bit(v, bits[1]) + bit(v, bits[2])


def pack(whole, third, third_rolled, put):
    low = lax.broadcasted_iota(jnp.int32, (48, 128), 1) < HEAD
    for b in range(8):
        r = 96 * b
        tail = jnp.where(low, third[r : r + 48], third_rolled[r + 48 : r + 96])
        put(b, jnp.concatenate([whole[r : r + 96], tail], 0).astype(BF))


def pack_halves(full, put0, put1):
    low = lax.broadcasted_iota(jnp.int32, (full.shape[0], 128), 1) < HEAD
    a, b, c = full[:, 0:128], full[:, 128:256], full[:, 256:384]
    b_turned, c_turned = pltpu.roll(b, HEAD, 1), pltpu.roll(c, HEAD, 1)
    pack(a, b, b_turned, put0)
    pack(jnp.where(low, b_turned, c_turned), c_turned, c, put1)


def latent_weights(dp_ref, *refs):
    me = dp_ref[0]
    norms, grads, (h0, h1, h_far), (e0, e1) = refs[:4], refs[4:8], refs[8:11], refs[11:13]
    far = norms[2]
    heads = (h0, h1.at[0], h_far.at[0:576, :], h_far.at[576:1152, :])
    outs = (e0, e1.at[0], far.at[768:1152, :], far.at[1152:1536, :])
    keep, send, one_keep, one_send, rows, one_rows = refs[13:]
    for k in range(5):
        if k < 3:
            left = jnp.concatenate([n[0:768, :] for n in norms], 1)
            right = jnp.concatenate([h[k * 192 : (k + 1) * 192, :] for h in heads], 1)
        else:
            at = (k - 3) * 768
            left = jnp.concatenate([g[at : at + 768, :] for g in grads], 1)
            at = (k - 3) * 192
            right = jnp.concatenate([o[at : at + 192, :] for o in outs], 1)
        full = dot_nt(left, jnp.concatenate([right, right[128:192]], 0))

        def put(b, piece, k=k):
            if k < 4:
                rows[place_of(me, b, (1, 0, 2)), k * 144 : (k + 1) * 144, :] = piece
            else:
                one_rows[place_of(me, b, (0, 1, 2)), :, :] = piece

        pack(full[:, :128], full[:, 128:], full[:, 128:], put)
    keep[...] = rows[0:4]
    send[...] = rows[4:8]
    one_keep[...] = one_rows[0:4]
    one_send[...] = one_rows[4:8]


def total(a, b):
    return a.astype(F32) + b.astype(F32)


def mix_first(dw, dw_got, one_send, up, up_got, down, down_got, *outs):
    sent, far_keep, up_keep, up_send, down_keep, down_send = outs
    far_keep[...] = total(dw[0:4], dw_got[0:4]).astype(BF)
    sent[0:1728, :] = total(dw[4:8], dw_got[4:8]).astype(BF).reshape(1728, 128)
    sent[1728:2304, :] = one_send[...].reshape(576, 128)
    for k, (up_out, down_out) in enumerate(((up_keep, down_keep), (up_send, down_send))):
        up_out[...] = total(up[k], up_got[k]).astype(BF)
        down_out[...] = total(down[k], down_got[k]).astype(BF)


def mix_second(dw, dw_got, far, got, one, own, own_got, *outs):
    keep, send, far_send, one_keep, one_send, own_keep, own_send = outs
    keep[...] = total(dw[0:4], dw_got[0:4]).astype(BF)
    send[...] = total(dw[4:8], dw_got[4:8]).astype(BF)
    far_send[...] = total(far[...], got[0:1728, :].reshape(4, 432, 128)).astype(BF)
    one_got = got[1728:2304, :].reshape(4, 144, 128)
    one_keep[...] = total(one[0:2], one_got[0:2]).astype(BF)
    one_send[...] = total(one[2:4], one_got[2:4]).astype(BF)
    own_keep[...] = total(own[0:2], own_got[0:2]).astype(BF)
    own_send[...] = total(own[2:4], own_got[2:4]).astype(BF)


def mix_third(dw, got, far_got, one_send, keep, send):
    keep[...] = (total(dw[0:2], got[0:2]) + far_got[0:2].astype(F32)).astype(BF)
    part = total(dw[2:4], got[2:4]) + far_got[2:4].astype(F32)
    send[0:864, :] = part.astype(BF).reshape(864, 128)
    send[864:1152, :] = one_send[...].reshape(288, 128)


def mix_fourth(dw, got, one, own, own_got, keep, send):
    for k, out in enumerate((keep, send)):
        out[0:432, :] = total(dw[k], got[k * 432 : (k + 1) * 432, :]).astype(BF)
        at = 864 + k * 144
        out[432:576, :] = total(one[k], got[at : at + 144, :]).astype(BF)
        out[576:1152, :] = total(own[k], own_got[k]).astype(BF)


def unpack(v, out):
    out[:, 0:128] = v[0:96]
    out[0:48, 128:192] = v[96:144, 0:64]
    out[48:96, 128:192] = v[96:144, 64:128]


def last_mlp(up, up_got, down, down_got, *outs):
    for out, sums in zip(outs, (total(up[...], up_got[...]), total(down[...], down_got[...]))):
        for c in range(6):
            out[:, c * 128 : (c + 1) * 128] = sums[c * 96 : (c + 1) * 96]


def last_heads(kept, got, *outs):
    sums = total(kept[...], got[...])
    for k, out in enumerate(outs):
        unpack(sums[k * 144 : (k + 1) * 144], out)


def cross_backward(dp_ref, *refs, half):
    me = dp_ref[0]
    pays = refs[:4]
    x_ref, tnt, ltt, tbs, hot, w0, w1 = refs[4:11]
    rest = refs[11:]
    if half == 0:
        early, dg_in, rest = rest[0], rest[1], rest[2:]
        dk, dv, mine, other, dw0, dw1, dg = rest[:7]
    else:
        dk, dv, dq_out, dw0, dw1, dg = rest[:6]
    kn, vn, kt, qt, dq, do, own, lse, delta = rest[-9:]
    ws = [
        jnp.concatenate([v[k * 192 : (k + 1) * 192, :] for v in (w0, w1)], 0) for k in range(3)
    ]
    qt[...] = (dot(ws[0], ltt[...]).astype(BF).astype(F32) * SCALE).astype(BF)
    kn[...] = dot_nt(x_ref[...], ws[1]).astype(BF)
    vn[...] = dot_nt(x_ref[...], ws[2]).astype(BF)
    kt[...] = kn[...].astype(F32).T.astype(BF)
    for r in range(4):
        st = pays[r][768:848, :].astype(F32)
        sums = (st[0:16] + st[16:32] + st[32:48], st[48:64] + st[64:80])
        for gi in range(2):
            src = (2 * half + gi) ^ r
            do[gi * 192 : (gi + 1) * 192, r * LAT : (r + 1) * LAT] = pays[r][
                src * 192 : (src + 1) * 192, :
            ]
            for j in range(GROUP):
                for table, v in zip((lse, delta), sums):
                    at = src * GROUP + j
                    table[gi * GROUP + j, r : r + 1, :] = v[at : at + 1, :]
    fill_masks(tbs[...], own)
    block_rows = hot[...]

    def two_heads(i, _):
        lanes = pl.ds(pl.multiple_of(i * 128, 128), 128)
        tb = tbs[...]
        qp, dop = qt[lanes, :], do[lanes, :]
        s = dot(widen(kn[:, lanes], own[...]), pile(qp))
        dp = dot(widen(vn[:, lanes], own[...]), pile(dop))
        probs, grads = [], []
        for j in range(2):
            h = 2 * i + j
            rows = [lse[h, b : b + 1, :] for b in range(NSEG)]
            p = jnp.exp(s[:, j * LAT : (j + 1) * LAT] - pick(tb, rows))
            rows = [delta[h, b : b + 1, :] for b in range(NSEG)]
            ds = (p * (dp[:, j * LAT : (j + 1) * LAT] - pick(tb, rows))).astype(BF)
            probs.append(widen(p.astype(BF), own[...]))
            grads.append(widen(ds, own[...]))
            at = pl.ds(pl.multiple_of(i * 128 + j * HEAD, HEAD), HEAD)
            kth = kt[at, :]
            k4 = jnp.concatenate([kth * block_rows[b : b + 1, :] for b in range(NSEG)], 0)
            dqh = (dot(k4, ds) * SCALE).astype(BF)
            dq[at, :] = jnp.concatenate(
                [dqh[b * HEAD : (b + 1) * HEAD, :] for b in range(NSEG)], 1
            )
        top = lax.broadcasted_iota(jnp.int32, qp.shape, 0) < HEAD
        zero = jnp.zeros_like(qp)
        for out, parts, t in ((dk, grads, qp), (dv, probs, dop)):
            right = jnp.concatenate([jnp.where(top, t, zero), jnp.where(top, zero, t)], 1)
            out[:, lanes] = dot_nt(jnp.concatenate(parts, 1), right).astype(BF)
        return 0

    lax.fori_loop(0, 3, two_heads, 0, unroll=True)

    for k in range(3):
        full = dot_nt(ltt[...], dq[...]) if k == 2 else dot(tnt[...], (dk, dv)[k][...])

        def put0(b, piece, k=k):
            dw0[place_of(me, b, (0, 1, 2)), k * 144 : (k + 1) * 144, :] = piece

        def put1(b, piece, k=k):
            dw1[place_of(me, b, (0, 1, 2)), k * 144 : (k + 1) * 144, :] = piece

        pack_halves(full, put0, put1)
        prod = full * ws[(k + 1) % 3].astype(F32).T
        part = prod[:, 0:128] + prod[:, 128:256] + prod[:, 256:384]
        if k == 0:
            gain_tok = part
            continue
        if k == 1:
            part += gain_tok
        part = jnp.sum(part.T, axis=0, keepdims=True)
        dg[k - 1 : k, :] = part if half == 1 else dg_in[k - 1 : k, :] + part
    if half == 0:
        for b in range(NSEG):
            out = (mine, other)[b & 1]
            out[b >> 1, 0:384, :] = dq[:, b * LAT : (b + 1) * LAT]
            out[b >> 1, 384:768, :] = early[:, b * LAT : (b + 1) * LAT]
    else:
        dq_out[...] = dq[...]


def pair_queries(mine, got, mlp, mlp_got, two, near, send, out):
    for k in range(2):
        for g in range(4):
            at, there = g * 192, (g ^ 1) * 192
            v = total(mine[k, at : at + 192, :], got[k, there : there + 192, :])
            if k:
                send[at : at + 192, :] = v.astype(BF)
            else:
                near[at : at + 192, :] = v
    out[...] = two[...] + total(mlp[0], mlp_got[0])
    v = total(mlp[1], mlp_got[1]).astype(BF)
    for c in range(6):
        send[768 + c * 128 : 896 + c * 128, :] = v[:, c * 128 : (c + 1) * 128]


def opening(side_ref, lat, gain, wq, wk, wv, out, ws, first):
    y = (standardize(lat[...].astype(F32))[0] * as_row(gain)).astype(BF)
    out[...] = y
    for k, w in enumerate((wq, wk, wv)):
        ws[k * 192 : (k + 1) * 192, :] = w[...]
    first[0:128, :] = y
    first[128:416, :] = ws[pl.ds(pl.multiple_of(side_ref[0] * 288, 16), 288), :]


def stack_weights(side_ref, *refs):
    stack, half, last = refs[5:]
    for k in range(5):
        stack[k * 192 : (k + 1) * 192, :] = refs[k][...]
    half[...] = stack[pl.ds(pl.multiple_of(side_ref[0] * 320, 16), 320), :]
    last[...] = stack[640:960, :]


def prepare(rank_ref, ids, owner, tok, gain, out, out_t, tbs, hot):
    rank = rank_ref[0]
    rows = tok.shape[0]
    mine = ids[:, 0:rows]
    for r in range(1, ids.shape[1] // rows):
        mine = jnp.where(rank == r, ids[:, r * rows : (r + 1) * rows], mine)
    block = jnp.zeros((1, rows), jnp.int32)
    for seg in range(NSEG):
        block = jnp.where(mine == seg, lax.bitwise_xor(owner[0, seg], rank), block)
    block = block.astype(F32)
    eight = lax.broadcasted_iota(jnp.int32, (8, rows), 0).astype(F32)
    hot[...] = jnp.where(jnp.broadcast_to(block, (8, rows)) == eight, 1.0, 0.0).astype(BF)
    tbs[...] = jnp.broadcast_to(block, (128, rows)).T
    xhat, _ = standardize(tok[...].astype(F32))
    y = (xhat * as_row(gain)).astype(BF)
    out[...] = y
    out_t[...] = y.astype(F32).T.astype(BF)


def token_end(dk0, dv0, dk1, dv1, w0, w1, w2, w3, tok, gain, out):
    xhat, inv = standardize(tok[...].astype(F32))
    dy = None
    for k, (a, b) in enumerate(((dk0, dk1), (dv0, dv1))):
        at = (k + 1) * 192
        for grad, pieces in ((a, (w0, w1)), (b, (w2, w3))):
            w = jnp.concatenate([p[at : at + 192, :] for p in pieces], 0)
            part = dot(grad[...], w)
            dy = part if dy is None else dy + part
    out[...] = norm_back(dy, xhat, inv, as_row(gain))


def latent_end(*refs):
    near, far, part, w0, w1, w2, w3, lat, g1, gain, out, new, dqt = refs
    for c in range(6):
        at = slice(c * 128, (c + 1) * 128)
        v = part[:, at] + far[768 + c * 128 : 896 + c * 128, :].astype(F32)
        new[:, at] = v.astype(BF)
    for g in range(4):
        at, there = g * 192, (g ^ 2) * 192
        v = near[at : at + 192, :] + far[there : there + 192, :].astype(F32)
        dqt[at : at + 192, :] = v.astype(BF)
    wq = jnp.concatenate([w[0:192, :] for w in (w0, w1, w2, w3)], 0)
    dlat = dot(dqt[...].astype(F32).T.astype(BF), wq)
    xhat, inv = standardize(lat[...].astype(F32))
    out[...] = g1[...] + norm_back(dlat, xhat, inv, as_row(gain))


def per_device(
    tokens,
    latents,
    segment_ids,
    segment_block,
    block_mask,
    gain_tok,
    gain_cross,
    gain_self,
    gain_mlp,
    wq_cross,
    wk_cross,
    wv_cross,
    wo_cross,
    wq_self,
    wk_self,
    wv_self,
    wo_self,
    w_up,
    w_down,
    d_latents,
):
    mp, dp = lax.axis_size("mp"), lax.axis_size("dp")
    fine = dp // 8
    low = fine.bit_length() - 1
    rank, place = lax.axis_index("mp"), lax.axis_index("dp")
    row = place // fine
    side = (place >> low) & 1
    _, n_tok, width = tokens.shape
    hid = w_up.shape[1]
    part = width // 8
    tok, lat, cot = tokens[0], latents[0], d_latents[0]
    full, sq = (LAT, width), (width, LAT)

    def after(v, *first):
        return lax.optimization_barrier((v,) + first)[0]

    def together(*v):
        return lax.optimization_barrier(v)

    def swap(v, r):
        return lax.ppermute(v, "mp", [(i, i ^ r) for i in range(mp)])

    def cross(v, k):
        flip = (1 << low) * (1, 2, 4, 6)[k]
        return lax.ppermute(v, "dp", [(i, i ^ flip) for i in range(dp)])

    def share(outs):
        return [outs[0]] + [swap(outs[r], r) for r in (1, 2, 3)]

    def add(a, b):
        return a.astype(F32) + b.astype(F32)

    latn, own, first = kernel_call(
        opening,
        [(full, BF), ((576, width), BF), ((416, width), BF)],
        0,
        lat,
        gain_cross,
        wq_cross.T,
        wk_cross.T,
        wv_cross.T,
        scalars=(side,),
        vmem=56,
    )
    l_near, near = swap(latn, 1), swap(own, 1)
    first2 = swap(first, 2)
    stack, half, last = kernel_call(
        stack_weights,
        [((960, width), BF)] + [((320, width), BF)] * 2,
        0,
        wo_cross.T,
        after(wq_self.T, latn),
        wk_self.T,
        wv_self.T,
        wo_self.T,
        scalars=(side,),
        vmem=56,
    )
    tokn, toknt, tbs, hot = kernel_call(
        prepare,
        [((n_tok, width), BF), ((width, n_tok), BF), ((n_tok, 128), F32), ((8, n_tok), BF)],
        2 * 10**9,
        segment_ids,
        segment_block,
        after(tok, stack),
        gain_tok,
        scalars=(rank,),
        tables=(1,),
        vmem=16,
    )
    first2 = after(first2, tokn, l_near, near)
    lats = [latn, l_near, first2, swap(first2, 1)]

    def cross_call(weights, early, gate):
        second = bool(early)
        outs = kernel_call(
            functools.partial(cross_forward, second=second),
            [((2, SHARE * (1 + second), LAT), BF)] * 2
            + [((576, width), BF)] * (2 * second),
            9 * 10**9,
            after(tokn, *gate),
            *lats,
            tbs,
            hot,
            *weights,
            *early,
            scalars=(side,),
            scratch=[((n_tok, 384), BF), ((384, n_tok), BF), ((384, NSEG * LAT), BF)]
            + [((n_tok, 512), BF), ((NSEG, 8, LAT), F32)],
            vmem=VMEM_CROSS,
        )
        return outs[:2], outs[2:]

    half2, last2 = swap(after(half, first), 2), swap(after(last, first), 2)
    far_x = cross(first2[128:416], 0)
    pays, _ = cross_call([own, near], [], [])
    far_x, half2, *pays = together(far_x, half2, *pays)
    half_x, half3 = cross(after(half2, far_x), 0), swap(half2, 1)
    (mine, other), (far, far_near) = cross_call(
        [far_x, swap(far_x, 1)], pays, [half3]
    )
    stack_near = swap(after(stack, far_x), 1)
    other, half_x, last2, stack_near = together(other, half_x, last2, stack_near)
    got = swap(other, 1)
    mine, pay_send = kernel_call(
        merge_pair, [((2 * SHARE, LAT), BF)] * 2, 10**9, mine, got
    )
    pay_far = swap(pay_send, 2)
    pieces = [stack, stack_near, half2, half_x, last2]
    pieces += [half3, swap(after(half_x, mine), 1), swap(after(last2, mine), 1)]
    weights = [((768, width), BF)] * 5
    pays = [mine, pay_far]

    attn, lse, one, two, e_send, mlp_in, at, probs, kts, qts, vs, e_other, e_own = kernel_call(
        latent_forward,
        [
            (sq, BF),
            ((16, LAT), F32),
            (full, F32),
            (full, F32),
            ((1152, LAT), BF),
            (full, BF),
            (sq, BF),
            ((12 * LAT, LAT), F32),
            (sq, BF),
            (sq, BF),
            (full, BF),
            ((2, 384, LAT), BF),
            ((384, LAT), BF),
        ],
        8 * 10**9,
        block_mask,
        *pays,
        lat,
        gain_self,
        gain_mlp,
        *pieces,
        scalars=(rank, side),
        scratch=weights + [pltpu.SemaphoreType.DMA((32,))],
        loose=range(6, 14),
        tables=(0,),
        vmem=16,
    )
    x_far, x_near = swap(mlp_in, 2), swap(mlp_in, 1)
    e_got = swap(e_other, 1)
    c_far = after(swap(after(cot, pay_send), 2), mlp_in)
    cots = [cot, swap(after(cot, pay_send), 1), c_far, swap(c_far, 1)]
    dh, cot_t, lat_t = kernel_call(
        mlp_before,
        [((4 * LAT, hid), F32), ((width, 4 * LAT), BF), ((width, 4 * LAT), BF)],
        4 * 10**9,
        *cots[:3],
        after(cots[3], mlp_in),
        *lats,
        w_down,
    )
    x_far, e_got = together(x_far, e_got)
    xs = [mlp_in, x_near, x_far, swap(after(x_far, dh), 1)]
    mine, other, hidden, dpre = kernel_call(
        mlp_main,
        [((2, LAT, width), BF)] * 2 + [((4 * LAT, hid), BF)] * 2,
        3 * 10**9,
        *xs,
        dh,
        w_up,
    )
    got = swap(other, 1)
    back_near, back_send = add(mine[0], got[0]), add(mine[1], got[1]).astype(BF)
    back_far = swap(back_send, 2)
    rows_of = part * hid // 128
    up, up_send, down, down_send = kernel_call(
        mlp_weights,
        [((4, rows_of, 128), BF)] * 4,
        3 * 10**9,
        *xs,
        cot_t,
        hidden,
        after(dpre, back_send),
        scalars=(row,),
        scratch=[((8, rows_of, 128), BF)],
    )
    up_got, down_got = cross(up_send, 1), cross(down_send, 0)
    n_far = swap(jnp.concatenate([after(e_send, up_send), e_got[1]], 0), 2)
    e_near = swap(after(e_send, up_send), 1)

    pay, g1, grads, m_own, m_other, m_send, dg_mlp, dg_self = kernel_call(
        latent_backward,
        [((848, LAT), BF), (full, F32), ((1536, LAT), BF)]
        + [((576, LAT), BF), ((2, 576, LAT), BF), ((576, LAT), BF)]
        + [((1, width), F32)] * 2,
        9 * 10**9,
        block_mask,
        back_near,
        after(back_far, up_send),
        two,
        one,
        cot,
        attn,
        lse,
        probs,
        kts,
        qts,
        vs,
        gain_self,
        gain_mlp,
        *pieces,
        scalars=(rank, side),
        scratch=[(sq, BF)] * 3 + weights,
        tables=(0,),
        vmem=VMEM_LATENT,
    )
    pay, n_far = together(pay, n_far)
    p_far, p_near = swap(pay, 2), swap(pay, 1)
    pays = [pay, p_near, p_far, swap(p_far, 1)]

    def part_sum(kept, got):
        n = kept.shape[0] // 2
        return add(kept[:n], got[:n]).astype(BF), add(kept[n:], got[n:]).astype(BF)

    up, up_send = part_sum(up, up_got)
    down, down_send = part_sum(down, down_got)
    forwards = kernel_call(
        mlp_out, [((2, LAT, width), BF)] * 2, 10**9, after(hidden, pay), w_down
    )
    f_got = swap(forwards[1], 1)
    grads = after(grads, pay)
    g_far, g_near = swap(grads, 2), swap(grads, 1)
    m_near, n_last = swap(after(m_other, p_far), 1), swap(after(n_far, p_far), 1)

    def cross_back(half, ws, more, gate):
        return kernel_call(
            functools.partial(cross_backward, half=half),
            [((n_tok, 384), BF)] * 2
            + ([((2, 768, LAT), BF)] * 2 if half == 0 else [((384, NSEG * LAT), BF)])
            + [((8, 432, 128), BF)] * 2
            + [((2, width), F32)],
            11 * 10**9,
            after(pays[0], *gate),
            *pays[1:],
            tokn,
            toknt,
            lat_t,
            tbs,
            hot,
            *ws,
            *more,
            scalars=(row,),
            scratch=[((n_tok, 384), BF)] * 2
            + [((384, n_tok), BF)]
            + [((384, NSEG * LAT), BF)] * 3
            + [((n_tok, 512), BF)]
            + [((8, NSEG, LAT), F32)] * 2,
            vmem=VMEM_CROSS,
        )

    m_send = jnp.concatenate([m_send, m_near[1]], 0)
    dk1, dv1, dq1, dw, other, dg_cross = cross_back(
        1, (far, far_near), (), (up_send, down_send, f_got, g_near, m_send, n_last)
    )
    up_got, down_got = cross(up_send, 0), cross(down_send, 2)
    m_far = swap(m_send, 2)
    other, up_got, down_got, g_far, m_far = together(other, up_got, down_got, g_far, m_far)
    dw_got, g_last = swap(other, 1), swap(g_far, 1)
    mine, mine_send, one_keep, one_send = kernel_call(
        latent_weights,
        [((4, 576, 128), BF)] * 2 + [((4, 144, 128), BF)] * 2,
        2 * 10**9,
        e_send,
        e_near,
        n_far,
        n_last,
        grads,
        g_near,
        g_far,
        g_last,
        m_own,
        m_near,
        m_far,
        e_own,
        e_got,
        scalars=(row,),
        scratch=[((8, 576, 128), BF), ((8, 144, 128), BF)],
    )
    sent, far_dw, up, up_send, down, down_send = kernel_call(
        mix_first,
        [((2304, 128), BF), ((4, 432, 128), BF)] + [((rows_of, 128), BF)] * 4,
        10**9,
        dw,
        dw_got,
        one_send,
        up,
        up_got,
        down,
        down_got,
    )
    dk0, dv0, dq_mine, dq_other, dw, other, dg_cross = cross_back(
        0, (own, near), (dq1, dg_cross), (sent, mine_send)
    )
    got, mine_got = cross(sent, 0), cross(mine_send, 1)
    dg_tok, dg_cross = (
        dg_cross[k : k + 1] / g.astype(F32)[None, :] for k, g in enumerate((gain_tok, gain_cross))
    )
    gains = jnp.concatenate([dg_tok, dg_cross, dg_self, dg_mlp], 0)
    other, got, mine_got, gains = together(other, got, mine_got, gains)
    gains_got = swap(gains, 1)
    dw_got, dq_got = swap(other, 1), swap(after(dq_other, other), 1)
    dw, sent, far_send, one_keep, one_send, mine, mine_send = kernel_call(
        mix_second,
        [((4, 432, 128), BF)] * 3 + [((2, 144, 128), BF)] * 2 + [((2, 576, 128), BF)] * 2,
        10**9,
        dw,
        dw_got,
        far_dw,
        got,
        one_keep,
        mine,
        mine_got,
    )
    got, far_got = cross(sent, 0), swap(far_send, 2)
    up_got, down_got = cross(after(up_send, sent), 2), cross(after(down_send, sent), 1)
    gains = after(gains + gains_got, sent)
    gains_got = cross(gains, 1)
    (out_tok,) = kernel_call(
        token_end,
        [((n_tok, width), F32)],
        5 * 10**9,
        dk0,
        dv0,
        dk1,
        after(dv1, sent, far_send),
        own,
        near,
        far,
        far_near,
        tok,
        gain_tok,
        vmem=24,
    )
    got, far_got, up_got, down_got, gains_got, out_tok, mine_send = together(
        got, far_got, up_got, down_got, gains_got, out_tok, mine_send
    )
    dw, sent = kernel_call(
        mix_third, [((2, 432, 128), BF), ((1152, 128), BF)], 10**9, dw, got, far_got, one_send
    )
    got, mine_got = cross(sent, 1), cross(mine_send, 0)
    gains = after(gains + gains_got, sent)
    gains_got = cross(gains, 0)
    dq_near, dq_send, new_near = kernel_call(
        pair_queries,
        [(sq, F32), ((2 * width, LAT), BF), (full, F32)],
        10**9,
        after(dq_mine, sent),
        dq_got,
        forwards[0],
        f_got,
        two,
    )
    dq_far = swap(dq_send, 2)
    mlps = kernel_call(
        last_mlp, [((96, hid), F32)] * 2, 10**9, up, after(up_got, dq_send), down, down_got
    )
    got, mine_got, gains_got, dq_far, *mlps = together(got, mine_got, gains_got, dq_far, *mlps)
    kept, sent = kernel_call(
        mix_fourth, [((1152, 128), BF)] * 2, 10**9, dw, got, one_keep, mine, mine_got
    )
    got = cross(sent, 2)
    grad_lat, new_latents, _ = kernel_call(
        latent_end,
        [(full, F32), (full, BF), (sq, BF)],
        3 * 10**9,
        dq_near,
        after(dq_far, sent),
        new_near,
        own,
        near,
        far,
        far_near,
        lat,
        g1,
        gain_cross,
    )
    gains = after(gains + gains_got, sent)
    gains = gains + swap(gains, 2)
    gains = gains + cross(gains, 2)
    for k in range(low):
        gains = gains + lax.ppermute(gains, "dp", [(i, i ^ (1 << k)) for i in range(dp)])
    lasts = kernel_call(last_heads, [((96, 192), F32)] * 8, 10**9, kept, got)

    groups = [list(range(k * fine, (k + 1) * fine)) for k in range(8)]

    def shard(v):
        if fine == 1:
            return v
        return lax.psum_scatter(v, "dp", scatter_dimension=0, axis_index_groups=groups, tiled=True)

    order = (lasts[2], lasts[0], lasts[1], *lasts[3:], *mlps)
    return (
        new_latents[None],
        out_tok[None],
        grad_lat[None],
        *(gains[k] for k in range(4)),
        *(shard(v) for v in order),
    )


def solution(mesh):
    rows, cols, lone = P("dp", "mp", None), P(None, "mp"), P("dp", None)
    in_specs = (rows, rows, lone, lone, lone) + (P(),) * 4 + (cols,) * 10 + (rows,)
    out_specs = (rows,) * 3 + (P(),) * 4 + (P("dp", "mp"),) * 10
    return jax.shard_map(
        per_device, mesh=mesh, in_specs=in_specs, out_specs=out_specs, check_vma=False
    )
```

```python
import functools
import math

import jax
import jax.numpy as jnp
from jax import lax
from jax.experimental import pallas as pl
from jax.experimental.pallas import tpu as pltpu
from jax.sharding import PartitionSpec as P

HEAD = 64
LAT = 128
NSEG = 4
GROUP = 3
EPS = 1e-05
FAR = -1e30
F32 = jnp.float32
BF = jnp.bfloat16
SCALE = 1.0 / math.sqrt(HEAD)
MIB = 1024 * 1024
VMEM_CROSS = 20
VMEM_LATENT = 20


def dot(a, b):
    return lax.dot_general(a, b, (((1,), (0,)), ((), ())), preferred_element_type=F32)


def dot_nt(a, b):
    return lax.dot_general(a, b, (((1,), (1,)), ((), ())), preferred_element_type=F32)


def standardize(v):
    center = v - jnp.mean(v, axis=-1, keepdims=True)
    inv = lax.rsqrt(jnp.mean(center * center, axis=-1, keepdims=True) + EPS)
    return center * inv, inv


def norm_back(dy, xhat, inv, gain):
    s = dy * gain
    return inv * (
        s - jnp.mean(s, axis=-1, keepdims=True) - xhat * jnp.mean(s * xhat, axis=-1, keepdims=True)
    )


def as_row(gain):
    return gain[...].astype(F32).reshape(1, -1)


def kernel_call(body, outs, flops, *args, scalars=(), scratch=(), tables=(), vmem=12, far=(), loose=()):
    n = len(scalars)
    specs = [pl.BlockSpec(memory_space=pltpu.SMEM)] * n
    specs += [
        pl.BlockSpec(
            memory_space=pltpu.SMEM if i in tables else pl.ANY if i in loose else pltpu.VMEM
        )
        for i in range(len(args))
    ]
    moved = sum(a.size * a.dtype.itemsize for a in args)
    moved += sum(math.prod(s) * jnp.dtype(d).itemsize for s, d in outs)
    return pl.pallas_call(
        body,
        out_shape=[jax.ShapeDtypeStruct(s, d) for s, d in outs],
        in_specs=specs,
        out_specs=[
            pl.BlockSpec(memory_space=pltpu.HBM if i in far else pltpu.VMEM)
            for i in range(len(outs))
        ],
        scratch_shapes=[
            pltpu.VMEM(*x) if isinstance(x, tuple) else x for x in scratch
        ],
        compiler_params=pltpu.CompilerParams(vmem_limit_bytes=vmem * MIB),
        cost_estimate=pl.CostEstimate(flops=flops, bytes_accessed=moved, transcendentals=0),
    )(*[jnp.reshape(s, (1,)).astype(jnp.int32) for s in scalars], *args)


def split3(v):
    a = v.astype(BF).astype(F32)
    b = (v - a).astype(BF).astype(F32)
    return a, b, v - a - b


def stack_rows(rows, pad):
    return jnp.concatenate(rows + [jnp.zeros((pad - len(rows), rows[0].shape[1]), F32)], 0)


def pick(tb, rows):
    out = rows[NSEG - 1]
    for b in range(NSEG - 2, -1, -1):
        out = jnp.where(tb == b, rows[b], out)
    return out


def widen(v, own):
    return jnp.concatenate([v] * NSEG, 1) * own


def pile(t):
    top = lax.broadcasted_iota(jnp.int32, (2 * HEAD, LAT), 0) < HEAD
    zero = jnp.zeros((2 * HEAD, LAT), t.dtype)
    rows = []
    for b in range(NSEG):
        part = t[:, b * LAT : (b + 1) * LAT]
        rows.append(
            jnp.concatenate([jnp.where(top, part, zero), jnp.where(top, zero, part)], 1)
        )
    return jnp.concatenate(rows, 0)


def fill_masks(tb, own):
    for b in range(NSEG):
        own[:, b * 128 : (b + 1) * 128] = jnp.where(tb == b, 1.0, 0.0).astype(BF)


SHARE = 416


def cross_forward(side_ref, *refs, second):
    x_ref, l0, l1, first2, first3, tbs, hot = refs[:7]
    rest = refs[7:]
    if second:
        halves, early, rest = rest[:2], rest[2:4], rest[4:]
    else:
        pieces, rest = rest[:2], rest[2:]
    mine, other = rest[:2]
    if second:
        pieces, rest = rest[2:4], rest[4:]
        for piece, by_mp, by_dp in zip(pieces, (first2, first3), halves):
            low = side_ref[0] == 0
            piece[0:288, :] = jnp.where(low, by_mp[128:416, :], by_dp[...])
            piece[288:576, :] = jnp.where(low, by_dp[...], by_mp[128:416, :])
    else:
        rest = rest[2:]
    kn, vt, qt, own, stat = rest
    w = [
        jnp.concatenate([p[k * 192 : (k + 1) * 192, :] for p in pieces], 0) for k in range(3)
    ]
    lat = jnp.concatenate([l0[...], l1[...], first2[0:128, :], first3[0:128, :]], 0)
    qt[...] = (dot_nt(w[0], lat).astype(BF).astype(F32) * SCALE).astype(BF)
    kn[...] = dot_nt(x_ref[...], w[1]).astype(BF)
    vt[...] = dot_nt(x_ref[...], w[2]).T.astype(BF)
    fill_masks(tbs[...], own)
    base = SHARE if second else 0
    stat[...] = jnp.zeros_like(stat)
    block_rows = hot[...]

    def two_heads(i, _):
        lanes = pl.ds(pl.multiple_of(i * 128, 128), 128)
        tb = tbs[...]
        s = dot(widen(kn[:, lanes], own[...]), pile(qt[lanes, :]))
        for j in range(2):
            sj = s[:, j * LAT : (j + 1) * LAT]
            top = [
                jnp.max(jnp.where(tb == b, sj, FAR), axis=0, keepdims=True) for b in range(NSEG)
            ]
            p = jnp.exp(sj - pick(tb, top)).astype(BF)
            total_of = dot(block_rows, p)
            rows = pl.ds(pl.multiple_of(i * 128 + j * HEAD, HEAD), HEAD)
            vth = vt[rows, :]
            v4 = jnp.concatenate([vth * block_rows[b : b + 1, :] for b in range(NSEG)], 0)
            o = dot(v4, p)
            to = pl.ds(pl.multiple_of(base + i * 128 + j * HEAD, 32), HEAD)
            for b in range(NSEG):
                tot = total_of[b : b + 1, :]
                some = tot > 0.0
                safe = jnp.where(some, tot, 1.0)
                stat[b, pl.ds(2 * i + j, 1), :] = jnp.where(some, top[b] + jnp.log(safe), FAR)
                out = (mine, other)[b & 1]
                out[b >> 1, to, :] = (o[b * HEAD : (b + 1) * HEAD, :] / safe).astype(BF)
        return 0

    lax.fori_loop(0, 3, two_heads, 0, unroll=True)
    for b in range(NSEG):
        out = (mine, other)[b & 1]
        out[b >> 1, base + 384 : base + SHARE, :] = jnp.concatenate(
            list(split3(stat[b])) + [jnp.zeros((8, LAT), F32)], 0
        ).astype(BF)
    if second:
        for out, first in ((mine, early[0]), (other, early[1])):
            out[:, 0:SHARE, :] = first[...]


def merge(parts, head, lse_of):
    tables = []
    for read, _ in parts:
        one = []
        for half in range(2):
            st = read(half * SHARE + 384, 32).astype(F32)
            one.append(st[0:8] + st[8:16] + st[16:24])
        tables.append(one)
    for g in range(4):
        for j in range(GROUP):
            found = []
            for (read, flip), table in zip(parts, tables):
                src = g ^ flip
                half, at = src >> 1, (src & 1) * GROUP + j
                found.append(
                    (table[half][at : at + 1, :], read(half * SHARE + at * HEAD, HEAD).astype(F32))
                )
            top = functools.reduce(jnp.maximum, [f[0] for f in found])
            w = [jnp.exp(f[0] - top) for f in found]
            all_w = functools.reduce(jnp.add, w)
            o = functools.reduce(jnp.add, [a * f[1] for a, f in zip(w, found)]) / all_w
            head(g, j, o.astype(BF))
            lse_of(g, j, top + jnp.log(all_w))


def merge_pair(mine, got, keep, send):
    for k, out in enumerate((keep, send)):
        rows = [[], []]

        def head(g, j, o, out=out):
            at = (g >> 1) * SHARE + ((g & 1) * GROUP + j) * HEAD
            out[at : at + HEAD, :] = o

        def lse_of(g, j, v, rows=rows):
            rows[g >> 1].append(v)

        merge(
            [
                (lambda a, n, k=k: mine[k, a : a + n, :], 0),
                (lambda a, n, k=k: got[k, a : a + n, :], 1),
            ],
            head,
            lse_of,
        )
        for half in range(2):
            parts = list(split3(stack_rows(rows[half], 8))) + [jnp.zeros((8, LAT), F32)]
            out[half * SHARE + 384 : (half + 1) * SHARE, :] = jnp.concatenate(parts, 0).astype(BF)


def join_weights(side_ref, *refs):
    side, pieces, full = side_ref[0], refs[:8], refs[8:]
    own, near = pieces[:2]
    for r, stack in ((0, own), (1, near)):
        for k in range(5):
            full[k][r * 192 : (r + 1) * 192, :] = stack[k * 192 : (k + 1) * 192, :]
    for r, (by_mp, by_dp, last) in ((2, pieces[2:5]), (3, pieces[5:8])):
        low = side == 0
        stack = jnp.concatenate(
            [
                jnp.where(low, by_mp[...], by_dp[...]),
                jnp.where(low, by_dp[...], by_mp[...]),
                last[...],
            ],
            0,
        )
        for k in range(5):
            full[k][r * 192 : (r + 1) * 192, :] = stack[k * 192 : (k + 1) * 192, :]


def latent_forward(rank_ref, mask_ref, *refs):
    pay = refs[:2]
    lat, g_self, g_mlp = refs[2], refs[3], refs[4]
    full = refs[5:10]
    (
        attn_ref,
        lse_ref,
        one_ref,
        two_ref,
        norm_ref,
        mlp_ref,
        at_ref,
        p_ref,
        kt_ref,
        qt_ref,
        v_ref,
        early_other,
        early_own,
    ) = refs[10:]
    wo_c, wq, wk, wv, wo = full
    keep = mask_ref[0, rank_ref[0]].astype(F32)
    lse_rows = []

    def head(g, j, o):
        at = (g * GROUP + j) * HEAD
        attn_ref[at : at + HEAD, :] = o

    merge(
        [(lambda a, n: pay[0][a : a + n, :], 0), (lambda a, n: pay[1][a : a + n, :], 2)],
        head,
        lambda g, j, v: lse_rows.append(v),
    )
    lse_ref[...] = stack_rows(lse_rows, 16)
    attn = attn_ref[...].astype(F32).T.astype(BF)
    one = lat[...].astype(F32) + keep * dot(attn, wo_c[...])
    one_ref[...] = one
    zhat, _ = standardize(one)
    x = (zhat * as_row(g_self)).astype(BF)
    norm_ref[0:768, :] = x.astype(F32).T.astype(BF)
    qt_ref[...] = (dot_nt(wq[...], x).astype(BF).astype(F32) * SCALE).astype(BF)
    kt_ref[...] = dot_nt(wk[...], x).astype(BF)
    vt = dot_nt(wv[...], x).astype(BF)
    k = dot_nt(x, wk[...]).astype(BF)
    v_ref[...] = dot_nt(x, wv[...]).astype(BF)
    zero = jnp.zeros((HEAD, LAT), BF)
    for h in range(4 * GROUP):
        hs = slice(h * HEAD, (h + 1) * HEAD)
        ps = slice((h // 2) * 128, (h // 2) * 128 + 128)
        qh = qt_ref[hs, :]
        s = dot(k[:, ps], jnp.concatenate([qh, zero] if h % 2 == 0 else [zero, qh], 0))
        e = jnp.exp(s - jnp.max(s, axis=0, keepdims=True))
        p = e / jnp.sum(e, axis=0, keepdims=True)
        p_ref[h * LAT : (h + 1) * LAT, :] = p
        at_ref[hs, :] = dot(vt[hs, :], p.astype(BF)).astype(BF)
    two = one + dot(at_ref[...].astype(F32).T.astype(BF), wo[...])
    for r, to in enumerate((early_own, early_other.at[0], norm_ref.at[768:1152, :], early_other.at[1])):
        to[0:192, :] = at_ref[r * 192 : (r + 1) * 192, :]
        to[192:384, :] = attn_ref[r * 192 : (r + 1) * 192, :]
    two_ref[...] = two
    zhat, _ = standardize(two)
    mlp_ref[...] = (zhat * as_row(g_mlp)).astype(BF)


def mlp_before(c0, c1, c2, c3, l0, l1, first2, first3, down, dh_ref, cot_t, lat_t):
    g = jnp.concatenate([c0[...], c1[...], c2[...], c3[...]], 0)
    dh_ref[...] = dot(g, down[...])
    cot_t[...] = g.astype(F32).T.astype(BF)
    lat = jnp.concatenate([l0[...], l1[...], first2[0:128, :], first3[0:128, :]], 0)
    lat_t[...] = lat.astype(F32).T.astype(BF)


def deal(v, mine, other):
    for r in range(4):
        out = (mine, other)[r & 1]
        out[r >> 1, :, :] = v[r * LAT : (r + 1) * LAT, :]


def mlp_main(x0, x1, x2, x3, dh_ref, up, *outs):
    mine, other, h_ref, d_ref = outs
    c = math.sqrt(2.0 / math.pi)
    x = jnp.concatenate([x0[...], x1[...], x2[...], x3[...]], 0)
    pre = dot(x, up[...])
    sq = pre * pre
    t = jnp.tanh(c * pre * (1.0 + 0.044715 * sq))
    h_ref[...] = (0.5 * pre * (1.0 + t)).astype(BF)
    slope = 0.5 * (1.0 + t) + 0.5 * pre * (1.0 - t * t) * c * (1.0 + 3 * 0.044715 * sq)
    d = (dh_ref[...] * slope).astype(BF)
    d_ref[...] = d
    deal(dot_nt(d, up[...]).astype(BF), mine, other)


def mlp_weights(dp_ref, x0, x1, x2, x3, gt, h_ref, d_ref, *outs):
    me = dp_ref[0]
    rows = outs[4]
    xt = jnp.concatenate([x0[...], x1[...], x2[...], x3[...]], 0).astype(F32).T.astype(BF)
    for k, (lhs, rhs) in enumerate(((xt, d_ref[...]), (gt[...], h_ref[...]))):
        full = dot(lhs, rhs).astype(BF)
        for b in range(8):
            at = place_of(me, b, ((1, 0, 2), (0, 1, 2))[k])
            for c in range(6):
                rows[at, c * 96 : (c + 1) * 96, :] = full[
                    b * 96 : (b + 1) * 96, c * 128 : (c + 1) * 128
                ]
        outs[2 * k][...] = rows[0:4]
        outs[2 * k + 1][...] = rows[4:8]


def mlp_out(h_ref, down, mine, other):
    deal(dot_nt(h_ref[...], down[...]).astype(BF), mine, other)


def latent_backward(rank_ref, mask_ref, *refs):
    b0, b1, two, one, cot, attn, lse, p_ref, kt, qt, v, g_self, g_mlp = refs[:13]
    full = refs[13:18]
    pay, g1_ref, grads, mine, other, dg_mlp, dg_self = refs[18:-3]
    dqt_ref, dkt_ref, dvt_ref = refs[-3:]
    wo_c, wq, wk, wv, wo = full
    keep = mask_ref[0, rank_ref[0]].astype(F32)
    dmlp = b0[...] + b1[...].astype(F32)
    zhat, inv = standardize(two[...])
    g2 = cot[...].astype(F32) + norm_back(dmlp, zhat, inv, as_row(g_mlp))
    dg_mlp[...] = jnp.sum(dmlp * zhat, axis=0, keepdims=True)
    low = g2.astype(BF)
    grads[0:768, :] = g2.T.astype(BF)
    dat = dot_nt(wo[...], low).astype(BF)
    zero = jnp.zeros((HEAD, LAT), BF)
    for h in range(4 * GROUP):
        hs = slice(h * HEAD, (h + 1) * HEAD)
        ps = slice((h // 2) * 128, (h // 2) * 128 + 128)
        dh = dat[hs, :]
        p = p_ref[h * LAT : (h + 1) * LAT, :]
        dp = dot(v[:, ps], jnp.concatenate([dh, zero] if h % 2 == 0 else [zero, dh], 0))
        ds = (p * (dp - jnp.sum(p * dp, axis=0, keepdims=True))).astype(BF)
        dvt_ref[hs, :] = dot_nt(dh, p.astype(BF)).astype(BF)
        dqt_ref[hs, :] = (dot(kt[hs, :], ds) * SCALE).astype(BF)
        dkt_ref[hs, :] = dot_nt(qt[hs, :], ds).astype(BF)
    back = dot(dqt_ref[...].astype(F32).T.astype(BF), wq[...])
    back += dot(dkt_ref[...].astype(F32).T.astype(BF), wk[...])
    back += dot(dvt_ref[...].astype(F32).T.astype(BF), wv[...])
    zhat, inv = standardize(one[...])
    g1 = g2 + norm_back(back, zhat, inv, as_row(g_self))
    dg_self[...] = jnp.sum(back * zhat, axis=0, keepdims=True)
    g1_ref[...] = g1
    gc = (keep * g1).astype(BF)
    grads[768:1536, :] = (keep * g1).T.astype(BF)
    for r, to in enumerate((mine, other.at[0], grads.at[1536:2112, :], other.at[1])):
        for k, part in enumerate((dqt_ref, dkt_ref, dvt_ref)):
            to[k * 192 : (k + 1) * 192, :] = part[r * 192 : (r + 1) * 192, :]
    do = dot_nt(wo_c[...], gc).astype(BF)
    pay[0:768, :] = do
    deltas = []
    for h in range(4 * GROUP):
        hs = slice(h * HEAD, (h + 1) * HEAD)
        deltas.append(
            jnp.sum(do[hs, :].astype(F32) * attn[hs, :].astype(F32), axis=0, keepdims=True)
        )
    parts = list(split3(lse[...])) + list(split3(stack_rows(deltas, 16))[:2])
    pay[768:848, :] = jnp.concatenate(parts, 0).astype(BF)


def bit(v, k):
    return lax.bitwise_and(lax.shift_right_logical(v, k), 1)


def place_of(me, b, bits):
    v = lax.bitwise_xor(me, b)
    return 4 * bit(v, bits[0]) + 2 * bit(v, bits[1]) + bit(v, bits[2])


def pack(whole, third, third_rolled, put):
    low = lax.broadcasted_iota(jnp.int32, (48, 128), 1) < HEAD
    for b in range(8):
        r = 96 * b
        tail = jnp.where(low, third[r : r + 48], third_rolled[r + 48 : r + 96])
        put(b, jnp.concatenate([whole[r : r + 96], tail], 0).astype(BF))


def pack_halves(full, put0, put1):
    low = lax.broadcasted_iota(jnp.int32, (full.shape[0], 128), 1) < HEAD
    a, b, c = full[:, 0:128], full[:, 128:256], full[:, 256:384]
    b_turned, c_turned = pltpu.roll(b, HEAD, 1), pltpu.roll(c, HEAD, 1)
    pack(a, b, b_turned, put0)
    pack(jnp.where(low, b_turned, c_turned), c_turned, c, put1)


def latent_weights(dp_ref, *refs):
    me = dp_ref[0]
    norms, grads, (h0, h1, e0, e1) = refs[:4], refs[4:8], refs[8:12]
    far = norms[2]
    heads = (h0, h1.at[0], grads[2].at[1536:2112, :], grads[2].at[2112:2688, :])
    outs = (e0, e1.at[0], far.at[768:1152, :], far.at[1152:1536, :])
    keep, send, one_keep, one_send, rows, one_rows = refs[12:]
    for k in range(5):
        if k < 3:
            left = jnp.concatenate([n[0:768, :] for n in norms], 1)
            right = jnp.concatenate([h[k * 192 : (k + 1) * 192, :] for h in heads], 1)
        else:
            at = (k - 3) * 768
            left = jnp.concatenate([g[at : at + 768, :] for g in grads], 1)
            at = (k - 3) * 192
            right = jnp.concatenate([o[at : at + 192, :] for o in outs], 1)
        full = dot_nt(left, jnp.concatenate([right, right[128:192]], 0))

        def put(b, piece, k=k):
            if k < 4:
                rows[place_of(me, b, (1, 0, 2)), k * 144 : (k + 1) * 144, :] = piece
            else:
                one_rows[place_of(me, b, (0, 1, 2)), :, :] = piece

        pack(full[:, :128], full[:, 128:], full[:, 128:], put)
    keep[...] = rows[0:4]
    send[...] = rows[4:8]
    one_keep[...] = one_rows[0:4]
    one_send[...] = one_rows[4:8]


def total(a, b):
    return a.astype(F32) + b.astype(F32)


def mix_first(dw, dw_got, up, up_got, down, down_got, *outs):
    sent, far_keep, mlp_keep, mlp_send = outs
    far_keep[...] = total(dw[0:4], dw_got[0:4]).astype(BF)
    sent[...] = total(dw[4:8], dw_got[4:8]).astype(BF)
    for k, out in enumerate((mlp_keep, mlp_send)):
        out[0:576, :] = total(up[k], up_got[k]).astype(BF)
        out[576:1152, :] = total(down[k], down_got[k]).astype(BF)


def mix_second(dw, dw_got, far, got, one_send, keep, send, far_send):
    keep[...] = total(dw[0:4], dw_got[0:4]).astype(BF)
    send[0:1728, :] = total(dw[4:8], dw_got[4:8]).astype(BF).reshape(1728, 128)
    send[1728:2304, :] = one_send[...].reshape(576, 128)
    far_send[...] = total(far[...], got[...]).astype(BF)


def mix_third(dw, got, far_got, one, own, own_got, *outs):
    keep, send, one_keep, own_keep, own_send = outs
    dw_got = got[0:1728, :].reshape(4, 432, 128)
    one_got = got[1728:2304, :].reshape(4, 144, 128)
    keep[...] = (total(dw[0:2], dw_got[0:2]) + far_got[0:2].astype(F32)).astype(BF)
    part = total(dw[2:4], dw_got[2:4]) + far_got[2:4].astype(F32)
    send[0:864, :] = part.astype(BF).reshape(864, 128)
    one_keep[...] = total(one[0:2], one_got[0:2]).astype(BF)
    send[864:1152, :] = total(one[2:4], one_got[2:4]).astype(BF).reshape(288, 128)
    own_keep[...] = total(own[0:2], own_got[0:2]).astype(BF)
    own_send[...] = total(own[2:4], own_got[2:4]).astype(BF)


def mix_fourth(dw, got, one, own, own_got, keep, send):
    for k, out in enumerate((keep, send)):
        out[0:432, :] = total(dw[k], got[k * 432 : (k + 1) * 432, :]).astype(BF)
        at = 864 + k * 144
        out[432:576, :] = total(one[k], got[at : at + 144, :]).astype(BF)
        out[576:1152, :] = total(own[k], own_got[k]).astype(BF)


def unpack(v, out):
    out[:, 0:128] = v[0:96]
    out[0:48, 128:192] = v[96:144, 0:64]
    out[48:96, 128:192] = v[96:144, 64:128]


def last_mlp(kept, got, *outs):
    sums = total(kept[...], got[...])
    for k in range(2):
        for c in range(6):
            at = (6 * k + c) * 96
            outs[k][:, c * 128 : (c + 1) * 128] = sums[at : at + 96]


def last_heads(kept, got, *outs):
    sums = total(kept[...], got[...])
    for k, out in enumerate(outs):
        unpack(sums[k * 144 : (k + 1) * 144], out)


def keys_again(x_ref, ltt, w0, w1, kn, vn, kt, qt):
    ws = [
        jnp.concatenate([v[k * 192 : (k + 1) * 192, :] for v in (w0, w1)], 0) for k in range(3)
    ]
    qt[...] = (dot(ws[0], ltt[...]).astype(BF).astype(F32) * SCALE).astype(BF)
    keys = dot_nt(x_ref[...], ws[1]).astype(BF)
    kn[...] = keys
    vn[...] = dot_nt(x_ref[...], ws[2]).astype(BF)
    kt[...] = keys.astype(F32).T.astype(BF)


def cross_backward(dp_ref, *refs, half):
    me = dp_ref[0]
    pays = refs[:4]
    tnt, ltt, tbs, hot, w0, w1, kn, vn, kt, qt = refs[4:14]
    rest = refs[14:]
    if half == 0:
        early, dg_in, rest = rest[0], rest[1], rest[2:]
        dk, dv, mine, other, dw0, dw1, dg = rest[:7]
    else:
        dk, dv, dq_out, dw0, dw1, dg = rest[:6]
    dq, do, own, lse, delta = rest[-5:]
    ws = [
        jnp.concatenate([v[k * 192 : (k + 1) * 192, :] for v in (w0, w1)], 0) for k in range(3)
    ]
    for r in range(4):
        st = pays[r][768:848, :].astype(F32)
        sums = (st[0:16] + st[16:32] + st[32:48], st[48:64] + st[64:80])
        for gi in range(2):
            src = (2 * half + gi) ^ r
            do[gi * 192 : (gi + 1) * 192, r * LAT : (r + 1) * LAT] = pays[r][
                src * 192 : (src + 1) * 192, :
            ]
            for j in range(GROUP):
                for table, v in zip((lse, delta), sums):
                    at = src * GROUP + j
                    table[gi * GROUP + j, r : r + 1, :] = v[at : at + 1, :]
    fill_masks(tbs[...], own)
    block_rows = hot[...]

    def two_heads(i, _):
        lanes = pl.ds(pl.multiple_of(i * 128, 128), 128)
        tb = tbs[...]
        qp, dop = qt[lanes, :], do[lanes, :]
        s = dot(widen(kn[:, lanes], own[...]), pile(qp))
        dp = dot(widen(vn[:, lanes], own[...]), pile(dop))
        probs, grads = [], []
        for j in range(2):
            h = 2 * i + j
            rows = [lse[h, b : b + 1, :] for b in range(NSEG)]
            p = jnp.exp(s[:, j * LAT : (j + 1) * LAT] - pick(tb, rows))
            rows = [delta[h, b : b + 1, :] for b in range(NSEG)]
            ds = (p * (dp[:, j * LAT : (j + 1) * LAT] - pick(tb, rows))).astype(BF)
            probs.append(widen(p.astype(BF), own[...]))
            grads.append(widen(ds, own[...]))
            at = pl.ds(pl.multiple_of(i * 128 + j * HEAD, HEAD), HEAD)
            kth = kt[at, :]
            k4 = jnp.concatenate([kth * block_rows[b : b + 1, :] for b in range(NSEG)], 0)
            dqh = (dot(k4, ds) * SCALE).astype(BF)
            dq[at, :] = jnp.concatenate(
                [dqh[b * HEAD : (b + 1) * HEAD, :] for b in range(NSEG)], 1
            )
        top = lax.broadcasted_iota(jnp.int32, qp.shape, 0) < HEAD
        zero = jnp.zeros_like(qp)
        for out, parts, t in ((dk, grads, qp), (dv, probs, dop)):
            right = jnp.concatenate([jnp.where(top, t, zero), jnp.where(top, zero, t)], 1)
            out[:, lanes] = dot_nt(jnp.concatenate(parts, 1), right).astype(BF)
        return 0

    lax.fori_loop(0, 3, two_heads, 0, unroll=True)

    for k in range(3):
        full = dot_nt(ltt[...], dq[...]) if k == 2 else dot(tnt[...], (dk, dv)[k][...])

        def put0(b, piece, k=k):
            dw0[place_of(me, b, (0, 1, 2)), k * 144 : (k + 1) * 144, :] = piece

        def put1(b, piece, k=k):
            dw1[place_of(me, b, (0, 1, 2)), k * 144 : (k + 1) * 144, :] = piece

        pack_halves(full, put0, put1)
        prod = full * ws[(k + 1) % 3].astype(F32).T
        part = prod[:, 0:128] + prod[:, 128:256] + prod[:, 256:384]
        if k == 0:
            gain_tok = part
            continue
        if k == 1:
            part += gain_tok
        part = jnp.sum(part.T, axis=0, keepdims=True)
        dg[k - 1 : k, :] = part if half == 1 else dg_in[k - 1 : k, :] + part
    if half == 0:
        for b in range(NSEG):
            out = (mine, other)[b & 1]
            out[b >> 1, 0:384, :] = dq[:, b * LAT : (b + 1) * LAT]
            out[b >> 1, 384:768, :] = early[:, b * LAT : (b + 1) * LAT]
    else:
        dq_out[...] = dq[...]


def pair_queries(mine, got, mlp, mlp_got, two, near, send, out):
    for k in range(2):
        for g in range(4):
            at, there = g * 192, (g ^ 1) * 192
            v = total(mine[k, at : at + 192, :], got[k, there : there + 192, :])
            if k:
                send[at : at + 192, :] = v.astype(BF)
            else:
                near[at : at + 192, :] = v
    out[...] = two[...] + total(mlp[0], mlp_got[0])
    v = total(mlp[1], mlp_got[1]).astype(BF)
    for c in range(6):
        send[768 + c * 128 : 896 + c * 128, :] = v[:, c * 128 : (c + 1) * 128]


def opening(side_ref, lat, gain, wq, wk, wv, out, ws, first):
    y = (standardize(lat[...].astype(F32))[0] * as_row(gain)).astype(BF)
    out[...] = y
    for k, w in enumerate((wq, wk, wv)):
        ws[k * 192 : (k + 1) * 192, :] = w[...]
    first[0:128, :] = y
    first[128:416, :] = ws[pl.ds(pl.multiple_of(side_ref[0] * 288, 16), 288), :]


def stack_weights(side_ref, *refs):
    stack, half, last = refs[5:]
    for k in range(5):
        stack[k * 192 : (k + 1) * 192, :] = refs[k][...]
    half[...] = stack[pl.ds(pl.multiple_of(side_ref[0] * 320, 16), 320), :]
    last[...] = stack[640:960, :]


def prepare(rank_ref, ids, owner, tok, gain, out, out_t, tbs, hot):
    rank = rank_ref[0]
    rows = tok.shape[0]
    mine = ids[:, 0:rows]
    for r in range(1, ids.shape[1] // rows):
        mine = jnp.where(rank == r, ids[:, r * rows : (r + 1) * rows], mine)
    block = jnp.zeros((1, rows), jnp.int32)
    for seg in range(NSEG):
        block = jnp.where(mine == seg, lax.bitwise_xor(owner[0, seg], rank), block)
    block = block.astype(F32)
    eight = lax.broadcasted_iota(jnp.int32, (8, rows), 0).astype(F32)
    hot[...] = jnp.where(jnp.broadcast_to(block, (8, rows)) == eight, 1.0, 0.0).astype(BF)
    tbs[...] = jnp.broadcast_to(block, (128, rows)).T
    xhat, _ = standardize(tok[...].astype(F32))
    y = (xhat * as_row(gain)).astype(BF)
    out[...] = y
    out_t[...] = y.astype(F32).T.astype(BF)


def token_end(dk0, dv0, dk1, dv1, w0, w1, w2, w3, tok, gain, out):
    xhat, inv = standardize(tok[...].astype(F32))
    dy = None
    for k, (a, b) in enumerate(((dk0, dk1), (dv0, dv1))):
        at = (k + 1) * 192
        for grad, pieces in ((a, (w0, w1)), (b, (w2, w3))):
            w = jnp.concatenate([p[at : at + 192, :] for p in pieces], 0)
            part = dot(grad[...], w)
            dy = part if dy is None else dy + part
    out[...] = norm_back(dy, xhat, inv, as_row(gain))


def latent_end(*refs):
    near, far, part, w0, w1, w2, w3, lat, g1, gain, out, new, dqt = refs
    for c in range(6):
        at = slice(c * 128, (c + 1) * 128)
        v = part[:, at] + far[768 + c * 128 : 896 + c * 128, :].astype(F32)
        new[:, at] = v.astype(BF)
    for g in range(4):
        at, there = g * 192, (g ^ 2) * 192
        v = near[at : at + 192, :] + far[there : there + 192, :].astype(F32)
        dqt[at : at + 192, :] = v.astype(BF)
    wq = jnp.concatenate([w[0:192, :] for w in (w0, w1, w2, w3)], 0)
    dlat = dot(dqt[...].astype(F32).T.astype(BF), wq)
    xhat, inv = standardize(lat[...].astype(F32))
    out[...] = g1[...] + norm_back(dlat, xhat, inv, as_row(gain))


def per_device(
    tokens,
    latents,
    segment_ids,
    segment_block,
    block_mask,
    gain_tok,
    gain_cross,
    gain_self,
    gain_mlp,
    wq_cross,
    wk_cross,
    wv_cross,
    wo_cross,
    wq_self,
    wk_self,
    wv_self,
    wo_self,
    w_up,
    w_down,
    d_latents,
):
    mp, dp = lax.axis_size("mp"), lax.axis_size("dp")
    fine = dp // 8
    low = fine.bit_length() - 1
    rank, place = lax.axis_index("mp"), lax.axis_index("dp")
    row = place // fine
    side = (place >> low) & 1
    _, n_tok, width = tokens.shape
    hid = w_up.shape[1]
    part = width // 8
    tok, lat, cot = tokens[0], latents[0], d_latents[0]
    full, sq = (LAT, width), (width, LAT)

    def after(v, *first):
        return lax.optimization_barrier((v,) + first)[0]

    def together(*v):
        return lax.optimization_barrier(v)

    def swap(v, r):
        return lax.ppermute(v, "mp", [(i, i ^ r) for i in range(mp)])

    def cross(v, k):
        flip = (1 << low) * (1, 2, 4, 6)[k]
        return lax.ppermute(v, "dp", [(i, i ^ flip) for i in range(dp)])

    def share(outs):
        return [outs[0]] + [swap(outs[r], r) for r in (1, 2, 3)]

    def add(a, b):
        return a.astype(F32) + b.astype(F32)

    latn, own, first = kernel_call(
        opening,
        [(full, BF), ((576, width), BF), ((416, width), BF)],
        0,
        lat,
        gain_cross,
        wq_cross.T,
        wk_cross.T,
        wv_cross.T,
        scalars=(side,),
        vmem=56,
    )
    l_near, near = swap(latn, 1), swap(own, 1)
    first2 = swap(first, 2)
    stack, half, last = kernel_call(
        stack_weights,
        [((960, width), BF)] + [((320, width), BF)] * 2,
        0,
        wo_cross.T,
        after(wq_self.T, latn),
        wk_self.T,
        wv_self.T,
        wo_self.T,
        scalars=(side,),
        vmem=56,
    )
    tokn, toknt, tbs, hot = kernel_call(
        prepare,
        [((n_tok, width), BF), ((width, n_tok), BF), ((n_tok, 128), F32), ((8, n_tok), BF)],
        2 * 10**9,
        segment_ids,
        segment_block,
        after(tok, stack),
        gain_tok,
        scalars=(rank,),
        tables=(1,),
        vmem=16,
    )
    first2 = after(first2, tokn, l_near, near)
    lats = [latn, l_near, first2, swap(first2, 1)]

    def cross_call(weights, early, gate):
        second = bool(early)
        outs = kernel_call(
            functools.partial(cross_forward, second=second),
            [((2, SHARE * (1 + second), LAT), BF)] * 2
            + [((576, width), BF)] * (2 * second),
            9 * 10**9,
            after(tokn, *gate),
            *lats,
            tbs,
            hot,
            *weights,
            *early,
            scalars=(side,),
            scratch=[((n_tok, 384), BF), ((384, n_tok), BF), ((384, NSEG * LAT), BF)]
            + [((n_tok, 512), BF), ((NSEG, 8, LAT), F32)],
            vmem=VMEM_CROSS,
        )
        return outs[:2], outs[2:]

    half2, last2 = swap(after(half, first), 2), swap(after(last, first), 2)
    far_x = cross(first2[128:416], 0)
    pays, _ = cross_call([own, near], [], [])
    far_x, half2, *pays = together(far_x, half2, *pays)
    half_x, half3 = cross(after(half2, far_x), 0), swap(half2, 1)
    (mine, other), (far, far_near) = cross_call(
        [far_x, swap(far_x, 1)], pays, [half3]
    )
    stack_near = swap(after(stack, far_x), 1)
    got = swap(other, 1)
    mine, half_x, last2, stack_near = together(mine, half_x, last2, stack_near)
    mine, pay_send = kernel_call(
        merge_pair, [((2 * SHARE, LAT), BF)] * 2, 10**9, mine, got
    )
    pay_far = swap(pay_send, 2)
    pieces = [stack, stack_near, half2, half_x, last2]
    pieces += [half3, swap(after(half_x, mine), 1), swap(after(last2, mine), 1)]
    weights = kernel_call(
        join_weights, [((768, width), BF)] * 5, 3 * 10**9, *pieces, scalars=(side,), vmem=20
    )
    pays = [mine, pay_far]

    attn, lse, one, two, e_send, mlp_in, at, probs, kts, qts, vs, e_other, e_own = kernel_call(
        latent_forward,
        [
            (sq, BF),
            ((16, LAT), F32),
            (full, F32),
            (full, F32),
            ((1152, LAT), BF),
            (full, BF),
            (sq, BF),
            ((12 * LAT, LAT), F32),
            (sq, BF),
            (sq, BF),
            (full, BF),
            ((2, 384, LAT), BF),
            ((384, LAT), BF),
        ],
        8 * 10**9,
        block_mask,
        *pays,
        lat,
        gain_self,
        gain_mlp,
        *weights,
        scalars=(rank,),
        tables=(0,),
        vmem=16,
    )
    x_far, x_near = swap(mlp_in, 2), swap(mlp_in, 1)
    e_got = swap(e_other, 1)
    c_far = after(swap(after(cot, pay_send), 2), mlp_in)
    cots = [cot, swap(after(cot, pay_send), 1), c_far, swap(c_far, 1)]
    dh, cot_t, lat_t = kernel_call(
        mlp_before,
        [((4 * LAT, hid), F32), ((width, 4 * LAT), BF), ((width, 4 * LAT), BF)],
        4 * 10**9,
        *cots[:3],
        after(cots[3], mlp_in),
        *lats,
        w_down,
    )
    xs = [mlp_in, x_near, x_far, swap(after(x_far, dh), 1)]
    mine, other, hidden, dpre = kernel_call(
        mlp_main,
        [((2, LAT, width), BF)] * 2 + [((4 * LAT, hid), BF)] * 2,
        3 * 10**9,
        *xs,
        dh,
        w_up,
    )
    got = swap(other, 1)
    back_near, back_send = add(mine[0], got[0]), add(mine[1], got[1]).astype(BF)
    back_far = swap(back_send, 2)
    rows_of = part * hid // 128
    up, up_send, down, down_send = kernel_call(
        mlp_weights,
        [((4, rows_of, 128), BF)] * 4,
        3 * 10**9,
        *xs,
        cot_t,
        hidden,
        after(dpre, back_send),
        scalars=(row,),
        scratch=[((8, rows_of, 128), BF)],
    )
    up_got, down_got = cross(up_send, 1), cross(down_send, 0)
    n_far = swap(jnp.concatenate([after(e_send, up_send), e_got[1]], 0), 2)
    e_near = swap(after(e_send, up_send), 1)

    pay, g1, late, m_own, m_other, dg_mlp, dg_self = kernel_call(
        latent_backward,
        [((848, LAT), BF), (full, F32), ((2112, LAT), BF)]
        + [((576, LAT), BF), ((2, 576, LAT), BF)]
        + [((1, width), F32)] * 2,
        9 * 10**9,
        block_mask,
        back_near,
        after(back_far, up_send),
        two,
        one,
        cot,
        attn,
        lse,
        probs,
        kts,
        qts,
        vs,
        gain_self,
        gain_mlp,
        *weights,
        scalars=(rank,),
        scratch=[(sq, BF)] * 3,
        tables=(0,),
        vmem=VMEM_LATENT,
    )
    pay, n_far = together(pay, n_far)
    p_far, p_near = swap(pay, 2), swap(pay, 1)
    pays = [pay, p_near, p_far, swap(p_far, 1)]

    def part_sum(kept, got):
        n = kept.shape[0] // 2
        return add(kept[:n], got[:n]).astype(BF), add(kept[n:], got[n:]).astype(BF)

    up, up_send = part_sum(up, up_got)
    down, down_send = part_sum(down, down_got)
    forwards = kernel_call(
        mlp_out, [((2, LAT, width), BF)] * 2, 10**9, after(hidden, pay), w_down
    )
    f_got = swap(forwards[1], 1)
    late = after(late, pay)
    m_near, g_near = swap(after(m_other, pay), 1), swap(late, 1)
    n_last = swap(after(n_far, p_far), 1)
    g_send = jnp.concatenate([after(late, p_far), m_near[1]], 0)

    def again(ws, gate):
        return kernel_call(
            keys_again,
            [((n_tok, 384), BF)] * 2 + [((384, n_tok), BF), ((384, NSEG * LAT), BF)],
            2 * 10**9,
            after(tokn, gate),
            lat_t,
            *ws,
        )

    keys1 = again((far, far_near), pay)

    def cross_back(half, ws, keys, more, gate):
        return kernel_call(
            functools.partial(cross_backward, half=half),
            [((n_tok, 384), BF)] * 2
            + ([((2, 768, LAT), BF)] * 2 if half == 0 else [((384, NSEG * LAT), BF)])
            + [((8, 432, 128), BF)] * 2
            + [((2, width), F32)],
            11 * 10**9,
            after(pays[0], *gate),
            *pays[1:],
            toknt,
            lat_t,
            tbs,
            hot,
            *ws,
            *keys,
            *more,
            scalars=(row,),
            scratch=[((384, NSEG * LAT), BF)] * 2
            + [((n_tok, 512), BF)]
            + [((8, NSEG, LAT), F32)] * 2,
            vmem=VMEM_CROSS,
        )

    dk1, dv1, dq1, dw, other, dg_cross = cross_back(
        1, (far, far_near), keys1, (), (up_send, down_send, f_got, g_near, g_send, n_last)
    )
    g_far = swap(g_send, 2)
    up_got, down_got = cross(up_send, 0), cross(down_send, 1)
    other, up_got, down_got = together(other, up_got, down_got)
    sent, far_dw, mlp_keep, mlp_send = kernel_call(
        mix_first,
        [((4, 432, 128), BF)] * 2 + [((2 * rows_of, 128), BF)] * 2,
        10**9,
        dw,
        swap(other, 1),
        up,
        up_got,
        down,
        down_got,
    )
    dk0, dv0, dq_mine, dq_other, dw, other, dg_cross = cross_back(
        0, (own, near), again((own, near), other), (dq1, dg_cross), (sent,)
    )
    got, mlp_got = cross(sent, 0), cross(mlp_send, 2)
    other, got, mlp_got, g_far = together(other, got, mlp_got, g_far)
    dg_tok, dg_cross = (
        dg_cross[k : k + 1] / g.astype(F32)[None, :] for k, g in enumerate((gain_tok, gain_cross))
    )
    gains = jnp.concatenate([dg_tok, dg_cross, dg_self, dg_mlp], 0)
    dw_got, g_last = swap(other, 1), swap(g_far, 1)
    dq_got, gains_got = swap(after(dq_other, other), 1), swap(after(gains, other), 1)
    mine, mine_send, one_keep, one_send = kernel_call(
        latent_weights,
        [((4, 576, 128), BF)] * 2 + [((4, 144, 128), BF)] * 2,
        2 * 10**9,
        e_send,
        e_near,
        n_far,
        n_last,
        late,
        g_near,
        g_far,
        g_last,
        m_own,
        m_near,
        e_own,
        e_got,
        scalars=(row,),
        scratch=[((8, 576, 128), BF), ((8, 144, 128), BF)],
    )
    dw, sent, far_send = kernel_call(
        mix_second,
        [((4, 432, 128), BF), ((2304, 128), BF), ((4, 432, 128), BF)],
        10**9,
        dw,
        dw_got,
        far_dw,
        got,
        one_send,
    )
    got, far_got, mine_got = cross(sent, 0), swap(far_send, 2), cross(mine_send, 1)
    gains = after(gains + gains_got, sent)
    gains_got = swap(gains, 2)
    (out_tok,) = kernel_call(
        token_end,
        [((n_tok, width), F32)],
        5 * 10**9,
        dk0,
        dv0,
        dk1,
        after(dv1, sent, mine_send, far_send),
        own,
        near,
        far,
        far_near,
        tok,
        gain_tok,
        vmem=24,
    )
    got, far_got, mine_got, gains_got, out_tok = together(
        got, far_got, mine_got, gains_got, out_tok
    )
    dw, sent, one_keep, mine, mine_send = kernel_call(
        mix_third,
        [
            ((2, 432, 128), BF),
            ((1152, 128), BF),
            ((2, 144, 128), BF),
            ((2, 576, 128), BF),
            ((2, 576, 128), BF),
        ],
        10**9,
        dw,
        got,
        far_got,
        one_keep,
        mine,
        mine_got,
    )
    got, mine_got = cross(sent, 1), cross(mine_send, 0)
    gains = after(gains + gains_got, sent)
    gains_got = cross(gains, 0)
    dq_near, dq_send, new_near = kernel_call(
        pair_queries,
        [(sq, F32), ((2 * width, LAT), BF), (full, F32)],
        10**9,
        after(dq_mine, sent),
        dq_got,
        forwards[0],
        f_got,
        two,
    )
    dq_far = swap(dq_send, 2)
    mlps = kernel_call(
        last_mlp, [((96, hid), F32)] * 2, 10**9, mlp_keep, after(mlp_got, dq_send)
    )
    got, mine_got, gains_got, dq_far, *mlps = together(got, mine_got, gains_got, dq_far, *mlps)
    kept, sent = kernel_call(
        mix_fourth, [((1152, 128), BF)] * 2, 10**9, dw, got, one_keep, mine, mine_got
    )
    got = cross(sent, 2)
    grad_lat, new_latents, _ = kernel_call(
        latent_end,
        [(full, F32), (full, BF), (sq, BF)],
        3 * 10**9,
        dq_near,
        after(dq_far, sent),
        new_near,
        own,
        near,
        far,
        far_near,
        lat,
        g1,
        gain_cross,
    )
    gains = after(gains + gains_got, sent)
    gains = gains + cross(gains, 1)
    gains = gains + cross(gains, 2)
    for k in range(low):
        gains = gains + lax.ppermute(gains, "dp", [(i, i ^ (1 << k)) for i in range(dp)])
    lasts = kernel_call(last_heads, [((96, 192), F32)] * 8, 10**9, kept, got)

    groups = [list(range(k * fine, (k + 1) * fine)) for k in range(8)]

    def shard(v):
        if fine == 1:
            return v
        return lax.psum_scatter(v, "dp", scatter_dimension=0, axis_index_groups=groups, tiled=True)

    order = (lasts[2], lasts[0], lasts[1], *lasts[3:], *mlps)
    return (
        new_latents[None],
        out_tok[None],
        grad_lat[None],
        *(gains[k] for k in range(4)),
        *(shard(v) for v in order),
    )


def solution(mesh):
    rows, cols, lone = P("dp", "mp", None), P(None, "mp"), P("dp", None)
    in_specs = (rows, rows, lone, lone, lone) + (P(),) * 4 + (cols,) * 10 + (rows,)
    out_specs = (rows,) * 3 + (P(),) * 4 + (P("dp", "mp"),) * 10
    return jax.shard_map(
        per_device, mesh=mesh, in_specs=in_specs, out_specs=out_specs, check_vma=False
    )
```

```python
import functools
import math

import jax
import jax.numpy as jnp
from jax import lax
from jax.experimental import pallas as pl
from jax.experimental.pallas import tpu as pltpu
from jax.sharding import PartitionSpec as P

HEAD = 64
LAT = 128
NSEG = 4
GROUP = 3
EPS = 1e-05
FAR = -1e30
F32 = jnp.float32
BF = jnp.bfloat16
SCALE = 1.0 / math.sqrt(HEAD)
MIB = 1024 * 1024
VMEM_CROSS = 20
VMEM_LATENT = 20


def dot(a, b):
    return lax.dot_general(a, b, (((1,), (0,)), ((), ())), preferred_element_type=F32)


def dot_nt(a, b):
    return lax.dot_general(a, b, (((1,), (1,)), ((), ())), preferred_element_type=F32)


def standardize(v):
    center = v - jnp.mean(v, axis=-1, keepdims=True)
    inv = lax.rsqrt(jnp.mean(center * center, axis=-1, keepdims=True) + EPS)
    return center * inv, inv


def norm_back(dy, xhat, inv, gain):
    s = dy * gain
    return inv * (
        s - jnp.mean(s, axis=-1, keepdims=True) - xhat * jnp.mean(s * xhat, axis=-1, keepdims=True)
    )


def as_row(gain):
    return gain[...].astype(F32).reshape(1, -1)


def kernel_call(body, outs, flops, *args, scalars=(), scratch=(), tables=(), vmem=12, far=(), loose=()):
    n = len(scalars)
    specs = [pl.BlockSpec(memory_space=pltpu.SMEM)] * n
    specs += [
        pl.BlockSpec(
            memory_space=pltpu.SMEM if i in tables else pl.ANY if i in loose else pltpu.VMEM
        )
        for i in range(len(args))
    ]
    moved = sum(a.size * a.dtype.itemsize for a in args)
    moved += sum(math.prod(s) * jnp.dtype(d).itemsize for s, d in outs)
    return pl.pallas_call(
        body,
        out_shape=[jax.ShapeDtypeStruct(s, d) for s, d in outs],
        in_specs=specs,
        out_specs=[
            pl.BlockSpec(memory_space=pltpu.HBM if i in far else pltpu.VMEM)
            for i in range(len(outs))
        ],
        scratch_shapes=[
            pltpu.VMEM(*x) if isinstance(x, tuple) else x for x in scratch
        ],
        compiler_params=pltpu.CompilerParams(vmem_limit_bytes=vmem * MIB),
        cost_estimate=pl.CostEstimate(flops=flops, bytes_accessed=moved, transcendentals=0),
    )(*[jnp.reshape(s, (1,)).astype(jnp.int32) for s in scalars], *args)


def split3(v):
    a = v.astype(BF).astype(F32)
    b = (v - a).astype(BF).astype(F32)
    return a, b, v - a - b


def stack_rows(rows, pad):
    return jnp.concatenate(rows + [jnp.zeros((pad - len(rows), rows[0].shape[1]), F32)], 0)


def pick(tb, rows):
    out = rows[NSEG - 1]
    for b in range(NSEG - 2, -1, -1):
        out = jnp.where(tb == b, rows[b], out)
    return out


def widen(v, own):
    return jnp.concatenate([v] * NSEG, 1) * own


def pile(t):
    top = lax.broadcasted_iota(jnp.int32, (2 * HEAD, LAT), 0) < HEAD
    zero = jnp.zeros((2 * HEAD, LAT), t.dtype)
    rows = []
    for b in range(NSEG):
        part = t[:, b * LAT : (b + 1) * LAT]
        rows.append(
            jnp.concatenate([jnp.where(top, part, zero), jnp.where(top, zero, part)], 1)
        )
    return jnp.concatenate(rows, 0)


def fill_masks(tb, own):
    for b in range(NSEG):
        own[:, b * 128 : (b + 1) * 128] = jnp.where(tb == b, 1.0, 0.0).astype(BF)


SHARE = 416


def cross_forward(side_ref, *refs, second):
    x_ref, l0, l1, first2, first3, tbs, hot = refs[:7]
    rest = refs[7:]
    if second:
        halves, early, rest = rest[:2], rest[2:4], rest[4:]
    else:
        pieces, rest = rest[:2], rest[2:]
    mine, other = rest[:2]
    if second:
        pieces, rest = rest[2:4], rest[4:]
        for piece, by_mp, by_dp in zip(pieces, (first2, first3), halves):
            low = side_ref[0] == 0
            piece[0:288, :] = jnp.where(low, by_mp[128:416, :], by_dp[...])
            piece[288:576, :] = jnp.where(low, by_dp[...], by_mp[128:416, :])
    else:
        rest = rest[2:]
    kn, vt, qt, own, stat = rest
    w = [
        jnp.concatenate([p[k * 192 : (k + 1) * 192, :] for p in pieces], 0) for k in range(3)
    ]
    lat = jnp.concatenate([l0[...], l1[...], first2[0:128, :], first3[0:128, :]], 0)
    qt[...] = (dot_nt(w[0], lat).astype(BF).astype(F32) * SCALE).astype(BF)
    kn[...] = dot_nt(x_ref[...], w[1]).astype(BF)
    vt[...] = dot_nt(x_ref[...], w[2]).T.astype(BF)
    fill_masks(tbs[...], own)
    base = SHARE if second else 0
    stat[...] = jnp.zeros_like(stat)
    block_rows = hot[...]

    def two_heads(i, _):
        lanes = pl.ds(pl.multiple_of(i * 128, 128), 128)
        tb = tbs[...]
        s = dot(widen(kn[:, lanes], own[...]), pile(qt[lanes, :]))
        for j in range(2):
            sj = s[:, j * LAT : (j + 1) * LAT]
            top = [
                jnp.max(jnp.where(tb == b, sj, FAR), axis=0, keepdims=True) for b in range(NSEG)
            ]
            p = jnp.exp(sj - pick(tb, top)).astype(BF)
            total_of = dot(block_rows, p)
            rows = pl.ds(pl.multiple_of(i * 128 + j * HEAD, HEAD), HEAD)
            vth = vt[rows, :]
            v4 = jnp.concatenate([vth * block_rows[b : b + 1, :] for b in range(NSEG)], 0)
            o = dot(v4, p)
            to = pl.ds(pl.multiple_of(base + i * 128 + j * HEAD, 32), HEAD)
            for b in range(NSEG):
                tot = total_of[b : b + 1, :]
                some = tot > 0.0
                safe = jnp.where(some, tot, 1.0)
                stat[b, pl.ds(2 * i + j, 1), :] = jnp.where(some, top[b] + jnp.log(safe), FAR)
                out = (mine, other)[b & 1]
                out[b >> 1, to, :] = (o[b * HEAD : (b + 1) * HEAD, :] / safe).astype(BF)
        return 0

    lax.fori_loop(0, 3, two_heads, 0, unroll=True)
    for b in range(NSEG):
        out = (mine, other)[b & 1]
        out[b >> 1, base + 384 : base + SHARE, :] = jnp.concatenate(
            list(split3(stat[b])) + [jnp.zeros((8, LAT), F32)], 0
        ).astype(BF)
    if second:
        for out, first in ((mine, early[0]), (other, early[1])):
            out[:, 0:SHARE, :] = first[...]


def merge(parts, head, lse_of):
    tables = []
    for read, _ in parts:
        one = []
        for half in range(2):
            st = read(half * SHARE + 384, 32).astype(F32)
            one.append(st[0:8] + st[8:16] + st[16:24])
        tables.append(one)
    for g in range(4):
        for j in range(GROUP):
            found = []
            for (read, flip), table in zip(parts, tables):
                src = g ^ flip
                half, at = src >> 1, (src & 1) * GROUP + j
                found.append(
                    (table[half][at : at + 1, :], read(half * SHARE + at * HEAD, HEAD).astype(F32))
                )
            top = functools.reduce(jnp.maximum, [f[0] for f in found])
            w = [jnp.exp(f[0] - top) for f in found]
            all_w = functools.reduce(jnp.add, w)
            o = functools.reduce(jnp.add, [a * f[1] for a, f in zip(w, found)]) / all_w
            head(g, j, o.astype(BF))
            lse_of(g, j, top + jnp.log(all_w))


def merge_pair(mine, got, keep, send):
    for k, out in enumerate((keep, send)):
        rows = [[], []]

        def head(g, j, o, out=out):
            at = (g >> 1) * SHARE + ((g & 1) * GROUP + j) * HEAD
            out[at : at + HEAD, :] = o

        def lse_of(g, j, v, rows=rows):
            rows[g >> 1].append(v)

        merge(
            [
                (lambda a, n, k=k: mine[k, a : a + n, :], 0),
                (lambda a, n, k=k: got[k, a : a + n, :], 1),
            ],
            head,
            lse_of,
        )
        for half in range(2):
            parts = list(split3(stack_rows(rows[half], 8))) + [jnp.zeros((8, LAT), F32)]
            out[half * SHARE + 384 : (half + 1) * SHARE, :] = jnp.concatenate(parts, 0).astype(BF)


def join_weights(side_ref, *refs):
    side, pieces, full = side_ref[0], refs[:8], refs[8:]
    own, near = pieces[:2]
    for r, stack in ((0, own), (1, near)):
        for k in range(5):
            full[k][r * 192 : (r + 1) * 192, :] = stack[k * 192 : (k + 1) * 192, :]
    for r, (by_mp, by_dp, last) in ((2, pieces[2:5]), (3, pieces[5:8])):
        low = side == 0
        stack = jnp.concatenate(
            [
                jnp.where(low, by_mp[...], by_dp[...]),
                jnp.where(low, by_dp[...], by_mp[...]),
                last[...],
            ],
            0,
        )
        for k in range(5):
            full[k][r * 192 : (r + 1) * 192, :] = stack[k * 192 : (k + 1) * 192, :]


def latent_forward(rank_ref, mask_ref, *refs):
    pay = refs[:2]
    lat, g_self, g_mlp = refs[2], refs[3], refs[4]
    full = refs[5:10]
    (
        attn_ref,
        lse_ref,
        one_ref,
        two_ref,
        norm_ref,
        mlp_ref,
        at_ref,
        p_ref,
        kt_ref,
        qt_ref,
        v_ref,
        early_other,
        early_own,
        early_send,
    ) = refs[10:]
    wo_c, wq, wk, wv, wo = full
    keep = mask_ref[0, rank_ref[0]].astype(F32)
    lse_rows = []

    def head(g, j, o):
        at = (g * GROUP + j) * HEAD
        attn_ref[at : at + HEAD, :] = o

    merge(
        [(lambda a, n: pay[0][a : a + n, :], 0), (lambda a, n: pay[1][a : a + n, :], 2)],
        head,
        lambda g, j, v: lse_rows.append(v),
    )
    lse_ref[...] = stack_rows(lse_rows, 16)
    attn = attn_ref[...].astype(F32).T.astype(BF)
    one = lat[...].astype(F32) + keep * dot(attn, wo_c[...])
    one_ref[...] = one
    zhat, _ = standardize(one)
    x = (zhat * as_row(g_self)).astype(BF)
    norm_ref[...] = x.astype(F32).T.astype(BF)
    qt_ref[...] = (dot_nt(wq[...], x).astype(BF).astype(F32) * SCALE).astype(BF)
    kt_ref[...] = dot_nt(wk[...], x).astype(BF)
    vt = dot_nt(wv[...], x).astype(BF)
    k = dot_nt(x, wk[...]).astype(BF)
    v_ref[...] = dot_nt(x, wv[...]).astype(BF)
    zero = jnp.zeros((HEAD, LAT), BF)
    for h in range(4 * GROUP):
        hs = slice(h * HEAD, (h + 1) * HEAD)
        ps = slice((h // 2) * 128, (h // 2) * 128 + 128)
        qh = qt_ref[hs, :]
        s = dot(k[:, ps], jnp.concatenate([qh, zero] if h % 2 == 0 else [zero, qh], 0))
        e = jnp.exp(s - jnp.max(s, axis=0, keepdims=True))
        p = e / jnp.sum(e, axis=0, keepdims=True)
        p_ref[h * LAT : (h + 1) * LAT, :] = p
        at_ref[hs, :] = dot(vt[hs, :], p.astype(BF)).astype(BF)
    two = one + dot(at_ref[...].astype(F32).T.astype(BF), wo[...])
    for r, to in enumerate((early_own, early_other.at[0], early_send, early_other.at[1])):
        to[0:192, :] = at_ref[r * 192 : (r + 1) * 192, :]
        to[192:384, :] = attn_ref[r * 192 : (r + 1) * 192, :]
    two_ref[...] = two
    zhat, _ = standardize(two)
    mlp_ref[...] = (zhat * as_row(g_mlp)).astype(BF)


def mlp_before(c0, c1, c2, c3, l0, l1, first2, first3, down, dh_ref, cot_t, lat_t):
    g = jnp.concatenate([c0[...], c1[...], c2[...], c3[...]], 0)
    dh_ref[...] = dot(g, down[...])
    cot_t[...] = g.astype(F32).T.astype(BF)
    lat = jnp.concatenate([l0[...], l1[...], first2[0:128, :], first3[0:128, :]], 0)
    lat_t[...] = lat.astype(F32).T.astype(BF)


def deal(v, mine, other):
    for r in range(4):
        out = (mine, other)[r & 1]
        out[r >> 1, :, :] = v[r * LAT : (r + 1) * LAT, :]


def mlp_main(x0, x1, x2, x3, dh_ref, up, *outs):
    mine, other, h_ref, d_ref = outs
    c = math.sqrt(2.0 / math.pi)
    x = jnp.concatenate([x0[...], x1[...], x2[...], x3[...]], 0)
    pre = dot(x, up[...])
    sq = pre * pre
    t = jnp.tanh(c * pre * (1.0 + 0.044715 * sq))
    h_ref[...] = (0.5 * pre * (1.0 + t)).astype(BF)
    slope = 0.5 * (1.0 + t) + 0.5 * pre * (1.0 - t * t) * c * (1.0 + 3 * 0.044715 * sq)
    d = (dh_ref[...] * slope).astype(BF)
    d_ref[...] = d
    deal(dot_nt(d, up[...]).astype(BF), mine, other)


def mlp_weights(dp_ref, x0, x1, x2, x3, gt, h_ref, d_ref, *outs):
    me = dp_ref[0]
    rows = outs[4]
    xt = jnp.concatenate([x0[...], x1[...], x2[...], x3[...]], 0).astype(F32).T.astype(BF)
    for k, (lhs, rhs) in enumerate(((xt, d_ref[...]), (gt[...], h_ref[...]))):
        full = dot(lhs, rhs).astype(BF)
        for b in range(8):
            at = place_of(me, b, ((1, 0, 2), (0, 1, 2))[k])
            for c in range(6):
                rows[at, c * 96 : (c + 1) * 96, :] = full[
                    b * 96 : (b + 1) * 96, c * 128 : (c + 1) * 128
                ]
        outs[2 * k][...] = rows[0:4]
        outs[2 * k + 1][...] = rows[4:8]


def mlp_out(h_ref, down, mine, other):
    deal(dot_nt(h_ref[...], down[...]).astype(BF), mine, other)


def latent_backward(rank_ref, mask_ref, *refs):
    b0, b1, two, one, cot, attn, lse, p_ref, kt, qt, v, g_self, g_mlp = refs[:13]
    full = refs[13:18]
    pay, g1_ref, grads, mine, other, send, dg_mlp, dg_self = refs[18:-3]
    dqt_ref, dkt_ref, dvt_ref = refs[-3:]
    wo_c, wq, wk, wv, wo = full
    keep = mask_ref[0, rank_ref[0]].astype(F32)
    dmlp = b0[...] + b1[...].astype(F32)
    zhat, inv = standardize(two[...])
    g2 = cot[...].astype(F32) + norm_back(dmlp, zhat, inv, as_row(g_mlp))
    dg_mlp[...] = jnp.sum(dmlp * zhat, axis=0, keepdims=True)
    low = g2.astype(BF)
    grads[0:768, :] = g2.T.astype(BF)
    dat = dot_nt(wo[...], low).astype(BF)
    zero = jnp.zeros((HEAD, LAT), BF)
    for h in range(4 * GROUP):
        hs = slice(h * HEAD, (h + 1) * HEAD)
        ps = slice((h // 2) * 128, (h // 2) * 128 + 128)
        dh = dat[hs, :]
        p = p_ref[h * LAT : (h + 1) * LAT, :]
        dp = dot(v[:, ps], jnp.concatenate([dh, zero] if h % 2 == 0 else [zero, dh], 0))
        ds = (p * (dp - jnp.sum(p * dp, axis=0, keepdims=True))).astype(BF)
        dvt_ref[hs, :] = dot_nt(dh, p.astype(BF)).astype(BF)
        dqt_ref[hs, :] = (dot(kt[hs, :], ds) * SCALE).astype(BF)
        dkt_ref[hs, :] = dot_nt(qt[hs, :], ds).astype(BF)
    back = dot(dqt_ref[...].astype(F32).T.astype(BF), wq[...])
    back += dot(dkt_ref[...].astype(F32).T.astype(BF), wk[...])
    back += dot(dvt_ref[...].astype(F32).T.astype(BF), wv[...])
    zhat, inv = standardize(one[...])
    g1 = g2 + norm_back(back, zhat, inv, as_row(g_self))
    dg_self[...] = jnp.sum(back * zhat, axis=0, keepdims=True)
    g1_ref[...] = g1
    gc = (keep * g1).astype(BF)
    grads[768:1536, :] = (keep * g1).T.astype(BF)
    for r, to in enumerate((mine, other.at[0], send, other.at[1])):
        for k, part in enumerate((dqt_ref, dkt_ref, dvt_ref)):
            to[k * 192 : (k + 1) * 192, :] = part[r * 192 : (r + 1) * 192, :]
    do = dot_nt(wo_c[...], gc).astype(BF)
    pay[0:768, :] = do
    deltas = []
    for h in range(4 * GROUP):
        hs = slice(h * HEAD, (h + 1) * HEAD)
        deltas.append(
            jnp.sum(do[hs, :].astype(F32) * attn[hs, :].astype(F32), axis=0, keepdims=True)
        )
    parts = list(split3(lse[...])) + list(split3(stack_rows(deltas, 16))[:2])
    pay[768:848, :] = jnp.concatenate(parts, 0).astype(BF)


def bit(v, k):
    return lax.bitwise_and(lax.shift_right_logical(v, k), 1)


def place_of(me, b, bits):
    v = lax.bitwise_xor(me, b)
    return 4 * bit(v, bits[0]) + 2 * bit(v, bits[1]) + bit(v, bits[2])


def pack(whole, third, third_rolled, put):
    low = lax.broadcasted_iota(jnp.int32, (48, 128), 1) < HEAD
    for b in range(8):
        r = 96 * b
        tail = jnp.where(low, third[r : r + 48], third_rolled[r + 48 : r + 96])
        put(b, jnp.concatenate([whole[r : r + 96], tail], 0).astype(BF))


def pack_halves(full, put0, put1):
    low = lax.broadcasted_iota(jnp.int32, (full.shape[0], 128), 1) < HEAD
    a, b, c = full[:, 0:128], full[:, 128:256], full[:, 256:384]
    b_turned, c_turned = pltpu.roll(b, HEAD, 1), pltpu.roll(c, HEAD, 1)
    pack(a, b, b_turned, put0)
    pack(jnp.where(low, b_turned, c_turned), c_turned, c, put1)


def latent_weights(dp_ref, *refs):
    me = dp_ref[0]
    norms, grads, (far, h0, h1, e0, e1) = refs[:4], refs[4:8], refs[8:13]
    heads = (h0, h1.at[0], far.at[0:576, :], far.at[576:1152, :])
    outs = (e0, e1.at[0], far.at[1152:1536, :], far.at[1536:1920, :])
    keep, send, one_keep, one_send, rows, one_rows = refs[13:]
    for k in range(5):
        if k < 3:
            left = jnp.concatenate([n[...] for n in norms], 1)
            right = jnp.concatenate([h[k * 192 : (k + 1) * 192, :] for h in heads], 1)
        else:
            at = (k - 3) * 768
            left = jnp.concatenate([g[at : at + 768, :] for g in grads], 1)
            at = (k - 3) * 192
            right = jnp.concatenate([o[at : at + 192, :] for o in outs], 1)
        full = dot_nt(left, jnp.concatenate([right, right[128:192]], 0))

        def put(b, piece, k=k):
            if k < 4:
                rows[place_of(me, b, (1, 0, 2)), k * 144 : (k + 1) * 144, :] = piece
            else:
                one_rows[place_of(me, b, (0, 1, 2)), :, :] = piece

        pack(full[:, :128], full[:, 128:], full[:, 128:], put)
    keep[...] = rows[0:4]
    send[...] = rows[4:8]
    one_keep[...] = one_rows[0:4]
    one_send[...] = one_rows[4:8]


def total(a, b):
    return a.astype(F32) + b.astype(F32)


def mix_first(dw, dw_got, up, up_got, down, down_got, *outs):
    sent, far_keep, mlp_keep, mlp_send = outs
    far_keep[...] = total(dw[0:4], dw_got[0:4]).astype(BF)
    sent[...] = total(dw[4:8], dw_got[4:8]).astype(BF)
    for k, out in enumerate((mlp_keep, mlp_send)):
        out[0:576, :] = total(up[k], up_got[k]).astype(BF)
        out[576:1152, :] = total(down[k], down_got[k]).astype(BF)


def mix_second(dw, dw_got, far, got, one_send, keep, send, far_send):
    keep[...] = total(dw[0:4], dw_got[0:4]).astype(BF)
    send[0:1728, :] = total(dw[4:8], dw_got[4:8]).astype(BF).reshape(1728, 128)
    send[1728:2304, :] = one_send[...].reshape(576, 128)
    far_send[...] = total(far[...], got[...]).astype(BF)


def mix_third(dw, got, far_got, one, own, own_got, *outs):
    keep, send, one_keep, own_keep, own_send = outs
    dw_got = got[0:1728, :].reshape(4, 432, 128)
    one_got = got[1728:2304, :].reshape(4, 144, 128)
    keep[...] = (total(dw[0:2], dw_got[0:2]) + far_got[0:2].astype(F32)).astype(BF)
    part = total(dw[2:4], dw_got[2:4]) + far_got[2:4].astype(F32)
    send[0:864, :] = part.astype(BF).reshape(864, 128)
    one_keep[...] = total(one[0:2], one_got[0:2]).astype(BF)
    send[864:1152, :] = total(one[2:4], one_got[2:4]).astype(BF).reshape(288, 128)
    own_keep[...] = total(own[0:2], own_got[0:2]).astype(BF)
    own_send[...] = total(own[2:4], own_got[2:4]).astype(BF)


def mix_fourth(dw, got, one, own, own_got, keep, send):
    for k, out in enumerate((keep, send)):
        out[0:432, :] = total(dw[k], got[k * 432 : (k + 1) * 432, :]).astype(BF)
        at = 864 + k * 144
        out[432:576, :] = total(one[k], got[at : at + 144, :]).astype(BF)
        out[576:1152, :] = total(own[k], own_got[k]).astype(BF)


def unpack(v, out):
    out[:, 0:128] = v[0:96]
    out[0:48, 128:192] = v[96:144, 0:64]
    out[48:96, 128:192] = v[96:144, 64:128]


def last_mlp(kept, got, *outs):
    sums = total(kept[...], got[...])
    for k in range(2):
        for c in range(6):
            at = (6 * k + c) * 96
            outs[k][:, c * 128 : (c + 1) * 128] = sums[at : at + 96]


def last_heads(kept, got, *outs):
    sums = total(kept[...], got[...])
    for k, out in enumerate(outs):
        unpack(sums[k * 144 : (k + 1) * 144], out)


def keys_again(x_ref, ltt, w0, w1, kn, vn, kt, qt):
    ws = [
        jnp.concatenate([v[k * 192 : (k + 1) * 192, :] for v in (w0, w1)], 0) for k in range(3)
    ]
    qt[...] = (dot(ws[0], ltt[...]).astype(BF).astype(F32) * SCALE).astype(BF)
    keys = dot_nt(x_ref[...], ws[1]).astype(BF)
    kn[...] = keys
    vn[...] = dot_nt(x_ref[...], ws[2]).astype(BF)
    kt[...] = keys.astype(F32).T.astype(BF)


def cross_backward(dp_ref, *refs, half):
    me = dp_ref[0]
    pays = refs[:4]
    tnt, ltt, tbs, hot, w0, w1, kn, vn, kt, qt = refs[4:14]
    rest = refs[14:]
    if half == 0:
        early, dg_in, rest = rest[0], rest[1], rest[2:]
        dk, dv, mine, other, dw0, dw1, dg = rest[:7]
    else:
        dk, dv, dq_out, dw0, dw1, dg = rest[:6]
    dq, do, own, lse, delta = rest[-5:]
    ws = [
        jnp.concatenate([v[k * 192 : (k + 1) * 192, :] for v in (w0, w1)], 0) for k in range(3)
    ]
    for r in range(4):
        st = pays[r][768:848, :].astype(F32)
        sums = (st[0:16] + st[16:32] + st[32:48], st[48:64] + st[64:80])
        for gi in range(2):
            src = (2 * half + gi) ^ r
            do[gi * 192 : (gi + 1) * 192, r * LAT : (r + 1) * LAT] = pays[r][
                src * 192 : (src + 1) * 192, :
            ]
            for j in range(GROUP):
                for table, v in zip((lse, delta), sums):
                    at = src * GROUP + j
                    table[gi * GROUP + j, r : r + 1, :] = v[at : at + 1, :]
    fill_masks(tbs[...], own)
    block_rows = hot[...]

    def two_heads(i, _):
        lanes = pl.ds(pl.multiple_of(i * 128, 128), 128)
        tb = tbs[...]
        qp, dop = qt[lanes, :], do[lanes, :]
        s = dot(widen(kn[:, lanes], own[...]), pile(qp))
        dp = dot(widen(vn[:, lanes], own[...]), pile(dop))
        probs, grads = [], []
        for j in range(2):
            h = 2 * i + j
            rows = [lse[h, b : b + 1, :] for b in range(NSEG)]
            p = jnp.exp(s[:, j * LAT : (j + 1) * LAT] - pick(tb, rows))
            rows = [delta[h, b : b + 1, :] for b in range(NSEG)]
            ds = (p * (dp[:, j * LAT : (j + 1) * LAT] - pick(tb, rows))).astype(BF)
            probs.append(widen(p.astype(BF), own[...]))
            grads.append(widen(ds, own[...]))
            at = pl.ds(pl.multiple_of(i * 128 + j * HEAD, HEAD), HEAD)
            kth = kt[at, :]
            k4 = jnp.concatenate([kth * block_rows[b : b + 1, :] for b in range(NSEG)], 0)
            dqh = (dot(k4, ds) * SCALE).astype(BF)
            dq[at, :] = jnp.concatenate(
                [dqh[b * HEAD : (b + 1) * HEAD, :] for b in range(NSEG)], 1
            )
        top = lax.broadcasted_iota(jnp.int32, qp.shape, 0) < HEAD
        zero = jnp.zeros_like(qp)
        for out, parts, t in ((dk, grads, qp), (dv, probs, dop)):
            right = jnp.concatenate([jnp.where(top, t, zero), jnp.where(top, zero, t)], 1)
            out[:, lanes] = dot_nt(jnp.concatenate(parts, 1), right).astype(BF)
        return 0

    lax.fori_loop(0, 3, two_heads, 0, unroll=True)

    for k in range(3):
        full = dot_nt(ltt[...], dq[...]) if k == 2 else dot(tnt[...], (dk, dv)[k][...])

        def put0(b, piece, k=k):
            dw0[place_of(me, b, (0, 1, 2)), k * 144 : (k + 1) * 144, :] = piece

        def put1(b, piece, k=k):
            dw1[place_of(me, b, (0, 1, 2)), k * 144 : (k + 1) * 144, :] = piece

        pack_halves(full, put0, put1)
        prod = full * ws[(k + 1) % 3].astype(F32).T
        part = prod[:, 0:128] + prod[:, 128:256] + prod[:, 256:384]
        if k == 0:
            gain_tok = part
            continue
        if k == 1:
            part += gain_tok
        part = jnp.sum(part.T, axis=0, keepdims=True)
        dg[k - 1 : k, :] = part if half == 1 else dg_in[k - 1 : k, :] + part
    if half == 0:
        for b in range(NSEG):
            out = (mine, other)[b & 1]
            out[b >> 1, 0:384, :] = dq[:, b * LAT : (b + 1) * LAT]
            out[b >> 1, 384:768, :] = early[:, b * LAT : (b + 1) * LAT]
    else:
        dq_out[...] = dq[...]


def pair_queries(mine, got, mlp, mlp_got, two, near, send, out):
    for k in range(2):
        for g in range(4):
            at, there = g * 192, (g ^ 1) * 192
            v = total(mine[k, at : at + 192, :], got[k, there : there + 192, :])
            if k:
                send[at : at + 192, :] = v.astype(BF)
            else:
                near[at : at + 192, :] = v
    out[...] = two[...] + total(mlp[0], mlp_got[0])
    v = total(mlp[1], mlp_got[1]).astype(BF)
    for c in range(6):
        send[768 + c * 128 : 896 + c * 128, :] = v[:, c * 128 : (c + 1) * 128]


def opening(side_ref, lat, gain, wq, wk, wv, out, ws, first):
    y = (standardize(lat[...].astype(F32))[0] * as_row(gain)).astype(BF)
    out[...] = y
    for k, w in enumerate((wq, wk, wv)):
        ws[k * 192 : (k + 1) * 192, :] = w[...]
    first[0:128, :] = y
    first[128:416, :] = ws[pl.ds(pl.multiple_of(side_ref[0] * 288, 16), 288), :]


def stack_weights(side_ref, *refs):
    stack, half, last = refs[5:]
    for k in range(5):
        stack[k * 192 : (k + 1) * 192, :] = refs[k][...]
    half[...] = stack[pl.ds(pl.multiple_of(side_ref[0] * 320, 16), 320), :]
    last[...] = stack[640:960, :]


def prepare(rank_ref, ids, owner, tok, gain, out, out_t, tbs, hot):
    rank = rank_ref[0]
    rows = tok.shape[0]
    mine = ids[:, 0:rows]
    for r in range(1, ids.shape[1] // rows):
        mine = jnp.where(rank == r, ids[:, r * rows : (r + 1) * rows], mine)
    block = jnp.zeros((1, rows), jnp.int32)
    for seg in range(NSEG):
        block = jnp.where(mine == seg, lax.bitwise_xor(owner[0, seg], rank), block)
    block = block.astype(F32)
    eight = lax.broadcasted_iota(jnp.int32, (8, rows), 0).astype(F32)
    hot[...] = jnp.where(jnp.broadcast_to(block, (8, rows)) == eight, 1.0, 0.0).astype(BF)
    tbs[...] = jnp.broadcast_to(block, (128, rows)).T
    xhat, _ = standardize(tok[...].astype(F32))
    y = (xhat * as_row(gain)).astype(BF)
    out[...] = y
    out_t[...] = y.astype(F32).T.astype(BF)


def token_end(dk0, dv0, dk1, dv1, w0, w1, w2, w3, tok, gain, out):
    xhat, inv = standardize(tok[...].astype(F32))
    dy = None
    for k, (a, b) in enumerate(((dk0, dk1), (dv0, dv1))):
        at = (k + 1) * 192
        for grad, pieces in ((a, (w0, w1)), (b, (w2, w3))):
            w = jnp.concatenate([p[at : at + 192, :] for p in pieces], 0)
            part = dot(grad[...], w)
            dy = part if dy is None else dy + part
    out[...] = norm_back(dy, xhat, inv, as_row(gain))


def latent_end(*refs):
    near, far, part, w0, w1, w2, w3, lat, g1, gain, out, new, dqt = refs
    for c in range(6):
        at = slice(c * 128, (c + 1) * 128)
        v = part[:, at] + far[768 + c * 128 : 896 + c * 128, :].astype(F32)
        new[:, at] = v.astype(BF)
    for g in range(4):
        at, there = g * 192, (g ^ 2) * 192
        v = near[at : at + 192, :] + far[there : there + 192, :].astype(F32)
        dqt[at : at + 192, :] = v.astype(BF)
    wq = jnp.concatenate([w[0:192, :] for w in (w0, w1, w2, w3)], 0)
    dlat = dot(dqt[...].astype(F32).T.astype(BF), wq)
    xhat, inv = standardize(lat[...].astype(F32))
    out[...] = g1[...] + norm_back(dlat, xhat, inv, as_row(gain))


def per_device(
    tokens,
    latents,
    segment_ids,
    segment_block,
    block_mask,
    gain_tok,
    gain_cross,
    gain_self,
    gain_mlp,
    wq_cross,
    wk_cross,
    wv_cross,
    wo_cross,
    wq_self,
    wk_self,
    wv_self,
    wo_self,
    w_up,
    w_down,
    d_latents,
):
    mp, dp = lax.axis_size("mp"), lax.axis_size("dp")
    fine = dp // 8
    low = fine.bit_length() - 1
    rank, place = lax.axis_index("mp"), lax.axis_index("dp")
    row = place // fine
    side = (place >> low) & 1
    _, n_tok, width = tokens.shape
    hid = w_up.shape[1]
    part = width // 8
    tok, lat, cot = tokens[0], latents[0], d_latents[0]
    full, sq = (LAT, width), (width, LAT)

    def after(v, *first):
        return lax.optimization_barrier((v,) + first)[0]

    def together(*v):
        return lax.optimization_barrier(v)

    def swap(v, r):
        return lax.ppermute(v, "mp", [(i, i ^ r) for i in range(mp)])

    def cross(v, k):
        flip = (1 << low) * (1, 2, 4, 6)[k]
        return lax.ppermute(v, "dp", [(i, i ^ flip) for i in range(dp)])

    def share(outs):
        return [outs[0]] + [swap(outs[r], r) for r in (1, 2, 3)]

    def add(a, b):
        return a.astype(F32) + b.astype(F32)

    latn, own, first = kernel_call(
        opening,
        [(full, BF), ((576, width), BF), ((416, width), BF)],
        0,
        lat,
        gain_cross,
        wq_cross.T,
        wk_cross.T,
        wv_cross.T,
        scalars=(side,),
        vmem=56,
    )
    l_near, near = swap(latn, 1), swap(own, 1)
    first2 = swap(first, 2)
    stack, half, last = kernel_call(
        stack_weights,
        [((960, width), BF)] + [((320, width), BF)] * 2,
        0,
        wo_cross.T,
        after(wq_self.T, latn),
        wk_self.T,
        wv_self.T,
        wo_self.T,
        scalars=(side,),
        vmem=56,
    )
    tokn, toknt, tbs, hot = kernel_call(
        prepare,
        [((n_tok, width), BF), ((width, n_tok), BF), ((n_tok, 128), F32), ((8, n_tok), BF)],
        2 * 10**9,
        segment_ids,
        segment_block,
        after(tok, stack),
        gain_tok,
        scalars=(rank,),
        tables=(1,),
        vmem=16,
    )
    first2 = after(first2, tokn, l_near, near)
    lats = [latn, l_near, first2, swap(first2, 1)]

    def cross_call(weights, early, gate):
        second = bool(early)
        outs = kernel_call(
            functools.partial(cross_forward, second=second),
            [((2, SHARE * (1 + second), LAT), BF)] * 2
            + [((576, width), BF)] * (2 * second),
            9 * 10**9,
            after(tokn, *gate),
            *lats,
            tbs,
            hot,
            *weights,
            *early,
            scalars=(side,),
            scratch=[((n_tok, 384), BF), ((384, n_tok), BF), ((384, NSEG * LAT), BF)]
            + [((n_tok, 512), BF), ((NSEG, 8, LAT), F32)],
            vmem=VMEM_CROSS,
        )
        return outs[:2], outs[2:]

    half2, last2 = swap(after(half, first), 2), swap(after(last, first), 2)
    far_x = cross(first2[128:416], 0)
    pays, _ = cross_call([own, near], [], [])
    far_x, half2, *pays = together(far_x, half2, *pays)
    half_x, half3 = cross(after(half2, far_x), 0), swap(half2, 1)
    (mine, other), (far, far_near) = cross_call(
        [far_x, swap(far_x, 1)], pays, [half3]
    )
    stack_near = swap(after(stack, far_x), 1)
    got = swap(other, 1)
    mine, half_x, last2, stack_near = together(mine, half_x, last2, stack_near)
    mine, pay_send = kernel_call(
        merge_pair, [((2 * SHARE, LAT), BF)] * 2, 10**9, mine, got
    )
    pay_far = swap(pay_send, 2)
    pieces = [stack, stack_near, half2, half_x, last2]
    pieces += [half3, swap(after(half_x, mine), 1), swap(after(last2, mine), 1)]
    weights = kernel_call(
        join_weights, [((768, width), BF)] * 5, 3 * 10**9, *pieces, scalars=(side,), vmem=20
    )
    pays = [mine, pay_far]

    attn, lse, one, two, selfn, mlp_in, at, probs, kts, qts, vs, e_other, e_own, e_send = kernel_call(
        latent_forward,
        [
            (sq, BF),
            ((16, LAT), F32),
            (full, F32),
            (full, F32),
            (sq, BF),
            (full, BF),
            (sq, BF),
            ((12 * LAT, LAT), F32),
            (sq, BF),
            (sq, BF),
            (full, BF),
            ((2, 384, LAT), BF),
            ((384, LAT), BF),
            ((384, LAT), BF),
        ],
        8 * 10**9,
        block_mask,
        *pays,
        lat,
        gain_self,
        gain_mlp,
        *weights,
        scalars=(rank,),
        tables=(0,),
        vmem=16,
    )
    x_far, x_near = swap(mlp_in, 2), swap(mlp_in, 1)
    e_got = swap(e_other, 1)
    c_far = after(swap(after(cot, pay_send), 2), mlp_in)
    cots = [cot, swap(after(cot, pay_send), 1), c_far, swap(c_far, 1)]
    dh, cot_t, lat_t = kernel_call(
        mlp_before,
        [((4 * LAT, hid), F32), ((width, 4 * LAT), BF), ((width, 4 * LAT), BF)],
        4 * 10**9,
        *cots[:3],
        after(cots[3], mlp_in),
        *lats,
        w_down,
    )
    xs = [mlp_in, x_near, x_far, swap(after(x_far, dh), 1)]
    mine, other, hidden, dpre = kernel_call(
        mlp_main,
        [((2, LAT, width), BF)] * 2 + [((4 * LAT, hid), BF)] * 2,
        3 * 10**9,
        *xs,
        dh,
        w_up,
    )
    got = swap(other, 1)
    back_near, back_send = add(mine[0], got[0]), add(mine[1], got[1]).astype(BF)
    back_far = swap(back_send, 2)
    rows_of = part * hid // 128
    up, up_send, down, down_send = kernel_call(
        mlp_weights,
        [((4, rows_of, 128), BF)] * 4,
        3 * 10**9,
        *xs,
        cot_t,
        hidden,
        after(dpre, back_send),
        scalars=(row,),
        scratch=[((8, rows_of, 128), BF)],
    )
    up_got, down_got = cross(up_send, 1), cross(down_send, 0)
    n_far, n_near = swap(after(selfn, up_send), 2), swap(after(selfn, up_send), 1)

    pay, g1, late, m_own, m_other, m_send, dg_mlp, dg_self = kernel_call(
        latent_backward,
        [((848, LAT), BF), (full, F32), ((1536, LAT), BF)]
        + [((576, LAT), BF), ((2, 576, LAT), BF), ((576, LAT), BF)]
        + [((1, width), F32)] * 2,
        9 * 10**9,
        block_mask,
        back_near,
        after(back_far, up_send),
        two,
        one,
        cot,
        attn,
        lse,
        probs,
        kts,
        qts,
        vs,
        gain_self,
        gain_mlp,
        *weights,
        scalars=(rank,),
        scratch=[(sq, BF)] * 3,
        tables=(0,),
        vmem=VMEM_LATENT,
    )
    pay, n_far = together(pay, n_far)
    p_far, p_near = swap(pay, 2), swap(pay, 1)
    pays = [pay, p_near, p_far, swap(p_far, 1)]

    def part_sum(kept, got):
        n = kept.shape[0] // 2
        return add(kept[:n], got[:n]).astype(BF), add(kept[n:], got[n:]).astype(BF)

    up, up_send = part_sum(up, up_got)
    down, down_send = part_sum(down, down_got)
    forwards = kernel_call(
        mlp_out, [((2, LAT, width), BF)] * 2, 10**9, after(hidden, pay), w_down
    )
    f_got = swap(forwards[1], 1)
    late = after(late, pay)
    m_near, g_near = swap(after(m_other, pay), 1), swap(late, 1)
    n_last = swap(after(n_far, p_far), 1)
    g_far = swap(after(late, p_far), 2)

    def again(ws, gate):
        return kernel_call(
            keys_again,
            [((n_tok, 384), BF)] * 2 + [((384, n_tok), BF), ((384, NSEG * LAT), BF)],
            2 * 10**9,
            after(tokn, gate),
            lat_t,
            *ws,
        )

    keys1, keys0 = again((far, far_near), pay), again((own, near), pay)

    def cross_back(half, ws, keys, more, gate):
        return kernel_call(
            functools.partial(cross_backward, half=half),
            [((n_tok, 384), BF)] * 2
            + ([((2, 768, LAT), BF)] * 2 if half == 0 else [((384, NSEG * LAT), BF)])
            + [((8, 432, 128), BF)] * 2
            + [((2, width), F32)],
            11 * 10**9,
            after(pays[0], *gate),
            *pays[1:],
            toknt,
            lat_t,
            tbs,
            hot,
            *ws,
            *keys,
            *more,
            scalars=(row,),
            scratch=[((384, NSEG * LAT), BF)] * 2
            + [((n_tok, 512), BF)]
            + [((8, NSEG, LAT), F32)] * 2,
            vmem=VMEM_CROSS,
        )

    dk1, dv1, dq1, dw, other, dg_cross = cross_back(
        1, (far, far_near), keys1, (), (keys0[0], up_send, down_send, g_near, m_near, n_last)
    )
    up_got, down_got = cross(up_send, 0), cross(down_send, 1)
    other, up_got, down_got, g_far, f_got = together(other, up_got, down_got, g_far, f_got)
    h_send = jnp.concatenate([after(m_send, other), m_near[1], e_send, e_got[1]], 0)
    g_last = swap(g_far, 1)
    sent, far_dw, mlp_keep, mlp_send = kernel_call(
        mix_first,
        [((4, 432, 128), BF)] * 2 + [((2 * rows_of, 128), BF)] * 2,
        10**9,
        dw,
        swap(other, 1),
        up,
        up_got,
        down,
        down_got,
    )
    dk0, dv0, dq_mine, dq_other, dw, other, dg_cross = cross_back(
        0, (own, near), keys0, (dq1, dg_cross), (sent,)
    )
    got, mlp_got = cross(sent, 0), cross(mlp_send, 2)
    h_far = swap(h_send, 2)
    other, got, mlp_got, h_far, g_last = together(other, got, mlp_got, h_far, g_last)
    dg_tok, dg_cross = (
        dg_cross[k : k + 1] / g.astype(F32)[None, :] for k, g in enumerate((gain_tok, gain_cross))
    )
    gains = jnp.concatenate([dg_tok, dg_cross, dg_self, dg_mlp], 0)
    dw_got = swap(other, 1)
    dq_got, gains_got = swap(after(dq_other, other), 1), swap(after(gains, other), 1)
    mine, mine_send, one_keep, one_send = kernel_call(
        latent_weights,
        [((4, 576, 128), BF)] * 2 + [((4, 144, 128), BF)] * 2,
        2 * 10**9,
        selfn,
        n_near,
        n_far,
        n_last,
        late,
        g_near,
        g_far,
        g_last,
        h_far,
        m_own,
        m_near,
        e_own,
        e_got,
        scalars=(row,),
        scratch=[((8, 576, 128), BF), ((8, 144, 128), BF)],
    )
    dw, sent, far_send = kernel_call(
        mix_second,
        [((4, 432, 128), BF), ((2304, 128), BF), ((4, 432, 128), BF)],
        10**9,
        dw,
        dw_got,
        far_dw,
        got,
        one_send,
    )
    got, far_got, mine_got = cross(sent, 0), swap(far_send, 2), cross(mine_send, 1)
    gains = after(gains + gains_got, sent)
    gains_got = swap(gains, 2)
    (out_tok,) = kernel_call(
        token_end,
        [((n_tok, width), F32)],
        5 * 10**9,
        dk0,
        dv0,
        dk1,
        after(dv1, sent, mine_send, far_send),
        own,
        near,
        far,
        far_near,
        tok,
        gain_tok,
        vmem=24,
    )
    got, far_got, mine_got, gains_got, out_tok = together(
        got, far_got, mine_got, gains_got, out_tok
    )
    dw, sent, one_keep, mine, mine_send = kernel_call(
        mix_third,
        [
            ((2, 432, 128), BF),
            ((1152, 128), BF),
            ((2, 144, 128), BF),
            ((2, 576, 128), BF),
            ((2, 576, 128), BF),
        ],
        10**9,
        dw,
        got,
        far_got,
        one_keep,
        mine,
        mine_got,
    )
    got, mine_got = cross(sent, 1), cross(mine_send, 0)
    gains = after(gains + gains_got, sent)
    gains_got = cross(gains, 0)
    dq_near, dq_send, new_near = kernel_call(
        pair_queries,
        [(sq, F32), ((2 * width, LAT), BF), (full, F32)],
        10**9,
        after(dq_mine, sent),
        dq_got,
        forwards[0],
        f_got,
        two,
    )
    dq_far = swap(dq_send, 2)
    mlps = kernel_call(
        last_mlp, [((96, hid), F32)] * 2, 10**9, mlp_keep, after(mlp_got, dq_send)
    )
    got, mine_got, gains_got, dq_far, *mlps = together(got, mine_got, gains_got, dq_far, *mlps)
    kept, sent = kernel_call(
        mix_fourth, [((1152, 128), BF)] * 2, 10**9, dw, got, one_keep, mine, mine_got
    )
    got = cross(sent, 2)
    grad_lat, new_latents, _ = kernel_call(
        latent_end,
        [(full, F32), (full, BF), (sq, BF)],
        3 * 10**9,
        dq_near,
        after(dq_far, sent),
        new_near,
        own,
        near,
        far,
        far_near,
        lat,
        g1,
        gain_cross,
    )
    gains = after(gains + gains_got, sent)
    gains = gains + cross(gains, 1)
    gains = gains + cross(gains, 2)
    for k in range(low):
        gains = gains + lax.ppermute(gains, "dp", [(i, i ^ (1 << k)) for i in range(dp)])
    lasts = kernel_call(last_heads, [((96, 192), F32)] * 8, 10**9, kept, got)

    groups = [list(range(k * fine, (k + 1) * fine)) for k in range(8)]

    def shard(v):
        if fine == 1:
            return v
        return lax.psum_scatter(v, "dp", scatter_dimension=0, axis_index_groups=groups, tiled=True)

    order = (lasts[2], lasts[0], lasts[1], *lasts[3:], *mlps)
    return (
        new_latents[None],
        out_tok[None],
        grad_lat[None],
        *(gains[k] for k in range(4)),
        *(shard(v) for v in order),
    )


def solution(mesh):
    rows, cols, lone = P("dp", "mp", None), P(None, "mp"), P("dp", None)
    in_specs = (rows, rows, lone, lone, lone) + (P(),) * 4 + (cols,) * 10 + (rows,)
    out_specs = (rows,) * 3 + (P(),) * 4 + (P("dp", "mp"),) * 10
    return jax.shard_map(
        per_device, mesh=mesh, in_specs=in_specs, out_specs=out_specs, check_vma=False
    )
```
